32 devices in a mesh: group: 2 (over y), gx: 4 (over z), gy: 2 (over x), ta: 2 (over core).
Axes of the slice: x: 2, y: 2, z: 4, core: 2. Of those that a mesh axis runs over, the one named last changes fastest.
Arguments:
- t_initial: float32 [8, 2048, 512], P('ta', ('group', 'gx'), 'gy'), parts along dimension 1, may hold values from -4 to 4
- power_mantissa: bfloat16 [8, 3072, 768], P('ta', ('group', 'gx'), 'gy'), parts along dimension 1, may hold values from -6 to 6
- tile_exponent: int32 [8, 48, 12], P('ta', ('group', 'gx'), 'gy'), parts along dimension 1, may hold values from -2 to 2
- channel_mask: int32 [8, 512], replicated, may hold values 0 or 1
- material: int32 [8], replicated, may hold values from 0 to 3
- conductivity: float32 [4], replicated, may hold values from 0.3 to 3
Outputs:
- temperature: float32 [8, 2048, 512], P('ta', ('group', 'gx'), 'gy'), parts along dimension 1
- heat_source: float32 [8, 2048, 512], P('ta', ('group', 'gx'), 'gy'), parts along dimension 1
The draws below stay inside these ranges and needn't reach their ends.
There are 2 independent parts, one for each index of `group`. The reference program is written for one: setup_inputs(seed, part) draws one part's arguments, and reference() takes and returns one part's arrays. A program takes and returns all parts, laid end to end along the dimension named above; an argument that names none is the same for every part. Nothing has to cross between parts.
All inputs are finite; a program needn't handle non-finite values.
Results may differ from the reference program's by a relative error of at most 0.0003.
Values sent between devices are 32-bit elements; how exact they have to be, the bound alone decides.
No kernel may reach another device: no remote copies, remote signals or barrier semaphores. Data moves between devices by JAX's collectives and lax.ppermute only.
A program may use at most 192 MiB of HBM per device.

```python
import math
import jax
import jax.numpy as jnp
from jax import lax

CX = 256
CY = 256
RIM = 64
TILE = 64
MATS = 4
STEPS = 2
SWEEPS = 3
LAYERS = 8
NX = 1024
NY = 512
N_GX = 4
N_GY = 2


def touch_ends(array, own_key, low, largest):
    place = [jax.random.randint(jax.random.fold_in(own_key, axis), (), 0, length) for axis, length in enumerate(array.shape)]
    longest = array.shape.index(max(array.shape))
    next_to = place[:longest] + [(place[longest] + 1) % array.shape[longest]] + place[longest + 1:]
    return array.at[tuple(place)].set(low).at[tuple(next_to)].set(largest)


def levels(rng, dims, cuts, smallest, top_value):
    def one(position, parts):
        steps = jax.random.uniform(jax.random.fold_in(jax.random.fold_in(rng, 6), position), (parts,), jnp.float32, smallest / len(cuts), top_value / len(cuts))
        return jnp.repeat(jnp.exp(steps), dims[position] // parts).reshape((-1,) + (1,) * (len(dims) - position - 1))

    level = one(*cuts[0])
    for cut in cuts[1:]:
        level = level * one(*cut)
    return level


def noise(key, shape, deviation, reach, shards=(), kind=jnp.bfloat16):
    values = jax.random.normal(key, shape, jnp.float32) * deviation
    if len(shards) > 0:
        values = levels(key, shape, shards, -0.22, 0.18) * values
    return jnp.clip(values, min=-reach, max=reach).astype(kind)


def setup_inputs(seed: int = 0, part: int = 0) -> dict:
    keys = jax.random.split(jax.random.key(seed), 7)
    own_keys = jax.random.split(jax.random.fold_in(keys[6], part), 7)
    t_initial = noise(own_keys[0], (LAYERS, NX, NY), 1.0, 4.0, ((0, 2), (1, 4), (2, 2)), jnp.float32)
    power_mantissa = noise(own_keys[1], (LAYERS, N_GX * (CX + 2 * RIM), N_GY * (CY + 2 * RIM)), 1.0, 6.0, ((0, 2), (1, 4), (2, 2)))
    tile_exponent = touch_ends(jax.random.randint(own_keys[2], (LAYERS, N_GX * (CX + 2 * RIM) // TILE, N_GY * (CY + 2 * RIM) // TILE), -2, 3), jax.random.fold_in(own_keys[2], 1), -2, 2).astype(jnp.int32)
    channel_mask = touch_ends((jax.random.randint(keys[3], (LAYERS, NY), 0, 2) < 1).astype(jnp.int32), jax.random.fold_in(keys[3], 1), 0, 1)
    material = touch_ends(jax.random.randint(keys[4], (LAYERS,), 0, MATS), jax.random.fold_in(keys[4], 1), 0, MATS - 1).astype(jnp.int32)
    conductivity = jnp.clip(jnp.exp(jax.random.uniform(keys[5], (MATS,), jnp.float32, math.log(0.3), math.log(3.0))), 0.3, 3.0)
    return dict(t_initial=t_initial, power_mantissa=power_mantissa, tile_exponent=tile_exponent, channel_mask=channel_mask, material=material, conductivity=conductivity)


CAPACITY = 1.0
COOLANT = 2.0
VERTICAL = 2.0


def decode(mantissa, exponent):
    scales = jnp.exp2(exponent.astype(jnp.float32))
    depth, rows, cols = scales.shape
    scales = jnp.broadcast_to(scales[:, :, None, :, None], (depth, rows, TILE, cols, TILE))
    return mantissa.astype(jnp.float32) * scales.reshape(depth, rows * TILE, cols * TILE)


def block_shift(values, axis, offset):
    count = values.shape[axis]
    zeros = jnp.zeros_like(lax.slice_in_dim(values, 0, 1, axis=axis))
    if offset == 1:
        return jnp.concatenate([zeros, lax.slice_in_dim(values, 0, count - 1, axis=axis)], axis=axis)
    return jnp.concatenate([lax.slice_in_dim(values, 1, count, axis=axis), zeros], axis=axis)


def add_edges(inner, from_prev, from_next, axis):
    length = inner.shape[axis]
    widths_head = [(0, 0)] * inner.ndim
    widths_head[axis] = (0, length - RIM)
    widths_tail = [(0, 0)] * inner.ndim
    widths_tail[axis] = (length - RIM, 0)
    inner = inner + jnp.pad(from_prev, widths_head)
    return inner + jnp.pad(from_next, widths_tail)


def fold_global(blocks, axis):
    length = blocks.shape[axis]
    inner = lax.slice_in_dim(blocks, RIM, length - RIM, axis=axis)
    upper = lax.slice_in_dim(blocks, 0, RIM, axis=axis)
    lower = lax.slice_in_dim(blocks, length - RIM, length, axis=axis)
    from_prev = block_shift(lower, axis - 1, 1)
    from_next = block_shift(upper, axis - 1, -1)
    return add_edges(inner, from_prev, from_next, axis)


def neighbours(padded):
    return [padded[:-2, 1:-1, 1:-1], padded[2:, 1:-1, 1:-1],
            padded[1:-1, :-2, 1:-1], padded[1:-1, 2:, 1:-1],
            padded[1:-1, 1:-1, :-2], padded[1:-1, 1:-1, 2:]]


def face_coeffs(cond_padded):
    centre = cond_padded[1:-1, 1:-1, 1:-1]
    weights = (VERTICAL, VERTICAL, 1.0, 1.0, 1.0, 1.0)
    return [weight * 0.5 * (centre + other) for weight, other in zip(weights, neighbours(cond_padded))]


def denominator(coeffs, flow):
    total = CAPACITY + flow
    for coeff in coeffs:
        total = total + coeff
    return total


def sweep(padded, coeffs, base, denom, flow):
    others = neighbours(padded)
    total = base
    for coeff, other in zip(coeffs, others):
        total = total + coeff * other
    total = total + flow * others[2]
    return total / denom


def reference(t_initial, power_mantissa, tile_exponent, channel_mask, material, conductivity):
    power = decode(power_mantissa, tile_exponent)
    depth, ext_x, ext_y = power.shape
    blocks = power.reshape(depth, N_GX, ext_x // N_GX, N_GY, ext_y // N_GY)
    blocks = fold_global(blocks, 2)
    blocks = fold_global(blocks, 4)
    heat_source = blocks.reshape(depth, N_GX * CX, N_GY * CY)
    onehot = (material[:, None] == jnp.arange(MATS, dtype=jnp.int32)[None, :]).astype(jnp.float32)
    layer_cond = jnp.sum(onehot * conductivity[None, :], axis=1)
    flow = COOLANT * channel_mask.astype(jnp.float32)[:, None, :]
    older = t_initial
    for step_index in range(STEPS):
        cond = layer_cond[:, None, None] * (1.0 + 0.5 * jnp.tanh(older))
        coeffs = face_coeffs(jnp.pad(cond, 1))
        denom = denominator(coeffs, flow)
        base = CAPACITY * older + heat_source
        field = older
        for sweep_index in range(SWEEPS):
            field = sweep(jnp.pad(field, 1), coeffs, base, denom, flow)
        older = field
    return older, heat_source
```

```python
import functools

import jax
import jax.numpy as jnp
from jax import lax
from jax.experimental import pallas as pl
from jax.experimental.pallas import tpu as pltpu
from jax.sharding import PartitionSpec as P

RIM = 64
TILE = 64
STEPS = 2
SWEEPS = 3
COOLANT = 2.0

LANES = 128
WIDE = 6
LOCAL = 200
REGION = 144
EDGE = 72
ROWS_P = 2 * EDGE + 8 + 16
ROWS_G = EDGE + 16
ROWS_D = 40
F32 = jnp.float32
VMEM = pl.BlockSpec(memory_space=pltpu.VMEM)
SMEM = pl.BlockSpec(memory_space=pltpu.SMEM)
ANY = pl.BlockSpec(memory_space=pl.ANY)
PARAMS = pltpu.CompilerParams(vmem_limit_bytes=48 << 20)


def rows8(start):
    return pl.ds(pl.multiple_of(start, 8), 8)


def lane_ids():
    return lax.broadcasted_iota(jnp.int32, (8, LANES), 1)


def turn(value, shift):
    shift = shift % LANES
    return pltpu.roll(value, shift, 1) if shift else value


def decode_kernel(mantissa, exponent, own, sent, plain, own_sem, sent_sem):
    core = lax.axis_index("ta")
    depth, rows, _ = mantissa.shape
    tiles = rows // TILE
    wide_lane = lax.broadcasted_iota(jnp.int32, (16, LANES), 1)
    first = pl.multiple_of(core * 184, 8)
    other = pl.multiple_of(184 - core * 184, 8)

    def copies(layer):
        return (
            pltpu.make_async_copy(plain.at[layer, :, pl.ds(other, LOCAL), :], sent.at[layer], sent_sem.at[layer]),
            pltpu.make_async_copy(plain.at[layer, :, pl.ds(first, LOCAL), :], own.at[layer], own_sem.at[layer]),
        )

    for layer in range(depth):

        @pl.loop(0, tiles)
        def _(tile_row):
            for col in range(3):
                low = exponent[layer, tile_row, 2 * col]
                high = exponent[layer, tile_row, 2 * col + 1]
                scale = jnp.exp2(jnp.where(wide_lane < TILE, low, high).astype(F32))
                for part in range(TILE // 16):
                    where = pl.ds(pl.multiple_of(tile_row * TILE + part * 16, 16), 16)
                    cells = mantissa[layer, where, col * LANES : (col + 1) * LANES]
                    plain[layer, col, where, :] = cells.astype(F32) * scale

        for copy in copies(layer):
            copy.start()
    for layer in range(depth):
        for copy in copies(layer):
            copy.wait()


def pack_kernel(sides, own, other, t_own, t_other, *outs):
    core = lax.axis_index("ta")
    lane = lane_ids()
    low = lane < 64
    to_p, to_g, to_d = outs[0], outs[1 : 1 + len(sides)], outs[1 + len(sides) :]
    edge = core * 128
    region = 56 - core * 56
    t_row = core * 120
    t_edge = core * 248

    def place(total, value, source, target, width):
        moved = turn(value, target - source)
        return jnp.where((lane >= target) & (lane < target + width), moved, total)

    def one(src, t_src, index, layer):
        def cells(col, row):
            return src[index, col, rows8(row), :]

        def t_cells(col, row):
            return t_src[index, rows8(row), col * LANES : (col + 1) * LANES]

        extra = jnp.zeros((8, LANES), F32)
        for j in range(9):
            left, right = cells(0, edge + 8 * j), cells(2, edge + 8 * j)
            to_p[layer, 8 * j : 8 * j + 8, :] = cells(1, edge + 8 * j)
            to_p[layer, EDGE + 8 * j : EDGE + 8 * j + 8, :] = jnp.where(low, right, left)
            extra = place(extra, jnp.where(low, left, right), 64 - WIDE, 2 * WIDE * j, 2 * WIDE)
        to_p[layer, 2 * EDGE : 2 * EDGE + 8, :] = extra
        for col in range(2):
            start = 2 * EDGE + 8 + 8 * col
            to_p[layer, start : start + 8, :] = t_cells(col, t_edge)

        def side_parts(right, g_ref, d_ref):
            col, t_col = (2, 1) if right else (0, 0)
            at, t_at = (LANES - WIDE, LANES - WIDE) if right else (64, 0)

            def strip(row):
                value = cells(col, row)
                return turn(value, 64) if right else value

            extra = jnp.zeros((8, LANES), F32)
            for j in range(9):
                one_strip, two_strip = strip(region + 8 * j), strip(region + EDGE + 8 * j)
                g_ref[layer, 8 * j : 8 * j + 8, :] = jnp.where(low, one_strip, turn(two_strip, 64))
                extra = place(extra, one_strip, at, WIDE * j, WIDE)
                extra = place(extra, two_strip, at, WIDE * (j + 9), WIDE)
            g_ref[layer, EDGE : EDGE + 8, :] = extra
            extra = jnp.zeros((8, LANES), F32)
            for j in range(17):
                extra = place(extra, t_cells(t_col, t_row + 8 * j), t_at, WIDE * j, WIDE)
            g_ref[layer, EDGE + 8 : EDGE + 16, :] = extra
            strips = [strip(edge + 8 * j) for j in range(9)]
            for j in range(4):
                d_ref[layer, 8 * j : 8 * j + 8, :] = jnp.where(low, strips[j], turn(strips[j + 5], 64))
            extra = strips[4]
            for j in range(9):
                extra = place(extra, strips[j], at, 64 + WIDE * j, WIDE)
            extra = place(extra, t_cells(t_col, t_edge), t_at, 64 + 9 * WIDE, WIDE)
            d_ref[layer, 32:40, :] = extra

        for side, g_ref, d_ref in zip(sides, to_g, to_d):
            if side is None:
                first = lax.axis_index("gy") == 0
                pl.when(first)(functools.partial(side_parts, True, g_ref, d_ref))
                pl.when(jnp.logical_not(first))(functools.partial(side_parts, False, g_ref, d_ref))
            else:
                side_parts(side, g_ref, d_ref)

    depth = own.shape[0]

    @pl.loop(0, depth)
    def _(index):
        one(own, t_own, index, core * depth + index)
        one(other, t_other, index, (1 - core) * depth + index)


def solve_kernel(sides, bounds, *refs):
    count = len(sides)
    from_p, refs = refs[0], refs[1:]
    from_g, from_d, refs = refs[:count], refs[count : 2 * count], refs[2 * count :]
    own, other, t_own, t_other, flow, material, conductivity = refs[:7]
    t_out, h_out, sent = refs[7:10]
    heat, now, later, cond, f_up, f_down, f_right, f_above, inverse, base, t_stage, h_stage, sems = refs[10:]
    core = lax.axis_index("ta")
    lane = lane_ids()
    row_id = lax.broadcasted_iota(jnp.int32, (8, LANES), 0)
    low = lane < 64
    zero = jnp.zeros((8, LANES), F32)
    depth = own.shape[0]
    layers = 2 * depth
    region = 56 - core * 56
    edge = core * EDGE
    tiles = REGION // 8
    t_row = core * 120
    t_first = 8 - core * 8
    t_halo = core * (REGION - 8)
    row_start = lax.axis_index("gx") * 256 + core * 128 - 8
    col_start = lax.axis_index("gy") * 256 - 64

    def inside(row, col):
        rows = row_id + (row_start + row)
        cols = lane + (col_start + col * LANES)
        ok = (rows >= 0) & (rows < bounds[0]) & (cols >= 0) & (cols < bounds[1])
        return jnp.where(ok, 1.0, 0.0)

    def spread(t_left, t_right):
        one, two = turn(t_left, 64), turn(t_right, 64)
        return jnp.where(low, zero, one), jnp.where(low, one, two), jnp.where(low, two, zero)

    def gather(src, t_src, index, layer):
        for j in range(tiles):
            for col in range(3):
                heat[layer * 3 + col, 8 * j : 8 * j + 8, :] = src[index, col, rows8(region + 8 * j), :]
        for j in range(17):
            row = rows8(t_row + 8 * j)
            parts = spread(t_src[index, row, :LANES], t_src[index, row, LANES:])
            for col in range(3):
                now[layer * 3 + col, rows8(8 + t_first + 8 * j), :] = parts[col]

    @pl.loop(0, depth)
    def _(index):
        gather(own, t_own, index, core * depth + index)
        gather(other, t_other, index, (1 - core) * depth + index)

    def add_side(layer, right, g_ref, d_ref):
        col = 2 if right else 0
        target = 64 if right else 64 - WIDE

        def put(ref, row, value):
            ref[layer * 3 + col, row, :] = ref[layer * 3 + col, row, :] + value

        def merge(main, extra, at):
            moved = turn(extra, target - at)
            if right:
                return jnp.where(low, main, jnp.where(lane < 64 + WIDE, moved, 0.0))
            return jnp.where(low, jnp.where(lane >= 64 - WIDE, moved, 0.0), main)

        def only(extra, at):
            moved = turn(extra, target - at)
            return jnp.where((lane >= target) & (lane < target + WIDE), moved, 0.0)

        extra = g_ref[layer, EDGE : EDGE + 8, :]
        for j in range(9):
            main = g_ref[layer, 8 * j : 8 * j + 8, :]
            turned = turn(main, 64)
            one, two = (main, turned) if right else (turned, main)
            put(heat, pl.ds(8 * j, 8), merge(one, extra, WIDE * j))
            put(heat, pl.ds(EDGE + 8 * j, 8), merge(two, extra, WIDE * (j + 9)))
        extra = g_ref[layer, EDGE + 8 : EDGE + 16, :]
        for j in range(17):
            put(now, rows8(8 + t_first + 8 * j), only(extra, WIDE * j))
        extra = d_ref[layer, 32:40, :]
        for j in range(9):
            main = d_ref[layer, 8 * (j % 5) : 8 * (j % 5) + 8, :]
            if (j < 5) != right:
                main = turn(main, 64)
            put(heat, rows8(edge + 8 * j), merge(main, extra, 64 + WIDE * j))
        put(now, rows8(8 + t_halo), only(extra, 64 + 9 * WIDE))

    @pl.loop(0, layers)
    def _(layer):
        extra = from_p[layer, 2 * EDGE : 2 * EDGE + 8, :]
        for j in range(9):
            row = rows8(edge + 8 * j)
            middle = from_p[layer, 8 * j : 8 * j + 8, :]
            ends = from_p[layer, EDGE + 8 * j : EDGE + 8 * j + 8, :]
            moved = turn(extra, 64 - WIDE - 2 * WIDE * j)
            left = jnp.where(low, jnp.where(lane >= 64 - WIDE, moved, 0.0), ends)
            right = jnp.where(low, ends, jnp.where(lane < 64 + WIDE, moved, 0.0))
            for col, value in enumerate((left, middle, right)):
                heat[layer * 3 + col, row, :] = heat[layer * 3 + col, row, :] + value
        start = 2 * EDGE + 8
        parts = spread(from_p[layer, start : start + 8, :], from_p[layer, start + 8 : start + 16, :])
        for col in range(3):
            now[layer * 3 + col, rows8(8 + t_halo), :] = parts[col]
            for ref in (now, later, cond):
                ref[layer * 3 + col, 0:8, :] = zero
                ref[layer * 3 + col, REGION + 8 : REGION + 16, :] = zero
        for side, g_ref, d_ref in zip(sides, from_g, from_d):
            if side is None:
                first = lax.axis_index("gy") == 0
                pl.when(first)(functools.partial(add_side, layer, True, g_ref, d_ref))
                pl.when(jnp.logical_not(first))(functools.partial(add_side, layer, False, g_ref, d_ref))
            else:
                add_side(layer, side, g_ref, d_ref)

    def to_stage(stage, layer, row, parts):
        turned = [turn(part, 64) for part in parts]
        for col in range(2):
            value = jnp.where(low, turned[col], turned[col + 1])
            stage[layer, rows8(row), col * LANES : (col + 1) * LANES] = value

    def outputs(stage, which, out):
        mine = stage.at[pl.ds(core * depth, depth)]
        theirs = stage.at[pl.ds((1 - core) * depth, depth)]
        half = stage.shape[1]
        place = pl.ds(pl.multiple_of(core * half, half), half)
        return (
            pltpu.make_async_copy(theirs, sent.at[which], sems.at[which, 0]),
            pltpu.make_async_copy(mine, out.at[:, place, :], sems.at[which, 1]),
        )

    @pl.loop(0, 16)
    def _(tile):
        for layer in range(layers):
            to_stage(h_stage, layer, 8 * tile, [heat[layer * 3 + col, rows8(8 + 8 * tile), :] for col in range(3)])

    for copy in outputs(h_stage, 1, h_out):
        copy.start()

    def neighbours_right(values):
        moved = [turn(value, -1) for value in values]
        last = lane == LANES - 1
        return [jnp.where(last, moved[col + 1], moved[col]) if col < 2 else moved[col] for col in range(3)]

    def neighbours_left(values):
        moved = [turn(value, 1) for value in values]
        first = lane == 0
        return [jnp.where(first, moved[col - 1], moved[col]) if col > 0 else moved[col] for col in range(3)]

    def conductances():
        @pl.loop(0, tiles)
        def _(tile):
            masks = [inside(8 * tile, col) for col in range(3)]
            row = rows8(8 + 8 * tile)
            for layer in range(layers):
                scale = conductivity[material[layer]]
                for col in range(3):
                    n = layer * 3 + col
                    cond[n, row, :] = scale * (1.0 + 0.5 * jnp.tanh(now[n, row, :])) * masks[col]

    def coefficients():
        @pl.loop(0, tiles)
        def _(tile):
            masks = [inside(8 * tile, col) for col in range(3)]
            row, inner = rows8(8 + 8 * tile), rows8(8 * tile)
            below = [zero] * 3
            here = [cond[col, row, :] for col in range(3)]
            for layer in range(layers):
                if layer + 1 < layers:
                    above = [cond[layer * 3 + 3 + col, row, :] for col in range(3)]
                else:
                    above = [zero] * 3
                rights, lefts = neighbours_right(here), neighbours_left(here)
                for col in range(3):
                    n = layer * 3 + col
                    centre = here[col]
                    up = 0.5 * (centre + cond[n, pl.ds(8 * tile + 7, 8), :]) + flow[n : n + 1, :]
                    down = 0.5 * (centre + cond[n, pl.ds(8 * tile + 9, 8), :])
                    right = 0.5 * (centre + rights[col])
                    left = 0.5 * (centre + lefts[col])
                    over = centre + above[col]
                    under = centre + below[col]
                    total = 1.0 + up + down + right + left + over + under
                    f_up[n, inner, :] = up
                    f_down[n, inner, :] = down
                    f_right[n, inner, :] = right
                    f_above[n, inner, :] = over
                    inverse[n, inner, :] = masks[col] / total
                    base[n, inner, :] = now[n, row, :] + heat[n, inner, :]
                below, here = here, above

    def sweep(src, dst):
        @pl.loop(0, tiles)
        def _(tile):
            row, inner = rows8(8 + 8 * tile), rows8(8 * tile)
            below, f_below = None, None
            here = [src[col, row, :] for col in range(3)]
            for layer in range(layers):
                f_over = [f_above[layer * 3 + col, inner, :] for col in range(3)]
                above = None
                if layer + 1 < layers:
                    above = [src[layer * 3 + 3 + col, row, :] for col in range(3)]
                f_side = [f_right[layer * 3 + col, inner, :] for col in range(3)]
                rights = neighbours_right(here)
                lefts = neighbours_left([f * v for f, v in zip(f_side, here)])
                for col in range(3):
                    n = layer * 3 + col
                    total = base[n, inner, :] + f_up[n, inner, :] * src[n, pl.ds(8 * tile + 7, 8), :]
                    total = total + f_down[n, inner, :] * src[n, pl.ds(8 * tile + 9, 8), :]
                    total = total + (f_side[col] * rights[col] + lefts[col])
                    if above is not None:
                        total = total + f_over[col] * above[col]
                    if below is not None:
                        total = total + f_below[col] * below[col]
                    dst[n, row, :] = total * inverse[n, inner, :]
                below, here, f_below = here, above, f_over

    refs_now, refs_later = now, later
    for step in range(STEPS):
        if step:
            now = refs_now
        conductances()
        coefficients()
        for _ in range(SWEEPS):
            sweep(refs_now, refs_later)
            refs_now, refs_later = refs_later, refs_now

    @pl.loop(0, 16)
    def _(tile):
        for layer in range(layers):
            to_stage(t_stage, layer, 8 * tile, [refs_now[layer * 3 + col, rows8(16 + 8 * tile), :] for col in range(3)])

    for copy in outputs(t_stage, 0, t_out):
        copy.start()
    for copy in outputs(h_stage, 1, h_out) + outputs(t_stage, 0, t_out):
        copy.wait()


def place_kernel(received, t_in, h_in, t_out, h_out, sems):
    core = lax.axis_index("ta")
    half = received.shape[2]
    place = pl.ds(pl.multiple_of((1 - core) * half, half), half)
    copies = [
        pltpu.make_async_copy(received.at[which], out.at[:, place, :], sems.at[which])
        for which, out in enumerate((t_out, h_out))
    ]
    for copy in copies:
        copy.start()
    for copy in copies:
        copy.wait()


def on_device(t_initial, power_mantissa, tile_exponent, channel_mask, material, conductivity):
    depth, rows, cols = t_initial.shape
    layers = 2 * depth
    n_gx, n_gy = lax.axis_size("gx"), lax.axis_size("gy")
    array = jax.ShapeDtypeStruct
    swap = [(0, 1), (1, 0)]

    t_other = lax.ppermute(t_initial, "ta", swap)
    local = array((depth, 3, LOCAL, LANES), F32)
    own, sent = pl.pallas_call(
        decode_kernel,
        out_shape=(local, local),
        in_specs=[VMEM, SMEM],
        out_specs=(ANY, ANY),
        scratch_shapes=[
            pltpu.VMEM((depth, 3, rows + 2 * RIM, LANES), F32),
            pltpu.SemaphoreType.DMA((depth,)),
            pltpu.SemaphoreType.DMA((depth,)),
        ],
        compiler_params=PARAMS,
        name="decode",
    )(power_mantissa, tile_exponent)
    other = lax.ppermute(sent, "ta", swap)

    out_sides = [None] if n_gy == 2 else [True, False]
    count = len(out_sides)
    packed = pl.pallas_call(
        functools.partial(pack_kernel, out_sides),
        out_shape=(array((layers, ROWS_P, LANES), F32),)
        + (array((layers, ROWS_G, LANES), F32),) * count
        + (array((layers, ROWS_D, LANES), F32),) * count,
        in_specs=[VMEM] * 4,
        out_specs=(VMEM,) * (1 + 2 * count),
        compiler_params=PARAMS,
        name="pack",
    )(own, other, t_initial, t_other)

    def moves(shift):
        pairs = []
        for z in range(n_gx):
            for x in range(n_gy):
                for c in range(2):
                    to_z = z + 2 * c - 1
                    to_x = x ^ 1 if shift is None else x + shift
                    if 0 <= to_z < n_gx and 0 <= to_x < n_gy:
                        pairs.append(((z * n_gy + x) * 2 + c, (to_z * n_gy + to_x) * 2 + 1 - c))
        return pairs

    along = ("gx", "gy", "ta")
    shifts = [None] if n_gy == 2 else [1, -1]
    from_g = []
    for shift, value in zip(shifts, packed[1 : 1 + count]):
        pairs = swap if shift is None else [(x, x + shift) for x in range(n_gy) if 0 <= x + shift < n_gy]
        from_g.append(lax.ppermute(value, "gy", pairs))
    from_d = [lax.ppermute(value, along, moves(shift)) for shift, value in zip(shifts, packed[1 + count :])]
    from_p = lax.ppermute(packed[0], along, moves(0))
    in_sides = [None] if n_gy == 2 else [False, True]

    wide = jnp.pad(channel_mask, ((0, 0), (RIM, RIM)))
    mask = lax.dynamic_slice_in_dim(wide, lax.axis_index("gy") * cols, cols + 2 * RIM, 1)
    flow = COOLANT * mask.astype(F32).reshape(layers * 3, LANES)

    whole = array((depth, rows, cols), F32)
    half = array((2, depth, rows // 2, cols), F32)
    inner = pltpu.VMEM((layers * 3, REGION, LANES), F32)
    outer = pltpu.VMEM((layers * 3, REGION + 16, LANES), F32)
    stage = pltpu.VMEM((layers, rows // 2, cols), F32)
    t_part, h_part, sent = pl.pallas_call(
        functools.partial(solve_kernel, in_sides, (n_gx * rows, n_gy * cols)),
        out_shape=(whole, whole, half),
        in_specs=[VMEM] * (1 + 2 * count + 5) + [SMEM, SMEM],
        out_specs=(ANY, ANY, ANY),
        scratch_shapes=[inner, outer, outer, outer] + [inner] * 6 + [stage, stage, pltpu.SemaphoreType.DMA((2, 2))],
        compiler_params=PARAMS,
        name="solve",
    )(from_p, *from_g, *from_d, own, other, t_initial, t_other, flow, material, conductivity)
    received = lax.ppermute(sent, "ta", swap)
    return pl.pallas_call(
        place_kernel,
        out_shape=(whole, whole),
        in_specs=[ANY, ANY, ANY],
        out_specs=(ANY, ANY),
        scratch_shapes=[pltpu.SemaphoreType.DMA((2,))],
        input_output_aliases={1: 0, 2: 1},
        compiler_params=PARAMS,
        name="place",
    )(received, t_part, h_part)


def solution(mesh):
    cells = P("ta", ("group", "gx"), "gy")
    return jax.shard_map(
        on_device,
        mesh=mesh,
        in_specs=(cells, cells, cells, P(), P(), P()),
        out_specs=(cells, cells),
        check_vma=False,
    )
```

```python
import functools

import jax
import jax.numpy as jnp
from jax import lax
from jax.experimental import pallas as pl
from jax.experimental.pallas import tpu as pltpu
from jax.sharding import PartitionSpec as P

RIM = 64
TILE = 64
STEPS = 2
SWEEPS = 3
COOLANT = 2.0

LANES = 128
WIDE = 6
LOCAL = 200
REGION = 144
EDGE = 72
ROWS_P = 2 * EDGE + 8 + 16
ROWS_G = EDGE + 16
ROWS_D = 40
F32 = jnp.float32
VMEM = pl.BlockSpec(memory_space=pltpu.VMEM)
SMEM = pl.BlockSpec(memory_space=pltpu.SMEM)
ANY = pl.BlockSpec(memory_space=pl.ANY)
PARAMS = pltpu.CompilerParams(vmem_limit_bytes=48 << 20)


def rows8(start):
    return pl.ds(pl.multiple_of(start, 8), 8)


def lane_ids():
    return lax.broadcasted_iota(jnp.int32, (8, LANES), 1)


def turn(value, shift):
    shift = shift % LANES
    return pltpu.roll(value, shift, 1) if shift else value


def decode_kernel(mantissa, exponent, own, sent, plain, own_sem, sent_sem):
    core = lax.axis_index("ta")
    depth, rows, _ = mantissa.shape
    tiles = rows // TILE
    wide_lane = lax.broadcasted_iota(jnp.int32, (16, LANES), 1)
    first = pl.multiple_of(core * 184, 8)
    other = pl.multiple_of(184 - core * 184, 8)

    def copies(layer):
        return (
            pltpu.make_async_copy(plain.at[layer, :, pl.ds(other, LOCAL), :], sent.at[layer], sent_sem.at[layer]),
            pltpu.make_async_copy(plain.at[layer, :, pl.ds(first, LOCAL), :], own.at[layer], own_sem.at[layer]),
        )

    for layer in range(depth):

        @pl.loop(0, tiles)
        def _(tile_row):
            for col in range(3):
                low = exponent[layer, tile_row, 2 * col]
                high = exponent[layer, tile_row, 2 * col + 1]
                scale = jnp.exp2(jnp.where(wide_lane < TILE, low, high).astype(F32))
                for part in range(TILE // 16):
                    where = pl.ds(pl.multiple_of(tile_row * TILE + part * 16, 16), 16)
                    cells = mantissa[layer, where, col * LANES : (col + 1) * LANES]
                    plain[layer, col, where, :] = cells.astype(F32) * scale

        for copy in copies(layer):
            copy.start()
    for layer in range(depth):
        for copy in copies(layer):
            copy.wait()


def pack_kernel(sides, own, other, t_own, t_other, *outs):
    core = lax.axis_index("ta")
    lane = lane_ids()
    low = lane < 64
    to_p, to_g, to_d = outs[0], outs[1 : 1 + len(sides)], outs[1 + len(sides) :]
    edge = core * 128
    region = 56 - core * 56
    t_row = core * 120
    t_edge = core * 248

    def place(total, value, source, target, width):
        moved = turn(value, target - source)
        return jnp.where((lane >= target) & (lane < target + width), moved, total)

    def one(src, t_src, index, layer):
        def cells(col, row):
            return src[index, col, rows8(row), :]

        def t_cells(col, row):
            return t_src[index, rows8(row), col * LANES : (col + 1) * LANES]

        extra = jnp.zeros((8, LANES), F32)
        for j in range(9):
            left, middle, right = (cells(col, edge + 8 * j) for col in range(3))
            one, two, three = turn(left, 64), turn(middle, 64), turn(right, 64)
            to_p[layer, 8 * j : 8 * j + 8, :] = jnp.where(low, one, two)
            to_p[layer, EDGE + 8 * j : EDGE + 8 * j + 8, :] = jnp.where(low, two, three)
            extra = place(extra, jnp.where(low, left, right), 64 - WIDE, 2 * WIDE * j, 2 * WIDE)
        to_p[layer, 2 * EDGE : 2 * EDGE + 8, :] = extra
        for col in range(2):
            start = 2 * EDGE + 8 + 8 * col
            to_p[layer, start : start + 8, :] = t_cells(col, t_edge)

        def side_parts(right, g_ref, d_ref):
            col, t_col = (2, 1) if right else (0, 0)
            at, t_at = (LANES - WIDE, LANES - WIDE) if right else (64, 0)

            def strip(row):
                value = cells(col, row)
                return turn(value, 64) if right else value

            extra = jnp.zeros((8, LANES), F32)
            for j in range(9):
                one_strip, two_strip = strip(region + 8 * j), strip(region + EDGE + 8 * j)
                g_ref[layer, 8 * j : 8 * j + 8, :] = jnp.where(low, one_strip, turn(two_strip, 64))
                extra = place(extra, one_strip, at, WIDE * j, WIDE)
                extra = place(extra, two_strip, at, WIDE * (j + 9), WIDE)
            g_ref[layer, EDGE : EDGE + 8, :] = extra
            extra = jnp.zeros((8, LANES), F32)
            for j in range(17):
                extra = place(extra, t_cells(t_col, t_row + 8 * j), t_at, WIDE * j, WIDE)
            g_ref[layer, EDGE + 8 : EDGE + 16, :] = extra
            strips = [strip(edge + 8 * j) for j in range(9)]
            for j in range(4):
                d_ref[layer, 8 * j : 8 * j + 8, :] = jnp.where(low, strips[j], turn(strips[j + 5], 64))
            extra = strips[4]
            for j in range(9):
                extra = place(extra, strips[j], at, 64 + WIDE * j, WIDE)
            extra = place(extra, t_cells(t_col, t_edge), t_at, 64 + 9 * WIDE, WIDE)
            d_ref[layer, 32:40, :] = extra

        for side, g_ref, d_ref in zip(sides, to_g, to_d):
            if side is None:
                first = lax.axis_index("gy") == 0
                pl.when(first)(functools.partial(side_parts, True, g_ref, d_ref))
                pl.when(jnp.logical_not(first))(functools.partial(side_parts, False, g_ref, d_ref))
            else:
                side_parts(side, g_ref, d_ref)

    depth = own.shape[0]

    @pl.loop(0, depth)
    def _(index):
        one(own, t_own, index, core * depth + index)
        one(other, t_other, index, (1 - core) * depth + index)


def stack_kernel(own, other, t_own, t_other, heat, now, cells, t_cells, sems, t_sems):
    core = lax.axis_index("ta")
    low = lane_ids() < 64
    zero = jnp.zeros((8, LANES), F32)
    depth, rows, _ = t_own.shape
    layers = 2 * depth
    height = own.shape[0] // depth
    t_height = REGION - 8
    copies = []
    for which, (src, t_src) in enumerate(((own, t_own), (other, t_other))):
        base = core * depth if which == 0 else (1 - core) * depth
        start = pl.multiple_of(base * height, 8)
        copies.append(pltpu.make_async_copy(src, cells.at[pl.ds(start, depth * height), :], sems.at[which]))
        for layer in range(depth):
            for col in range(2):
                row = pl.multiple_of(core * 120, 8)
                start = pl.multiple_of((base + layer) * t_height, 8)
                copies.append(
                    pltpu.make_async_copy(
                        t_src.at[layer, pl.ds(row, t_height), col * LANES : (col + 1) * LANES],
                        t_cells.at[col, pl.ds(start, t_height), :],
                        t_sems.at[which, layer, col],
                    )
                )
    for copy in copies:
        copy.start()
    for copy in copies:
        copy.wait()
    region = 56 - core * 56
    t_first = 8 - core * 8
    t_halo = core * t_height

    @pl.loop(0, REGION // 4)
    def _(block):
        for step in range(4):
            row = block * 4 + step
            parts = [turn(cells[pl.ds(region + row + col * LOCAL, layers, stride=height), :], 64) for col in range(3)]
            for col in range(3):
                heat[rows8(row * 24 + 8 * col), :] = jnp.where(low, parts[col], parts[(col + 1) % 3])

    @pl.loop(0, t_height // 4)
    def _(block):
        for step in range(4):
            row = block * 4 + step
            for col in range(2):
                part = t_cells[col, pl.ds(row, layers, stride=t_height), :]
                now[rows8((t_first + row) * 24 + 8 * col), :] = part
            now[rows8((t_first + row) * 24 + 16), :] = zero

    @pl.loop(0, 8)
    def _(row):
        for col in range(3):
            now[rows8((t_halo + row) * 24 + 8 * col), :] = zero


def solve_kernel(sides, bounds, *refs):
    count = len(sides)
    from_p, refs = refs[0], refs[1:]
    from_g, from_d, refs = refs[:count], refs[count : 2 * count], refs[2 * count :]
    heat_in, now_in, flow, material, conductivity = refs[:5]
    t_out, h_out, sent = refs[5:8]
    heat, now, later, cond, f_down, f_right, f_above, inverse, base, t_stage, h_stage, sems = refs[8:]
    core = lax.axis_index("ta")
    gx, gy = lax.axis_index("gx"), lax.axis_index("gy")
    lane = lane_ids()
    level = lax.broadcasted_iota(jnp.int32, (8, LANES), 0)
    low = lane < 64
    layers = 8
    depth = layers // 2
    edge = core * EDGE
    t_first = 8 - core * 8
    t_halo = core * (REGION - 8)

    def at(row, col):
        return rows8(row * 24 + 8 * col)

    def across(ref, row, height):
        return ref[pl.ds(row, layers, stride=height), :]

    def add(ref, row, col, value):
        ref[at(row, col), :] = ref[at(row, col), :] + value

    @pl.loop(0, REGION // 4)
    def _(block):
        for step in range(4):
            for col in range(3):
                where = at(block * 4 + step, col)
                heat[where, :] = heat_in[where, :]
                now[where, :] = now_in[where, :]

    def add_side(right, g_ref, d_ref):
        col = 1 if right else 0
        target = 0 if right else LANES - WIDE
        halo = (lane < WIDE) if right else (lane >= LANES - WIDE)
        main = (lane >= 64) if right else low

        @pl.loop(0, 8)
        def _(i):
            extra = across(g_ref, EDGE + i, ROWS_G)
            t_extra = across(g_ref, EDGE + 8 + i, ROWS_G)
            for j in range(9):
                value = across(g_ref, 8 * j + i, ROWS_G)
                turned = turn(value, 64)
                one, two = (turned, value) if right else (value, turned)
                add(heat, 8 * j + i, col, jnp.where(main, one, 0.0))
                add(heat, EDGE + 8 * j + i, col, jnp.where(main, two, 0.0))
            for j in range(18):
                add(heat, 8 * j + i, 2, jnp.where(halo, turn(extra, target - WIDE * j), 0.0))
            for j in range(17):
                add(now, t_first + 8 * j + i, 2, jnp.where(halo, turn(t_extra, target - WIDE * j), 0.0))
            extra = across(d_ref, 32 + i, ROWS_D)
            for j in range(9):
                value = across(d_ref, 8 * (j % 5) + i, ROWS_D)
                if (j < 5) == right:
                    value = turn(value, 64)
                add(heat, edge + 8 * j + i, col, jnp.where(main, value, 0.0))
                add(heat, edge + 8 * j + i, 2, jnp.where(halo, turn(extra, target - 64 - WIDE * j), 0.0))
            add(now, t_halo + i, 2, jnp.where(halo, turn(extra, target - 64 - 9 * WIDE), 0.0))

    halos = (lane < WIDE) | (lane >= LANES - WIDE)

    @pl.loop(0, 8)
    def _(i):
        extra = across(from_p, 2 * EDGE + i, ROWS_P)
        for j in range(9):
            row = edge + 8 * j + i
            for col in range(2):
                add(heat, row, col, across(from_p, col * EDGE + 8 * j + i, ROWS_P))
            add(heat, row, 2, jnp.where(halos, turn(extra, LANES - WIDE - 2 * WIDE * j), 0.0))
        for col in range(2):
            now[at(t_halo + i, col), :] = across(from_p, 2 * EDGE + 8 + 8 * col + i, ROWS_P)

    for side, g_ref, d_ref in zip(sides, from_g, from_d):
        if side is None:
            pl.when(gy == 0)(functools.partial(add_side, True, g_ref, d_ref))
            pl.when(gy > 0)(functools.partial(add_side, False, g_ref, d_ref))
        else:
            add_side(side, g_ref, d_ref)

    def to_stage(stage, src):
        @pl.loop(0, 16)
        def _(tile):
            for layer in range(layers):
                for col in range(2):
                    start = (8 + 8 * tile) * 24 + 8 * col + layer
                    value = src[pl.ds(start, 8, stride=24), :]
                    stage[layer, rows8(8 * tile), col * LANES : (col + 1) * LANES] = value

    def outputs(stage, which, out):
        mine = stage.at[pl.ds(core * depth, depth)]
        theirs = stage.at[pl.ds((1 - core) * depth, depth)]
        half = stage.shape[1]
        place = pl.ds(pl.multiple_of(core * half, half), half)
        return (
            pltpu.make_async_copy(theirs, sent.at[which], sems.at[which, 0]),
            pltpu.make_async_copy(mine, out.at[:, place, :], sems.at[which, 1]),
        )

    to_stage(h_stage, heat)
    for copy in outputs(h_stage, 1, h_out):
        copy.start()

    def to_right(values):
        moved = [turn(value, -1) for value in values]
        last = lane == LANES - 1
        return [jnp.where(last, moved[(col + 1) % 3], moved[col]) for col in range(3)]

    def to_left(values):
        moved = [turn(value, 1) for value in values]
        first = lane == 0
        return [jnp.where(first, moved[(col + 2) % 3], moved[col]) for col in range(3)]

    def upper(value):
        return pltpu.roll(value, 7, 0)

    def lower(value):
        return pltpu.roll(value, 1, 0)

    has_right = (gy + 1) * 256 < bounds[1]
    right_lanes = (lane < WIDE) & has_right
    left_lanes = (lane >= LANES - WIDE) & (gy > 0)
    one = jnp.full((8, LANES), 1.0, F32)
    col_masks = [one, one, jnp.where(right_lanes | left_lanes, 1.0, 0.0)]
    scale = jnp.full((8, LANES), conductivity[material[0]], F32)
    for layer in range(1, layers):
        scale = jnp.where(level == layer, conductivity[material[layer]], scale)
    scales = [scale * mask for mask in col_masks]
    not_top = jnp.where(level < layers - 1, 1.0, 0.0)
    not_bottom = jnp.where(level > 0, 1.0, 0.0)
    flows = [flow[:, col * LANES : (col + 1) * LANES] for col in range(3)]
    first_row = gx * 256 + core * 128 - 8

    def row_mask(row):
        place = first_row + row
        return jnp.where((place >= 0) & (place < bounds[0]), 1.0, 0.0)

    for ref in (now, later, cond, f_down):
        for row in (0, 1, REGION - 2, REGION - 1):
            for col in range(3):
                if ref is not now:
                    ref[at(row, col), :] = jnp.zeros((8, LANES), F32)

    def conductances(src, start, stop):
        @pl.loop(0, (stop - start) // 4)
        def _(block):
            for step in range(4):
                row = start + block * 4 + step
                mask = row_mask(row)
                for col in range(3):
                    where = at(row, col)
                    cond[where, :] = (scales[col] * mask) * (1.0 + 0.5 * jnp.tanh(src[where, :]))

    def coefficients(src, start, stop):
        @pl.loop(0, (stop - start) // 2)
        def _(block):
            first = start + block * 2
            lines = [[cond[at(first + step, col), :] for col in range(3)] for step in range(-1, 3)]
            for step in range(2):
                row = first + step
                up, here, down = lines[step], lines[step + 1], lines[step + 2]
                mask = row_mask(row)
                rights, lefts = to_right(here), to_left(here)
                for col in range(3):
                    where = at(row, col)
                    centre = here[col]
                    over = centre + upper(centre) * not_top
                    under = centre + lower(centre) * not_bottom
                    face_down = 0.5 * (centre + down[col])
                    face_right = 0.5 * (centre + rights[col])
                    total = (1.0 + flows[col]) + 0.5 * (centre + up[col]) + face_down
                    total = total + face_right + 0.5 * (centre + lefts[col]) + over + under
                    f_down[where, :] = face_down
                    f_right[where, :] = face_right
                    f_above[where, :] = over * not_top
                    inverse[where, :] = (mask * col_masks[col]) / total
                    base[where, :] = src[where, :] + heat[where, :]
            del lines

        for col in range(3):
            centre, down = cond[at(start - 1, col), :], cond[at(start, col), :]
            f_down[at(start - 1, col), :] = 0.5 * (centre + down)

    def sweep(src, dst, start, stop):
        @pl.loop(0, (stop - start) // 4)
        def _(block):
            first = start + block * 4
            lines = [[src[at(first + step, col), :] for col in range(3)] for step in range(-1, 5)]
            faces = [[f_down[at(first + step, col), :] for col in range(3)] for step in range(-1, 4)]
            for step in range(4):
                up, here, down = lines[step], lines[step + 1], lines[step + 2]
                sides_right = [f_right[at(first + step, col), :] for col in range(3)]
                rights = to_right(here)
                lefts = to_left([face * value for face, value in zip(sides_right, here)])
                for col in range(3):
                    where = at(first + step, col)
                    face_above = f_above[where, :]
                    total = base[where, :] + (faces[step][col] + flows[col]) * up[col]
                    total = total + faces[step + 1][col] * down[col]
                    total = total + (sides_right[col] * rights[col] + lefts[col])
                    total = total + (face_above * upper(here[col]) + lower(face_above * here[col]))
                    dst[where, :] = total * inverse[where, :]

    conductances(now, 2, 142)
    coefficients(now, 2, 142)
    sweep(now, later, 2, 142)
    sweep(later, now, 2, 142)
    sweep(now, later, 4, 140)
    conductances(later, 4, 140)
    coefficients(later, 6, 138)
    sweep(later, now, 6, 138)
    sweep(now, later, 6, 138)
    sweep(later, now, 8, 136)

    to_stage(t_stage, now)
    for copy in outputs(t_stage, 0, t_out):
        copy.start()
    for copy in outputs(h_stage, 1, h_out) + outputs(t_stage, 0, t_out):
        copy.wait()


def place_kernel(received, t_in, h_in, t_out, h_out, sems):
    core = lax.axis_index("ta")
    half = received.shape[2]
    place = pl.ds(pl.multiple_of((1 - core) * half, half), half)
    copies = [
        pltpu.make_async_copy(received.at[which], out.at[:, place, :], sems.at[which])
        for which, out in enumerate((t_out, h_out))
    ]
    for copy in copies:
        copy.start()
    for copy in copies:
        copy.wait()


def on_device(t_initial, power_mantissa, tile_exponent, channel_mask, material, conductivity):
    depth, rows, cols = t_initial.shape
    layers = 2 * depth
    n_gx, n_gy = lax.axis_size("gx"), lax.axis_size("gy")
    array = jax.ShapeDtypeStruct
    swap = [(0, 1), (1, 0)]

    t_other = lax.ppermute(t_initial, "ta", swap)
    local = array((depth, 3, LOCAL, LANES), F32)
    own, sent = pl.pallas_call(
        decode_kernel,
        out_shape=(local, local),
        in_specs=[VMEM, SMEM],
        out_specs=(ANY, ANY),
        scratch_shapes=[
            pltpu.VMEM((depth, 3, rows + 2 * RIM, LANES), F32),
            pltpu.SemaphoreType.DMA((depth,)),
            pltpu.SemaphoreType.DMA((depth,)),
        ],
        compiler_params=PARAMS,
        name="decode",
    )(power_mantissa, tile_exponent)
    other = lax.ppermute(sent, "ta", swap)

    out_sides = [None] if n_gy == 2 else [True, False]
    count = len(out_sides)
    packed = pl.pallas_call(
        functools.partial(pack_kernel, out_sides),
        out_shape=(array((layers, ROWS_P, LANES), F32),)
        + (array((layers, ROWS_G, LANES), F32),) * count
        + (array((layers, ROWS_D, LANES), F32),) * count,
        in_specs=[VMEM] * 4,
        out_specs=(VMEM,) * (1 + 2 * count),
        compiler_params=PARAMS,
        name="pack",
    )(own, other, t_initial, t_other)

    def moves(shift):
        pairs = []
        for z in range(n_gx):
            for x in range(n_gy):
                for c in range(2):
                    to_z = z + 2 * c - 1
                    to_x = x ^ 1 if shift is None else x + shift
                    if 0 <= to_z < n_gx and 0 <= to_x < n_gy:
                        pairs.append(((z * n_gy + x) * 2 + c, (to_z * n_gy + to_x) * 2 + 1 - c))
        return pairs

    along = ("gx", "gy", "ta")
    shifts = [None] if n_gy == 2 else [1, -1]
    from_g = []
    for shift, value in zip(shifts, packed[1 : 1 + count]):
        pairs = swap if shift is None else [(x, x + shift) for x in range(n_gy) if 0 <= x + shift < n_gy]
        from_g.append(lax.ppermute(value, "gy", pairs))
    from_d = [lax.ppermute(value, along, moves(shift)) for shift, value in zip(shifts, packed[1 + count :])]
    from_p = lax.ppermute(packed[0], along, moves(0))
    in_sides = [None] if n_gy == 2 else [False, True]

    wide = jnp.pad(channel_mask, ((0, 0), (RIM, RIM)))
    mask = lax.dynamic_slice_in_dim(wide, lax.axis_index("gy") * cols, cols + 2 * RIM, 1)
    flow = COOLANT * jnp.concatenate([mask[:, RIM:], mask[:, :RIM]], axis=1).astype(F32)

    stacked = array((REGION * 24, LANES), F32)
    heat, now = pl.pallas_call(
        stack_kernel,
        out_shape=(stacked, stacked),
        in_specs=[ANY] * 4,
        out_specs=(VMEM, VMEM),
        scratch_shapes=[
            pltpu.VMEM((layers * 3 * LOCAL, LANES), F32),
            pltpu.VMEM((2, layers * (REGION - 8), LANES), F32),
            pltpu.SemaphoreType.DMA((2,)),
            pltpu.SemaphoreType.DMA((2, depth, 2)),
        ],
        compiler_params=PARAMS,
        name="stack",
    )(own.reshape(-1, LANES), other.reshape(-1, LANES), t_initial, t_other)

    whole = array((depth, rows, cols), F32)
    half = array((2, depth, rows // 2, cols), F32)
    inner = pltpu.VMEM((REGION * 24, LANES), F32)
    stage = pltpu.VMEM((layers, rows // 2, cols), F32)

    def flat(value):
        return value.reshape(-1, LANES)

    t_part, h_part, sent = pl.pallas_call(
        functools.partial(solve_kernel, in_sides, (n_gx * rows, n_gy * cols)),
        out_shape=(whole, whole, half),
        in_specs=[VMEM] * (1 + 2 * count + 3) + [SMEM, SMEM],
        out_specs=(ANY, ANY, ANY),
        scratch_shapes=[inner] * 9 + [stage, stage, pltpu.SemaphoreType.DMA((2, 2))],
        compiler_params=PARAMS,
        name="solve",
    )(flat(from_p), *map(flat, from_g), *map(flat, from_d), heat, now, flow, material, conductivity)
    received = lax.ppermute(sent, "ta", swap)
    return pl.pallas_call(
        place_kernel,
        out_shape=(whole, whole),
        in_specs=[ANY, ANY, ANY],
        out_specs=(ANY, ANY),
        scratch_shapes=[pltpu.SemaphoreType.DMA((2,))],
        input_output_aliases={1: 0, 2: 1},
        compiler_params=PARAMS,
        name="place",
    )(received, t_part, h_part)


def solution(mesh):
    cells = P("ta", ("group", "gx"), "gy")
    return jax.shard_map(
        on_device,
        mesh=mesh,
        in_specs=(cells, cells, cells, P(), P(), P()),
        out_specs=(cells, cells),
        check_vma=False,
    )
```

```python
import functools

import jax
import jax.numpy as jnp
from jax import lax
from jax.experimental import pallas as pl
from jax.experimental.pallas import tpu as pltpu
from jax.sharding import PartitionSpec as P

RIM = 64
TILE = 64
STEPS = 2
SWEEPS = 3
COOLANT = 2.0

LANES = 128
WIDE = 6
LOCAL = 200
REGION = 140
STEP_ROWS = 70
BLOCK = 10
SPAN = 5
EDGE = 72
ROWS_P = 2 * EDGE + 8 + 16
ROWS_G = EDGE + 16
ROWS_D = 40
F32 = jnp.float32
VMEM = pl.BlockSpec(memory_space=pltpu.VMEM)
SMEM = pl.BlockSpec(memory_space=pltpu.SMEM)
ANY = pl.BlockSpec(memory_space=pl.ANY)
PARAMS = pltpu.CompilerParams(vmem_limit_bytes=48 << 20)


def rows8(start):
    return pl.ds(pl.multiple_of(start, 8), 8)


def lane_ids():
    return lax.broadcasted_iota(jnp.int32, (8, LANES), 1)


def turn(value, shift):
    shift = shift % LANES
    return pltpu.roll(value, shift, 1) if shift else value


def decode_kernel(mantissa, exponent, own, sent, plain, own_sem, sent_sem):
    core = lax.axis_index("ta")
    depth, rows, _ = mantissa.shape
    tiles = rows // TILE
    wide_lane = lax.broadcasted_iota(jnp.int32, (16, LANES), 1)
    first = pl.multiple_of(core * 184, 8)
    other = pl.multiple_of(184 - core * 184, 8)

    def copies(layer):
        return (
            pltpu.make_async_copy(plain.at[layer, :, pl.ds(other, LOCAL), :], sent.at[layer], sent_sem.at[layer]),
            pltpu.make_async_copy(plain.at[layer, :, pl.ds(first, LOCAL), :], own.at[layer], own_sem.at[layer]),
        )

    for layer in range(depth):

        @pl.loop(0, tiles)
        def _(tile_row):
            for col in range(3):
                low = exponent[layer, tile_row, 2 * col]
                high = exponent[layer, tile_row, 2 * col + 1]
                scale = jnp.exp2(jnp.where(wide_lane < TILE, low, high).astype(F32))
                for part in range(TILE // 16):
                    where = pl.ds(pl.multiple_of(tile_row * TILE + part * 16, 16), 16)
                    cells = mantissa[layer, where, col * LANES : (col + 1) * LANES]
                    plain[layer, col, where, :] = cells.astype(F32) * scale

        for copy in copies(layer):
            copy.start()
    for layer in range(depth):
        for copy in copies(layer):
            copy.wait()


def pack_kernel(sides, own, other, t_own, t_other, *outs):
    core = lax.axis_index("ta")
    lane = lane_ids()
    low = lane < 64
    to_p, to_g, to_d = outs[0], outs[1 : 1 + len(sides)], outs[1 + len(sides) :]
    edge = core * 128
    region = 56 - core * 56
    t_row = core * 120
    t_edge = core * 248

    def place(total, value, source, target, width):
        moved = turn(value, target - source)
        return jnp.where((lane >= target) & (lane < target + width), moved, total)

    def one(src, t_src, index, layer):
        def cells(col, row):
            return src[index, col, rows8(row), :]

        def t_cells(col, row):
            return t_src[index, rows8(row), col * LANES : (col + 1) * LANES]

        extra = jnp.zeros((8, LANES), F32)
        for j in range(9):
            left, middle, right = (cells(col, edge + 8 * j) for col in range(3))
            one, two, three = turn(left, 64), turn(middle, 64), turn(right, 64)
            to_p[layer, 8 * j : 8 * j + 8, :] = jnp.where(low, one, two)
            to_p[layer, EDGE + 8 * j : EDGE + 8 * j + 8, :] = jnp.where(low, two, three)
            extra = place(extra, jnp.where(low, left, right), 64 - WIDE, 2 * WIDE * j, 2 * WIDE)
        to_p[layer, 2 * EDGE : 2 * EDGE + 8, :] = extra
        for col in range(2):
            start = 2 * EDGE + 8 + 8 * col
            to_p[layer, start : start + 8, :] = t_cells(col, t_edge)

        def side_parts(right, g_ref, d_ref):
            col, t_col = (2, 1) if right else (0, 0)
            at, t_at = (LANES - WIDE, LANES - WIDE) if right else (64, 0)

            def strip(row):
                value = cells(col, row)
                return turn(value, 64) if right else value

            extra = jnp.zeros((8, LANES), F32)
            for j in range(9):
                one_strip, two_strip = strip(region + 8 * j), strip(region + EDGE + 8 * j)
                g_ref[layer, 8 * j : 8 * j + 8, :] = jnp.where(low, one_strip, turn(two_strip, 64))
                extra = place(extra, one_strip, at, WIDE * j, WIDE)
                extra = place(extra, two_strip, at, WIDE * (j + 9), WIDE)
            g_ref[layer, EDGE : EDGE + 8, :] = extra
            extra = jnp.zeros((8, LANES), F32)
            for j in range(17):
                extra = place(extra, t_cells(t_col, t_row + 8 * j), t_at, WIDE * j, WIDE)
            g_ref[layer, EDGE + 8 : EDGE + 16, :] = extra
            strips = [strip(edge + 8 * j) for j in range(9)]
            for j in range(4):
                d_ref[layer, 8 * j : 8 * j + 8, :] = jnp.where(low, strips[j], turn(strips[j + 5], 64))
            extra = strips[4]
            for j in range(9):
                extra = place(extra, strips[j], at, 64 + WIDE * j, WIDE)
            extra = place(extra, t_cells(t_col, t_edge), t_at, 64 + 9 * WIDE, WIDE)
            d_ref[layer, 32:40, :] = extra

        for side, g_ref, d_ref in zip(sides, to_g, to_d):
            if side is None:
                first = lax.axis_index("gy") == 0
                pl.when(first)(functools.partial(side_parts, True, g_ref, d_ref))
                pl.when(jnp.logical_not(first))(functools.partial(side_parts, False, g_ref, d_ref))
            else:
                side_parts(side, g_ref, d_ref)

    depth = own.shape[0]

    @pl.loop(0, depth)
    def _(index):
        one(own, t_own, index, core * depth + index)
        one(other, t_other, index, (1 - core) * depth + index)


def permutation(inverse):
    rows = lax.broadcasted_iota(jnp.int32, (256, 256), 0)
    cols = lax.broadcasted_iota(jnp.int32, (256, 256), 1)
    if inverse:
        rows, cols = cols, rows
    return jnp.where(rows == 4 * (cols % 64) + cols // 64, 1.0, 0.0).astype(jnp.bfloat16)


def permuted(value, matrix):
    total = None
    for _ in range(3):
        part = value.astype(jnp.bfloat16)
        value = value - part.astype(F32)
        moved = jnp.dot(part, matrix, preferred_element_type=F32)
        total = moved if total is None else total + moved
    return total


def to_groups(first, second):
    low = lane_ids() < 64
    out = []
    for half in range(2):
        one = first[:, half * LANES : (half + 1) * LANES]
        two = second[:, half * LANES : (half + 1) * LANES]
        out += [jnp.where(low, one, turn(two, 64)), jnp.where(low, turn(one, 64), two)]
    return out


def to_rows(parts):
    low = lane_ids() < 64
    one, two = [], []
    for half in range(2):
        left, right = parts[2 * half], parts[2 * half + 1]
        one.append(jnp.where(low, left, turn(right, 64)))
        two.append(jnp.where(low, turn(left, 64), right))
    return jnp.concatenate(one, axis=1), jnp.concatenate(two, axis=1)


def group_cells(src, dst, matrix, stop=None):
    @pl.loop(0, STEP_ROWS // BLOCK)
    def _(block):
        values = []
        for group in range(2):
            where = pl.ds(pl.multiple_of((group * STEP_ROWS + block * BLOCK) * 8, 8), BLOCK * 8)
            values.append(permuted(jnp.concatenate([src[0, where, :], src[1, where, :]], axis=1), matrix))
        for step in range(BLOCK):
            parts = to_groups(*(value[8 * step : 8 * step + 8] for value in values))
            for col in range(4):
                dst[rows8((block * BLOCK + step + 1) * 40 + 8 * col), :] = parts[col]


def stack_kernel(own, other, t_own, t_other, heat, heat_halo, now, cells, t_cells, t_rows, sems, t_sems):
    core = lax.axis_index("ta")
    low = lane_ids() < 64
    zero = jnp.zeros((8, LANES), F32)
    depth, rows, _ = t_own.shape
    layers = 2 * depth
    height = own.shape[0] // depth
    t_height = 136
    copies = []
    for which, (src, t_src) in enumerate(((own, t_own), (other, t_other))):
        base = core * depth if which == 0 else (1 - core) * depth
        start = pl.multiple_of(base * height, 8)
        copies.append(pltpu.make_async_copy(src, cells.at[pl.ds(start, depth * height), :], sems.at[which]))
        for layer in range(depth):
            for col in range(2):
                row = pl.multiple_of(core * 120, 8)
                start = pl.multiple_of((base + layer) * t_height, 8)
                copies.append(
                    pltpu.make_async_copy(
                        t_src.at[layer, pl.ds(row, t_height), col * LANES : (col + 1) * LANES],
                        t_cells.at[col, pl.ds(start, t_height), :],
                        t_sems.at[which, layer, col],
                    )
                )
    for copy in copies:
        copy.start()
    for copy in copies:
        copy.wait()
    region = 58 - core * 56

    @pl.loop(0, REGION // 4)
    def _(block):
        for step in range(4):
            row = block * 4 + step
            parts = [turn(cells[pl.ds(region + row + col * LOCAL, layers, stride=height), :], 64) for col in range(3)]
            for col in range(2):
                heat[col, rows8(row * 8), :] = jnp.where(low, parts[col], parts[col + 1])
            heat_halo[rows8(row * 8), :] = jnp.where(low, parts[2], parts[0])

    @pl.loop(0, (REGION - 6) // 2)
    def _(block):
        for step in range(2):
            row = block * 2 + step
            for col in range(2):
                part = t_cells[col, pl.ds(2 * core + row, layers, stride=t_height), :]
                t_rows[col, rows8((6 - 6 * core + row) * 8), :] = part

    for row in range(6):
        for col in range(2):
            t_rows[col, rows8((134 * core + row) * 8), :] = zero
    group_cells(t_rows, now, permutation(False))

    @pl.loop(0, STEP_ROWS + 2)
    def _(step):
        now[rows8(step * 40 + 32), :] = zero


def solve_kernel(sides, bounds, *refs):
    count = len(sides)
    from_p, refs = refs[0], refs[1:]
    from_g, from_d, refs = refs[:count], refs[count : 2 * count], refs[2 * count :]
    heat_in, halo_in, now_in, flow, material, conductivity = refs[:6]
    t_out, h_out, sent = refs[6:9]
    rows_heat, rows_halo, rows_t, t_halo, heat, now, later, cond = refs[9:17]
    f_down, f_right, f_above, inverse, base, t_stage, h_stage, sems = refs[17:]
    core = lax.axis_index("ta")
    gx, gy = lax.axis_index("gx"), lax.axis_index("gy")
    lane = lane_ids()
    level = lax.broadcasted_iota(jnp.int32, (8, LANES), 0)
    low = lane < 64
    zero = jnp.zeros((8, LANES), F32)
    layers = 8
    depth = layers // 2

    def at(step, col):
        return rows8(step * 40 + 8 * col)

    def across(ref, row, height):
        return ref[pl.ds(row, layers, stride=height), :]

    def add_side(right, fresh, g_ref, d_ref):
        col = 1 if right else 0
        target = 0 if right else LANES - WIDE
        halo = (lane < WIDE) if right else (lane >= LANES - WIDE)
        main = (lane >= 64) if right else low
        heat_from, halo_from = (heat_in, halo_in) if fresh else (rows_heat, rows_halo)

        @pl.loop(0, 8)
        def _(i):
            extra = across(g_ref, EDGE + i, ROWS_G)
            t_extra = across(g_ref, EDGE + 8 + i, ROWS_G)
            for j in range(9):
                value = across(g_ref, 8 * j + i, ROWS_G)
                turned = turn(value, 64)
                for k, part in ((j, turned if right else value), (j + 9, value if right else turned)):
                    row = 8 * k + i - 2

                    def put():
                        where = rows8(row * 8)
                        rows_heat[col, where, :] = heat_from[col, where, :] + jnp.where(main, part, 0.0)
                        if fresh:
                            rows_heat[1 - col, where, :] = heat_from[1 - col, where, :]
                        moved = turn(extra, target - WIDE * k)
                        rows_halo[where, :] = halo_from[where, :] + jnp.where(halo, moved, 0.0)

                    if k == 0:
                        pl.when(i >= 2)(put)
                    elif k == 17:
                        pl.when(i < 6)(put)
                    else:
                        put()
            for j in range(17):
                row = 8 * j + i
                where = rows8((row + 8 - 8 * core) * 8)
                t_halo[where, :] = t_halo[where, :] + jnp.where(halo, turn(t_extra, target - WIDE * j), 0.0)
            extra = across(d_ref, 32 + i, ROWS_D)
            where = rows8((core * 136 + i) * 8)
            t_halo[where, :] = t_halo[where, :] + jnp.where(halo, turn(extra, target - 64 - 9 * WIDE), 0.0)

        @pl.loop(0, 8)
        def _(i):
            extra = across(d_ref, 32 + i, ROWS_D)
            for j in range(9):
                value = across(d_ref, 8 * (j % 5) + i, ROWS_D)
                if (j < 5) == right:
                    value = turn(value, 64)

                def put():
                    where = rows8((edge + 8 * j + i) * 8)
                    rows_heat[col, where, :] = rows_heat[col, where, :] + jnp.where(main, value, 0.0)
                    moved = turn(extra, target - 64 - WIDE * j)
                    rows_halo[where, :] = rows_halo[where, :] + jnp.where(halo, moved, 0.0)

                edge_row(i, j, put)

    halos = (lane < WIDE) | (lane >= LANES - WIDE)
    edge = core * EDGE - 2

    def edge_row(i, j, put):
        row = edge + 8 * j + i
        if j in (0, 8):
            pl.when((row >= 0) & (row < REGION))(put)
        else:
            put()

    @pl.loop(0, 144 // 4)
    def _(block):
        for step in range(4):
            t_halo[rows8((block * 4 + step) * 8), :] = zero

    for place, (side, g_ref, d_ref) in enumerate(zip(sides, from_g, from_d)):
        if side is None:
            pl.when(gy == 0)(functools.partial(add_side, True, True, g_ref, d_ref))
            pl.when(gy > 0)(functools.partial(add_side, False, True, g_ref, d_ref))
        else:
            add_side(side, place == 0, g_ref, d_ref)

    @pl.loop(0, 8)
    def _(i):
        extra = across(from_p, 2 * EDGE + i, ROWS_P)
        for j in range(9):

            def put():
                where = rows8((edge + 8 * j + i) * 8)
                for col in range(2):
                    part = across(from_p, col * EDGE + 8 * j + i, ROWS_P)
                    rows_heat[col, where, :] = rows_heat[col, where, :] + part
                moved = turn(extra, LANES - WIDE - 2 * WIDE * j)
                rows_halo[where, :] = rows_halo[where, :] + jnp.where(halos, moved, 0.0)

            edge_row(i, j, put)

    def to_stage(stage, src):
        @pl.loop(0, 16)
        def _(tile):
            for layer in range(layers):
                for col in range(2):
                    value = src[col, pl.ds((6 + 8 * tile) * 8 + layer, 8, stride=8), :]
                    stage[layer, rows8(8 * tile), col * LANES : (col + 1) * LANES] = value

    def outputs(stage, which, out):
        mine = stage.at[pl.ds(core * depth, depth)]
        theirs = stage.at[pl.ds((1 - core) * depth, depth)]
        half = stage.shape[1]
        place = pl.ds(pl.multiple_of(core * half, half), half)
        return (
            pltpu.make_async_copy(theirs, sent.at[which], sems.at[which, 0]),
            pltpu.make_async_copy(mine, out.at[:, place, :], sems.at[which, 1]),
        )

    to_stage(h_stage, rows_heat)
    for copy in outputs(h_stage, 1, h_out):
        copy.start()

    matrix = permutation(False)
    group_cells(rows_heat, heat, matrix)

    def spread_halo(first, second):
        moved = jnp.where(lane < 64 + WIDE, turn(first, 64), first)
        other = jnp.where(lane < WIDE, second, turn(second, 64))
        value = jnp.where(low, other, moved)
        keep = (lane < WIDE) | ((lane >= 64 - WIDE) & (lane < 64 + WIDE)) | (lane >= LANES - WIDE)
        return jnp.where(keep, value, 0.0)

    t_edge = jnp.concatenate(
        [
            jnp.concatenate([across(from_p, 2 * EDGE + 8 + 8 * col + i, ROWS_P) for i in range(8)], axis=0)
            for col in range(2)
        ],
        axis=1,
    )
    t_edge = permuted(t_edge, matrix)

    @pl.loop(0, STEP_ROWS // 2)
    def _(block):
        for part in range(2):
            step = block * 2 + part
            first, second = rows8(step * 8), rows8((step + STEP_ROWS) * 8)
            heat[at(step + 1, 4), :] = spread_halo(rows_halo[first, :], rows_halo[second, :])
            first, second = rows8((step + 2) * 8), rows8((step + STEP_ROWS + 2) * 8)
            now[at(step + 1, 4), :] = spread_halo(t_halo[first, :], t_halo[second, :])
            for col in range(4):
                now[at(step + 1, col), :] = now_in[at(step + 1, col), :]

    @pl.when(core == 0)
    def _():
        for row in range(6):
            value = t_edge[8 * row + 16 : 8 * row + 24]
            parts = to_groups(value, value)
            for col in range(4):
                now[at(row + 1, col), :] = jnp.where(low, parts[col], now[at(row + 1, col), :])

    @pl.when(core == 1)
    def _():
        for row in range(6):
            value = t_edge[8 * row : 8 * row + 8]
            parts = to_groups(value, value)
            for col in range(4):
                now[at(row + 65, col), :] = jnp.where(low, now[at(row + 65, col), :], parts[col])

    def ghosts(ref):
        for col in range(5):
            ref[at(0, col), :] = turn(ref[at(STEP_ROWS, col), :], 64)
            ref[at(STEP_ROWS + 1, col), :] = turn(ref[at(1, col), :], 64)

    last = (lane == 63) | (lane == 127)
    first = (lane == 0) | (lane == 64)

    def to_right(values):
        inner, outer = turn(values[0], -1), turn(values[4], -1)
        return values[1:4] + [jnp.where(last, outer, inner), jnp.where(last, inner, outer)]

    def to_left(values):
        inner, outer = turn(values[3], 1), turn(values[4], 1)
        return [jnp.where(first, outer, inner)] + values[:3] + [jnp.where(first, inner, outer)]

    def upper(value):
        return pltpu.roll(value, 7, 0)

    def lower(value):
        return pltpu.roll(value, 1, 0)

    has_right = (gy + 1) * 256 < bounds[1]
    half_lane = jnp.where(low, lane, lane - 64)
    keep = ((half_lane < WIDE) & has_right) | ((half_lane >= 64 - WIDE) & (gy > 0))
    halo_mask = jnp.where(keep, 1.0, 0.0)
    scale = jnp.full((8, LANES), conductivity[material[0]], F32)
    for layer in range(1, layers):
        scale = jnp.where(level == layer, conductivity[material[layer]], scale)
    not_top = jnp.where(level < layers - 1, 1.0, 0.0)
    not_bottom = jnp.where(level > 0, 1.0, 0.0)
    flows = [flow[8 * col : 8 * col + 8, :] for col in range(5)]
    first_row = gx * 256 + core * 128 - 6

    def masks(step):
        ones = []
        for group in range(2):
            row = first_row + step + group * STEP_ROWS
            ones.append(jnp.where((row >= 0) & (row < bounds[0]), 1.0, 0.0))
        inner = jnp.where(low, ones[0], ones[1])
        return [inner] * 4 + [jnp.where(low, ones[1], ones[0]) * halo_mask]

    def conductances(src):
        @pl.loop(0, STEP_ROWS // 5)
        def _(block):
            for part in range(5):
                step = block * 5 + part
                mask = masks(step)
                for col in range(5):
                    where = at(step + 1, col)
                    cond[where, :] = (scale * mask[col]) * (1.0 + 0.5 * jnp.tanh(src[where, :]))

        ghosts(cond)

    def coefficients(src):
        @pl.loop(0, STEP_ROWS // 5)
        def _(block):
            start = block * 5
            lines = [[cond[at(start + part, col), :] for col in range(5)] for part in range(7)]
            for part in range(5):
                up, here, down = lines[part], lines[part + 1], lines[part + 2]
                mask = masks(start + part)
                rights, lefts = to_right(here), to_left(here)
                for col in range(5):
                    where = at(start + part + 1, col)
                    centre = here[col]
                    over = centre + upper(centre) * not_top
                    under = centre + lower(centre) * not_bottom
                    face_down = 0.5 * (centre + down[col])
                    face_right = 0.5 * (centre + rights[col])
                    total = (1.0 + flows[col]) + 0.5 * (centre + up[col]) + face_down
                    total = total + face_right + 0.5 * (centre + lefts[col]) + over + under
                    f_down[where, :] = face_down
                    f_right[where, :] = face_right
                    f_above[where, :] = over * not_top
                    inverse[where, :] = mask[col] / total
                    base[where, :] = src[where, :] + heat[where, :]

        for col in range(5):
            f_down[at(0, col), :] = 0.5 * (cond[at(0, col), :] + cond[at(1, col), :])

    def sweep(src, dst):
        @pl.loop(0, STEP_ROWS // SPAN)
        def _(block):
            start = block * SPAN
            lines = [[src[at(start + part, col), :] for col in range(5)] for part in range(SPAN + 2)]
            faces = [[f_down[at(start + part, col), :] for col in range(5)] for part in range(SPAN + 1)]
            for part in range(SPAN):
                up, here, down = lines[part], lines[part + 1], lines[part + 2]
                face_right = [f_right[at(start + part + 1, col), :] for col in range(5)]
                rights = to_right(here)
                lefts = to_left([face * value for face, value in zip(face_right, here)])
                for col in range(5):
                    where = at(start + part + 1, col)
                    face_above = f_above[where, :]
                    total = base[where, :] + (faces[part][col] + flows[col]) * up[col]
                    total = total + faces[part + 1][col] * down[col]
                    total = total + (face_right[col] * rights[col] + lefts[col])
                    total = total + (face_above * upper(here[col]) + lower(face_above * here[col]))
                    dst[where, :] = total * inverse[where, :]

        ghosts(dst)

    ghosts(now)
    for _ in range(STEPS):
        conductances(now)
        coefficients(now)
        for _ in range(SWEEPS):
            sweep(now, later)
            now, later = later, now

    back = permutation(True)

    @pl.loop(0, STEP_ROWS // BLOCK)
    def _(block):
        values = ([], [])
        for part in range(BLOCK):
            pair = to_rows([now[at(block * BLOCK + part + 1, col), :] for col in range(4)])
            for group in range(2):
                values[group].append(pair[group])
        for group in range(2):
            value = permuted(jnp.concatenate(values[group], axis=0), back)
            where = pl.ds(pl.multiple_of((group * STEP_ROWS + block * BLOCK) * 8, 8), BLOCK * 8)
            for col in range(2):
                rows_t[col, where, :] = value[:, col * LANES : (col + 1) * LANES]

    to_stage(t_stage, rows_t)
    for copy in outputs(t_stage, 0, t_out):
        copy.start()
    for copy in outputs(h_stage, 1, h_out) + outputs(t_stage, 0, t_out):
        copy.wait()


def place_kernel(received, t_in, h_in, t_out, h_out, sems):
    core = lax.axis_index("ta")
    half = received.shape[2]
    place = pl.ds(pl.multiple_of((1 - core) * half, half), half)
    copies = [
        pltpu.make_async_copy(received.at[which], out.at[:, place, :], sems.at[which])
        for which, out in enumerate((t_out, h_out))
    ]
    for copy in copies:
        copy.start()
    for copy in copies:
        copy.wait()


def on_device(t_initial, power_mantissa, tile_exponent, channel_mask, material, conductivity):
    depth, rows, cols = t_initial.shape
    layers = 2 * depth
    n_gx, n_gy = lax.axis_size("gx"), lax.axis_size("gy")
    array = jax.ShapeDtypeStruct
    swap = [(0, 1), (1, 0)]

    t_other = lax.ppermute(t_initial, "ta", swap)
    local = array((depth, 3, LOCAL, LANES), F32)
    own, sent = pl.pallas_call(
        decode_kernel,
        out_shape=(local, local),
        in_specs=[VMEM, SMEM],
        out_specs=(ANY, ANY),
        scratch_shapes=[
            pltpu.VMEM((depth, 3, rows + 2 * RIM, LANES), F32),
            pltpu.SemaphoreType.DMA((depth,)),
            pltpu.SemaphoreType.DMA((depth,)),
        ],
        compiler_params=PARAMS,
        name="decode",
    )(power_mantissa, tile_exponent)
    other = lax.ppermute(sent, "ta", swap)

    out_sides = [None] if n_gy == 2 else [True, False]
    count = len(out_sides)
    packed = pl.pallas_call(
        functools.partial(pack_kernel, out_sides),
        out_shape=(array((layers, ROWS_P, LANES), F32),)
        + (array((layers, ROWS_G, LANES), F32),) * count
        + (array((layers, ROWS_D, LANES), F32),) * count,
        in_specs=[VMEM] * 4,
        out_specs=(VMEM,) * (1 + 2 * count),
        compiler_params=PARAMS,
        name="pack",
    )(own, other, t_initial, t_other)

    def moves(shift):
        pairs = []
        for z in range(n_gx):
            for x in range(n_gy):
                for c in range(2):
                    to_z = z + 2 * c - 1
                    to_x = x ^ 1 if shift is None else x + shift
                    if 0 <= to_z < n_gx and 0 <= to_x < n_gy:
                        pairs.append(((z * n_gy + x) * 2 + c, (to_z * n_gy + to_x) * 2 + 1 - c))
        return pairs

    along = ("gx", "gy", "ta")
    shifts = [None] if n_gy == 2 else [1, -1]
    from_g = []
    for shift, value in zip(shifts, packed[1 : 1 + count]):
        pairs = swap if shift is None else [(x, x + shift) for x in range(n_gy) if 0 <= x + shift < n_gy]
        from_g.append(lax.ppermute(value, "gy", pairs))
    from_d = [lax.ppermute(value, along, moves(shift)) for shift, value in zip(shifts, packed[1 + count :])]
    from_p = lax.ppermute(packed[0], along, moves(0))
    in_sides = [None] if n_gy == 2 else [False, True]

    wide = jnp.pad(channel_mask, ((0, 0), (RIM, RIM)))
    mask = lax.dynamic_slice_in_dim(wide, lax.axis_index("gy") * cols, cols + 2 * RIM, 1).astype(F32) * COOLANT
    inner = mask[:, RIM : RIM + cols].reshape(layers, 64, 4).transpose(2, 0, 1)
    outer = jnp.zeros((layers, 64 - 2 * WIDE), F32)
    outer = jnp.concatenate([mask[:, RIM + cols :][:, :WIDE], outer, mask[:, RIM - WIDE : RIM]], axis=1)
    flow = jnp.concatenate([inner, outer[None]], axis=0).reshape(layers * 5, 64)
    flow = jnp.concatenate([flow, flow], axis=1)

    natural = array((2, REGION * 8, LANES), F32)
    edge = array((REGION * 8, LANES), F32)
    grouped = array(((STEP_ROWS + 2) * 40, LANES), F32)
    heat, heat_halo, now = pl.pallas_call(
        stack_kernel,
        out_shape=(natural, edge, grouped),
        in_specs=[ANY] * 4,
        out_specs=(VMEM, VMEM, VMEM),
        scratch_shapes=[
            pltpu.VMEM((layers * 3 * LOCAL, LANES), F32),
            pltpu.VMEM((2, layers * 136, LANES), F32),
            pltpu.VMEM(natural.shape, F32),
            pltpu.SemaphoreType.DMA((2,)),
            pltpu.SemaphoreType.DMA((2, depth, 2)),
        ],
        compiler_params=PARAMS,
        name="stack",
    )(own.reshape(-1, LANES), other.reshape(-1, LANES), t_initial, t_other)

    whole = array((depth, rows, cols), F32)
    half = array((2, depth, rows // 2, cols), F32)
    work = pltpu.VMEM(grouped.shape, F32)
    stage = pltpu.VMEM((layers, rows // 2, cols), F32)

    def flat(value):
        return value.reshape(-1, LANES)

    t_part, h_part, sent = pl.pallas_call(
        functools.partial(solve_kernel, in_sides, (n_gx * rows, n_gy * cols)),
        out_shape=(whole, whole, half),
        in_specs=[VMEM] * (1 + 2 * count + 4) + [SMEM, SMEM],
        out_specs=(ANY, ANY, ANY),
        scratch_shapes=[
            pltpu.VMEM(natural.shape, F32),
            pltpu.VMEM(edge.shape, F32),
            pltpu.VMEM(natural.shape, F32),
            pltpu.VMEM((144 * 8, LANES), F32),
        ]
        + [work] * 9
        + [stage, stage, pltpu.SemaphoreType.DMA((2, 2))],
        compiler_params=PARAMS,
        name="solve",
    )(flat(from_p), *map(flat, from_g), *map(flat, from_d), heat, heat_halo, now, flow, material, conductivity)
    received = lax.ppermute(sent, "ta", swap)
    return pl.pallas_call(
        place_kernel,
        out_shape=(whole, whole),
        in_specs=[ANY, ANY, ANY],
        out_specs=(ANY, ANY),
        scratch_shapes=[pltpu.SemaphoreType.DMA((2,))],
        input_output_aliases={1: 0, 2: 1},
        compiler_params=PARAMS,
        name="place",
    )(received, t_part, h_part)


def solution(mesh):
    cells = P("ta", ("group", "gx"), "gy")
    return jax.shard_map(
        on_device,
        mesh=mesh,
        in_specs=(cells, cells, cells, P(), P(), P()),
        out_specs=(cells, cells),
        check_vma=False,
    )
```

```python
import functools

import jax
import jax.numpy as jnp
from jax import lax
from jax.experimental import pallas as pl
from jax.experimental.pallas import tpu as pltpu
from jax.sharding import PartitionSpec as P

RIM = 64
TILE = 64
STEPS = 2
SWEEPS = 3
COOLANT = 2.0

LANES = 128
WIDE = 6
REGION = 140
STEP_ROWS = 70
BLOCK = 35
SPAN = 5
SUM_ROWS = 272
HALF_ROWS = 144
SWAP = 3 * HALF_ROWS + 16
EDGE = 72
SLOTS = LANES // WIDE
ROWS_P = 2 * EDGE + 8 + 16
ROWS_G = SUM_ROWS // 2 + 16 + 16
ROWS_D = 40
F32 = jnp.float32
VMEM = pl.BlockSpec(memory_space=pltpu.VMEM)
SMEM = pl.BlockSpec(memory_space=pltpu.SMEM)
ANY = pl.BlockSpec(memory_space=pl.ANY)


def params(megabytes):
    return pltpu.CompilerParams(vmem_limit_bytes=megabytes << 20)


def rows8(start):
    return pl.ds(pl.multiple_of(start, 8), 8)


def lane_ids():
    return lax.broadcasted_iota(jnp.int32, (8, LANES), 1)


def turn(value, shift):
    shift = shift % LANES
    return pltpu.roll(value, shift, 1) if shift else value


def by_side(sides, body, *lists):
    for place, side in enumerate(sides):
        rest = [values[place] for values in lists]
        if side is None:
            first = lax.axis_index("gy") == 0
            pl.when(first)(functools.partial(body, True, place, *rest))
            pl.when(jnp.logical_not(first))(functools.partial(body, False, place, *rest))
        else:
            body(side, place, *rest)


def send_kernel(sides, mantissa, exponent, t_ref, *refs):
    count = len(sides)
    whole, to_up, to_down = refs[:3]
    to_g, to_d_up, to_d_down = refs[3 : 3 + count], refs[3 + count : 3 + 2 * count], refs[3 + 2 * count : 3 + 3 * count]
    plain, sems = refs[3 + 3 * count :]
    depth, rows, _ = mantissa.shape
    lane = lane_ids()
    low = lane < 64
    wide_lane = lax.broadcasted_iota(jnp.int32, (16, LANES), 1)

    def place(total, value, source, target, width):
        moved = turn(value, target - source)
        return jnp.where((lane >= target) & (lane < target + width), moved, total)

    def copy(layer):
        return pltpu.make_async_copy(plain.at[layer], whole.at[layer], sems.at[layer])

    def pack(layer):
        def cells(col, row):
            return plain[layer, col, row : row + 8, :]

        def t_cells(col, row):
            return t_ref[layer, row : row + 8, col * LANES : (col + 1) * LANES]

        for out, edge, t_edge in ((to_up, 0, 0), (to_down, rows - EDGE, rows - 2 * RIM - 8)):
            extra = jnp.zeros((8, LANES), F32)
            for j in range(9):
                left, right = cells(0, edge + 8 * j), cells(2, edge + 8 * j)
                out[layer, 8 * j : 8 * j + 8, :] = cells(1, edge + 8 * j)
                out[layer, EDGE + 8 * j : EDGE + 8 * j + 8, :] = jnp.where(low, right, left)
                extra = place(extra, jnp.where(low, left, right), 64 - WIDE, 2 * WIDE * j, 2 * WIDE)
            out[layer, 2 * EDGE : 2 * EDGE + 8, :] = extra
            for col in range(2):
                start = 2 * EDGE + 8 + 8 * col
                out[layer, start : start + 8, :] = t_cells(col, t_edge)

        def side(right, _, g_ref, up_ref, down_ref):
            col, t_col = (2, 1) if right else (0, 0)
            at, t_at = (64 - WIDE, LANES - WIDE) if right else (64, 0)
            half = SUM_ROWS // 2

            def both(one, two):
                return jnp.where(low, turn(two, 64), one) if right else jnp.where(low, one, turn(two, 64))

            for j in range(17):
                one, two = cells(col, RIM - 8 + 8 * j), cells(col, RIM - 8 + half + 8 * j)
                g_ref[layer, 8 * j : 8 * j + 8, :] = both(one, two)
            for first, parts, source in (
                (half, [cells(col, RIM - 8 + 8 * j) for j in range(34)], at),
                (half + 16, [t_cells(t_col, 8 * j) for j in range(32)], t_at),
            ):
                for part in range(2):
                    extra = jnp.zeros((8, LANES), F32)
                    for slot, value in enumerate(parts[part * SLOTS : (part + 1) * SLOTS]):
                        extra = place(extra, value, source, WIDE * slot, WIDE)
                    g_ref[layer, first + 8 * part : first + 8 * part + 8, :] = extra
            for out, edge, t_edge in ((up_ref, 0, 0), (down_ref, rows - EDGE, rows - 2 * RIM - 8)):
                strips = [cells(col, edge + 8 * j) for j in range(9)]
                for j in range(4):
                    out[layer, 8 * j : 8 * j + 8, :] = both(strips[j], strips[j + 5])
                start = 0 if right else 64
                extra = strips[4]
                for j in range(9):
                    extra = place(extra, strips[j], at, start + WIDE * j, WIDE)
                extra = place(extra, t_cells(t_col, t_edge), t_at, start + 9 * WIDE, WIDE)
                out[layer, 32:40, :] = extra

        by_side(sides, side, to_g, to_d_up, to_d_down)

    @pl.loop(0, depth)
    def _(layer):
        @pl.loop(0, rows // TILE)
        def _(tile_row):
            for col in range(3):
                left = exponent[tile_row, layer, 2 * col]
                right = exponent[tile_row, layer, 2 * col + 1]
                scale = jnp.exp2(jnp.where(wide_lane < TILE, left, right).astype(F32))
                for part in range(TILE // 16):
                    where = pl.ds(pl.multiple_of(tile_row * TILE + part * 16, 16), 16)
                    cells = mantissa[layer, where, col * LANES : (col + 1) * LANES]
                    plain[layer, col, where, :] = cells.astype(F32) * scale

        copy(layer).start()
        pack(layer)

    for layer in range(depth):
        copy(layer).wait()


def sum_kernel(sides, *refs):
    count = len(sides)
    plain, from_below, from_above = refs[:3]
    from_g, d_below, d_above = refs[3 : 3 + count], refs[3 + count : 3 + 2 * count], refs[3 + 2 * count : 3 + 3 * count]
    own, other, total, t_edge, sems = refs[3 + 3 * count :]
    depth = plain.shape[0]
    core = lax.axis_index("ta")
    lane = lane_ids()
    low = lane < 64
    half = SUM_ROWS // 2
    centre = (lane >= 64 - WIDE) & (lane < 64 + WIDE)

    def copies(side, out, index):
        row = pl.multiple_of(side * (SUM_ROWS - HALF_ROWS), 8)
        made = [
            pltpu.make_async_copy(
                total.at[:, col, pl.ds(row, HALF_ROWS), :],
                out.at[:, pl.ds(col * HALF_ROWS, HALF_ROWS), :],
                sems.at[index, col],
            )
            for col in range(3)
        ]
        made.append(pltpu.make_async_copy(t_edge.at[side], out.at[:, pl.ds(3 * HALF_ROWS, 16), :], sems.at[index, 3]))
        return made

    @pl.loop(0, depth)
    def _(layer):
        for j in range(SUM_ROWS // 8):
            row, where = RIM - 8 + 8 * j, pl.ds(8 * j, 8)
            left, right = plain[layer, 0, row : row + 8, :], plain[layer, 2, row : row + 8, :]
            total[layer, 0, where, :] = plain[layer, 1, row : row + 8, :]
            total[layer, 1, where, :] = jnp.where(low, right, left)
            total[layer, 2, where, :] = jnp.where(centre, jnp.where(low, left, right), 0.0)

        def add(col, row, value):
            total[layer, col, row : row + 8, :] = total[layer, col, row : row + 8, :] + value

        for edge, ref in ((0, from_above), (SUM_ROWS - EDGE, from_below)):
            extra = ref[layer, 2 * EDGE : 2 * EDGE + 8, :]
            for j in range(9):
                add(0, edge + 8 * j, ref[layer, 8 * j : 8 * j + 8, :])
                add(1, edge + 8 * j, ref[layer, EDGE + 8 * j : EDGE + 8 * j + 8, :])
                add(2, edge + 8 * j, jnp.where(centre, turn(extra, 64 - WIDE - 2 * WIDE * j), 0.0))
        t_edge[0, layer, :, :] = from_above[layer, 2 * EDGE + 8 :, :]
        t_edge[1, layer, :, :] = from_below[layer, 2 * EDGE + 8 :, :]

        def side(right, _, g_ref, below_ref, above_ref):
            main = low if right else jnp.logical_not(low)
            at, t_at = (64, 0) if right else (64 - WIDE, LANES - WIDE)

            def window(value, source, target):
                return jnp.where((lane >= target) & (lane < target + WIDE), turn(value, target - source), 0.0)

            for j in range(17):
                value = g_ref[layer, 8 * j : 8 * j + 8, :]
                add(1, 8 * j, jnp.where(main, value, 0.0))
                add(1, half + 8 * j, jnp.where(main, turn(value, 64), 0.0))
            extras = [g_ref[layer, half + 8 * j : half + 8 * j + 8, :] for j in range(4)]
            for j in range(34):
                value = window(extras[j // SLOTS], WIDE * (j % SLOTS), at)
                if 1 <= j <= 32:
                    k = j - 1
                    value = value + window(extras[2 + k // SLOTS], WIDE * (k % SLOTS), t_at)
                add(2, 8 * j, value)
            for edge, ref, t_row in ((0, above_ref, 0), (SUM_ROWS - EDGE, below_ref, SUM_ROWS - 8)):
                extra = ref[layer, 32:40, :]
                start = 64 if right else 0
                for j in range(9):
                    value = ref[layer, 8 * (j % 5) : 8 * (j % 5) + 8, :]
                    if j > 4:
                        value = turn(value, 64)
                    add(1, edge + 8 * j, jnp.where(main, value, 0.0))
                    add(2, edge + 8 * j, window(extra, start + WIDE * j, at))
                add(2, t_row, window(extra, start + 9 * WIDE, t_at))

        by_side(sides, side, from_g, d_below, d_above)

    made = copies(1 - core, other, 0) + copies(core, own, 1)
    for one in made:
        one.start()
    for one in made:
        one.wait()


def heat_kernel(own, other, out):
    depth = own.shape[0]
    core = lax.axis_index("ta")
    low = lane_ids() < 64

    def move(src, first):
        @pl.loop(0, depth)
        def _(layer):
            for j in range(16):
                one = turn(src[layer, 8 + 8 * j : 16 + 8 * j, :], 64)
                two = turn(src[layer, HALF_ROWS + 8 + 8 * j : HALF_ROWS + 16 + 8 * j, :], 64)
                out[layer, rows8(first + 8 * j), :LANES] = jnp.where(low, two, one)
                out[layer, rows8(first + 8 * j), LANES:] = jnp.where(low, one, two)

    move(own, core * 128)
    move(other, 128 - core * 128)


def permutation(inverse=False, shift=0):
    rows = lax.broadcasted_iota(jnp.int32, (256, 256), 0)
    cols = lax.broadcasted_iota(jnp.int32, (256, 256), 1)
    if inverse:
        rows, cols = cols, rows
    return jnp.where((rows + shift) % 256 == 4 * (cols % 64) + cols // 64, 1.0, 0.0).astype(jnp.bfloat16)


def permuted(value, matrix):
    parts = []
    for _ in range(3):
        part = value.astype(jnp.bfloat16)
        value = value - part.astype(F32)
        parts.append(part)
    moved = jnp.dot(jnp.concatenate(parts, axis=0), matrix, preferred_element_type=F32)
    high, middle, low = (moved[k * value.shape[0] : (k + 1) * value.shape[0]] for k in range(3))
    return high + (middle + low)


def to_groups(first, second):
    low = lane_ids() < 64
    out = []
    for half in range(2):
        one = first[:, half * LANES : (half + 1) * LANES]
        two = second[:, half * LANES : (half + 1) * LANES]
        out += [jnp.where(low, one, turn(two, 64)), jnp.where(low, turn(one, 64), two)]
    return out


def to_rows(parts):
    low = lane_ids() < 64
    one, two = [], []
    for half in range(2):
        left, right = parts[2 * half], parts[2 * half + 1]
        one.append(jnp.where(low, left, turn(right, 64)))
        two.append(jnp.where(low, turn(left, 64), right))
    return jnp.concatenate(one, axis=1), jnp.concatenate(two, axis=1)


def group_cells(load, dst, matrix):
    @pl.loop(0, STEP_ROWS // BLOCK)
    def _(block):
        rows = [group * STEP_ROWS + block * BLOCK + step for group in range(2) for step in range(BLOCK)]
        halves = [jnp.concatenate([load(row, half) for row in rows], axis=0) for half in range(2)]
        value = permuted(jnp.concatenate(halves, axis=1), matrix)
        for step in range(BLOCK):
            parts = to_groups(*(value[8 * at : 8 * at + 8] for at in (step, BLOCK + step)))
            for col in range(4):
                dst[rows8((block * BLOCK + step + 1) * 40 + 8 * col), :] = parts[col]


def stack_kernel(t_own, t_other, now, t_cells, t_sems):
    core = lax.axis_index("ta")
    depth, rows, _ = t_own.shape
    layers = 2 * depth
    copies = []
    for which, t_src in enumerate((t_own, t_other)):
        base = core * depth if which == 0 else (1 - core) * depth
        for layer in range(depth):
            for col in range(2):
                copies.append(
                    pltpu.make_async_copy(
                        t_src.at[layer, :, col * LANES : (col + 1) * LANES],
                        t_cells.at[col, base + layer, pl.ds(8, rows), :],
                        t_sems.at[which, layer, col],
                    )
                )
    for copy in copies:
        copy.start()
    zero = jnp.zeros((8, LANES), F32)
    for col in range(2):
        for layer in range(layers):
            t_cells[col, layer, 0:8, :] = zero
            t_cells[col, layer, rows + 8 : rows + 16, :] = zero

    @pl.loop(0, STEP_ROWS + 2)
    def _(step):
        now[rows8(step * 40 + 32), :] = zero

    for copy in copies:
        copy.wait()
    flat = t_cells.reshape(2, layers * (rows + 16), LANES)
    first = 2 + core * 128

    def load(row, half):
        return flat[half, pl.ds(first + row, layers, stride=rows + 16), :]

    group_cells(load, now, permutation())


def solve_kernel(bounds, own, other, now_in, flow, material, conductivity, t_out, sent, *refs):
    cells, rows_t, heat, now, later, cond, f_down, f_right, f_above, inverse, base, t_stage, in_sems, sems = refs
    core = lax.axis_index("ta")
    gx, gy = lax.axis_index("gx"), lax.axis_index("gy")
    lane = lane_ids()
    level = lax.broadcasted_iota(jnp.int32, (8, LANES), 0)
    low = lane < 64
    layers = 8
    depth = layers // 2

    def at(step, col):
        return rows8(step * 40 + 8 * col)

    incoming = [
        pltpu.make_async_copy(src, cells.at[pl.ds(first, depth)], in_sems.at[which])
        for which, (src, first) in enumerate(((own, core * depth), (other, (1 - core) * depth)))
    ]
    for copy in incoming:
        copy.start()
    for copy in incoming:
        copy.wait()
    flat = cells.reshape(layers * SWAP, LANES)

    def across(row):
        return flat[pl.ds(row, layers, stride=SWAP), :]

    def to_stage(stage, src):
        @pl.loop(0, 16)
        def _(tile):
            for layer in range(layers):
                for col in range(2):
                    value = src[col, pl.ds((6 + 8 * tile) * 8 + layer, 8, stride=8), :]
                    stage[layer, rows8(8 * tile), col * LANES : (col + 1) * LANES] = value

    def outputs():
        mine = t_stage.at[pl.ds(core * depth, depth)]
        theirs = t_stage.at[pl.ds((1 - core) * depth, depth)]
        half = t_stage.shape[1]
        place = pl.ds(pl.multiple_of(core * half, half), half)
        return (
            pltpu.make_async_copy(theirs, sent, sems.at[0]),
            pltpu.make_async_copy(mine, t_out.at[:, place, :], sems.at[1]),
        )

    group_cells(lambda row, half: across(half * HALF_ROWS + 2 + row), heat, permutation(shift=64))
    t_edge = jnp.concatenate(
        [
            jnp.concatenate([across(3 * HALF_ROWS + 8 * col + i) for i in range(8)], axis=0)
            for col in range(2)
        ],
        axis=1,
    )
    t_edge = permuted(t_edge, permutation())
    halo_lanes = (lane < WIDE) | ((lane >= 64 - WIDE) & (lane < 64 + WIDE)) | (lane >= LANES - WIDE)

    @pl.loop(0, STEP_ROWS // 5)
    def _(block):
        for part in range(5):
            step = block * 5 + part
            first, second = across(2 * HALF_ROWS + 2 + step), across(2 * HALF_ROWS + 2 + step + STEP_ROWS)
            first_turned, second_turned = turn(first, 64), turn(second, 64)
            upper_lanes = jnp.where(lane < 64 + WIDE, first, first_turned)
            lower_lanes = jnp.where(lane < WIDE, second_turned, second)
            heat[at(step + 1, 4), :] = jnp.where(halo_lanes, jnp.where(low, lower_lanes, upper_lanes), 0.0)
            upper_lanes = jnp.where(lane < 64 + WIDE, first_turned, first)
            lower_lanes = jnp.where(lane < WIDE, second, second_turned)
            now[at(step + 1, 4), :] = jnp.where(halo_lanes, jnp.where(low, lower_lanes, upper_lanes), 0.0)
            for col in range(4):
                now[at(step + 1, col), :] = now_in[at(step + 1, col), :]

    @pl.when(core == 0)
    def _():
        for row in range(6):
            value = t_edge[8 * row + 16 : 8 * row + 24]
            parts = to_groups(value, value)
            for col in range(4):
                now[at(row + 1, col), :] = jnp.where(low, parts[col], now[at(row + 1, col), :])

    @pl.when(core == 1)
    def _():
        for row in range(6):
            value = t_edge[8 * row : 8 * row + 8]
            parts = to_groups(value, value)
            for col in range(4):
                now[at(row + 65, col), :] = jnp.where(low, now[at(row + 65, col), :], parts[col])

    def ghosts(ref):
        for col in range(5):
            ref[at(0, col), :] = turn(ref[at(STEP_ROWS, col), :], 64)
            ref[at(STEP_ROWS + 1, col), :] = turn(ref[at(1, col), :], 64)

    last = (lane == 63) | (lane == 127)
    first = (lane == 0) | (lane == 64)

    def to_right(values):
        inner, outer = turn(values[0], -1), turn(values[4], -1)
        return values[1:4] + [jnp.where(last, outer, inner), jnp.where(last, inner, outer)]

    def to_left(values):
        inner, outer = turn(values[3], 1), turn(values[4], 1)
        return [jnp.where(first, outer, inner)] + values[:3] + [jnp.where(first, inner, outer)]

    def upper(value):
        return pltpu.roll(value, 7, 0)

    def lower(value):
        return pltpu.roll(value, 1, 0)

    has_right = (gy + 1) * 256 < bounds[1]
    half_lane = jnp.where(low, lane, lane - 64)
    keep = ((half_lane < WIDE) & has_right) | ((half_lane >= 64 - WIDE) & (gy > 0))
    halo_mask = jnp.where(keep, 1.0, 0.0)
    scale = jnp.full((8, LANES), conductivity[material[0]], F32)
    for layer in range(1, layers):
        scale = jnp.where(level == layer, conductivity[material[layer]], scale)
    not_top = jnp.where(level < layers - 1, 1.0, 0.0)
    not_bottom = jnp.where(level > 0, 1.0, 0.0)
    flows = [flow[8 * col : 8 * col + 8, :] for col in range(5)]
    first_row = gx * 256 + core * 128 - 6

    def masks(step):
        ones = []
        for group in range(2):
            row = first_row + step + group * STEP_ROWS
            ones.append(jnp.where((row >= 0) & (row < bounds[0]), 1.0, 0.0))
        inner = jnp.where(low, ones[0], ones[1])
        return [inner] * 4 + [jnp.where(low, ones[1], ones[0]) * halo_mask]

    def conductances(src):
        @pl.loop(0, STEP_ROWS // 5)
        def _(block):
            for part in range(5):
                step = block * 5 + part
                mask = masks(step)
                for col in range(5):
                    where = at(step + 1, col)
                    cond[where, :] = (scale * mask[col]) * (1.0 + 0.5 * jnp.tanh(src[where, :]))

        ghosts(cond)

    def coefficients(src):
        @pl.loop(0, STEP_ROWS // 5)
        def _(block):
            start = block * 5
            lines = [[cond[at(start + part, col), :] for col in range(5)] for part in range(7)]
            for part in range(5):
                up, here, down = lines[part], lines[part + 1], lines[part + 2]
                mask = masks(start + part)
                rights, lefts = to_right(here), to_left(here)
                for col in range(5):
                    where = at(start + part + 1, col)
                    centre = here[col]
                    over = centre + upper(centre) * not_top
                    under = centre + lower(centre) * not_bottom
                    face_down = 0.5 * (centre + down[col])
                    face_right = 0.5 * (centre + rights[col])
                    total = (1.0 + flows[col]) + 0.5 * (centre + up[col]) + face_down
                    total = total + face_right + 0.5 * (centre + lefts[col]) + over + under
                    f_down[where, :] = face_down
                    f_right[where, :] = face_right
                    f_above[where, :] = over * not_top
                    inverse[where, :] = mask[col] / total
                    base[where, :] = src[where, :] + heat[where, :]

        for col in range(5):
            f_down[at(0, col), :] = 0.5 * (cond[at(0, col), :] + cond[at(1, col), :])

    def sweep(src, dst):
        @pl.loop(0, STEP_ROWS // SPAN)
        def _(block):
            start = block * SPAN
            lines = [[src[at(start + part, col), :] for col in range(5)] for part in range(SPAN + 2)]
            faces = [[f_down[at(start + part, col), :] for col in range(5)] for part in range(SPAN + 1)]
            for part in range(SPAN):
                up, here, down = lines[part], lines[part + 1], lines[part + 2]
                face_right = [f_right[at(start + part + 1, col), :] for col in range(5)]
                rights = to_right(here)
                lefts = to_left([face * value for face, value in zip(face_right, here)])
                for col in range(5):
                    where = at(start + part + 1, col)
                    face_above = f_above[where, :]
                    total = base[where, :] + (faces[part][col] + flows[col]) * up[col]
                    total = total + faces[part + 1][col] * down[col]
                    total = total + (face_right[col] * rights[col] + lefts[col])
                    total = total + (face_above * upper(here[col]) + lower(face_above * here[col]))
                    dst[where, :] = total * inverse[where, :]

        ghosts(dst)

    ghosts(now)
    for _ in range(STEPS):
        conductances(now)
        coefficients(now)
        for _ in range(SWEEPS):
            sweep(now, later)
            now, later = later, now

    back = permutation(inverse=True)

    @pl.loop(0, STEP_ROWS // BLOCK)
    def _(block):
        pairs = [
            to_rows([now[at(block * BLOCK + part + 1, col), :] for col in range(4)]) for part in range(BLOCK)
        ]
        value = jnp.concatenate([pair[group] for group in range(2) for pair in pairs], axis=0)
        value = permuted(value, back)
        for group in range(2):
            where = pl.ds(pl.multiple_of((group * STEP_ROWS + block * BLOCK) * 8, 8), BLOCK * 8)
            for col in range(2):
                part = value[group * BLOCK * 8 : (group + 1) * BLOCK * 8, col * LANES : (col + 1) * LANES]
                rows_t[col, where, :] = part

    to_stage(t_stage, rows_t)
    for copy in outputs():
        copy.start()
    for copy in outputs():
        copy.wait()


def place_kernel(received, t_in, t_out, sem):
    core = lax.axis_index("ta")
    half = received.shape[1]
    place = pl.ds(pl.multiple_of((1 - core) * half, half), half)
    copy = pltpu.make_async_copy(received, t_out.at[:, place, :], sem)
    copy.start()
    copy.wait()


def on_device(t_initial, power_mantissa, tile_exponent, channel_mask, material, conductivity):
    depth, rows, cols = t_initial.shape
    layers = 2 * depth
    n_gx, n_gy = lax.axis_size("gx"), lax.axis_size("gy")
    array = jax.ShapeDtypeStruct
    swap = [(0, 1), (1, 0)]
    out_sides = [None] if n_gy == 2 else [True, False]
    in_sides = [None] if n_gy == 2 else [False, True]
    count = len(out_sides)

    t_other = lax.ppermute(t_initial, "ta", swap)
    plain_shape = array((depth, 3, rows + 2 * RIM, LANES), F32)
    along = array((depth, ROWS_P, LANES), F32)
    across = (array((depth, ROWS_G, LANES), F32),) * count
    corner = (array((depth, ROWS_D, LANES), F32),) * (2 * count)
    sent = pl.pallas_call(
        functools.partial(send_kernel, out_sides),
        out_shape=(plain_shape, along, along) + across + corner,
        in_specs=[VMEM, SMEM, VMEM],
        out_specs=(ANY,) + (VMEM,) * (2 + 3 * count),
        scratch_shapes=[pltpu.VMEM(plain_shape.shape, F32), pltpu.SemaphoreType.DMA((depth,))],
        compiler_params=params(12),
        name="send",
    )(power_mantissa, tile_exponent.transpose(1, 0, 2), t_initial)
    plain, up, down = sent[:3]
    to_g, to_d_up, to_d_down = sent[3 : 3 + count], sent[3 + count : 3 + 2 * count], sent[3 + 2 * count :]

    def move(value, step_z, step_x):
        pairs = []
        for z in range(n_gx):
            for x in range(n_gy):
                to_z, to_x = z + step_z, x ^ 1 if step_x is None else x + step_x
                if 0 <= to_z < n_gx and 0 <= to_x < n_gy:
                    pairs.append((z * n_gy + x, to_z * n_gy + to_x))
        return lax.ppermute(value, ("gx", "gy"), pairs)

    steps = [None] if n_gy == 2 else [1, -1]
    from_g = [move(value, 0, step) for value, step in zip(to_g, steps)]
    from_above = move(down, 1, 0)
    from_below = move(up, -1, 0)
    d_above = [move(value, 1, step) for value, step in zip(to_d_down, steps)]
    d_below = [move(value, -1, step) for value, step in zip(to_d_up, steps)]

    wide = jnp.pad(channel_mask, ((0, 0), (RIM, RIM)))
    mask = lax.dynamic_slice_in_dim(wide, lax.axis_index("gy") * cols, cols + 2 * RIM, 1).astype(F32) * COOLANT
    inner = mask[:, RIM : RIM + cols].reshape(layers, 64, 4).transpose(2, 0, 1)
    outer = jnp.zeros((layers, 64 - 2 * WIDE), F32)
    outer = jnp.concatenate([mask[:, RIM + cols :][:, :WIDE], outer, mask[:, RIM - WIDE : RIM]], axis=1)
    flow = jnp.concatenate([inner, outer[None]], axis=0).reshape(layers * 5, 64)
    flow = jnp.concatenate([flow, flow], axis=1)

    grouped = array(((STEP_ROWS + 2) * 40, LANES), F32)
    now = pl.pallas_call(
        stack_kernel,
        out_shape=grouped,
        in_specs=[ANY] * 2,
        out_specs=VMEM,
        scratch_shapes=[
            pltpu.VMEM((2, layers, rows + 16, LANES), F32),
            pltpu.SemaphoreType.DMA((2, depth, 2)),
        ],
        compiler_params=params(24),
        name="stack",
    )(t_initial, t_other)

    half = array((depth, SWAP, LANES), F32)
    own, other = pl.pallas_call(
        functools.partial(sum_kernel, in_sides),
        out_shape=(half, half),
        in_specs=[VMEM] * (3 + 3 * count),
        out_specs=(ANY, ANY),
        scratch_shapes=[
            pltpu.VMEM((depth, 3, SUM_ROWS, LANES), F32),
            pltpu.VMEM((2, depth, 16, LANES), F32),
            pltpu.SemaphoreType.DMA((2, 4)),
        ],
        compiler_params=params(12),
        name="sum",
    )(plain, from_below, from_above, *from_g, *d_below, *d_above)
    received = lax.ppermute(other, "ta", swap)
    whole = array((depth, rows, cols), F32)
    heat_source = pl.pallas_call(
        heat_kernel,
        out_shape=whole,
        in_specs=[VMEM] * 2,
        out_specs=VMEM,
        compiler_params=params(8),
        name="heat",
    )(own, other)

    work = pltpu.VMEM(grouped.shape, F32)
    t_part, sent = pl.pallas_call(
        functools.partial(solve_kernel, (n_gx * rows, n_gy * cols)),
        out_shape=(whole, array((depth, rows // 2, cols), F32)),
        in_specs=[ANY, ANY] + [VMEM] * 2 + [SMEM, SMEM],
        out_specs=(ANY, ANY),
        scratch_shapes=[
            pltpu.VMEM((layers, SWAP, LANES), F32),
            pltpu.VMEM((2, REGION * 8, LANES), F32),
        ]
        + [work] * 9
        + [
            pltpu.VMEM((layers, rows // 2, cols), F32),
            pltpu.SemaphoreType.DMA((2,)),
            pltpu.SemaphoreType.DMA((2,)),
        ],
        compiler_params=params(44),
        name="solve",
    )(own, received, now, flow, material, conductivity)
    received = lax.ppermute(sent, "ta", swap)
    temperature = pl.pallas_call(
        place_kernel,
        out_shape=whole,
        in_specs=[ANY, ANY],
        out_specs=ANY,
        scratch_shapes=[pltpu.SemaphoreType.DMA],
        input_output_aliases={1: 0},
        compiler_params=params(4),
        name="place",
    )(received, t_part)
    return temperature, heat_source


def solution(mesh):
    cells = P("ta", ("group", "gx"), "gy")
    return jax.shard_map(
        on_device,
        mesh=mesh,
        in_specs=(cells, cells, cells, P(), P(), P()),
        out_specs=(cells, cells),
        check_vma=False,
    )
```

```python
import functools

import jax
import jax.numpy as jnp
from jax import lax
from jax.experimental import pallas as pl
from jax.experimental.pallas import tpu as pltpu
from jax.sharding import PartitionSpec as P

RIM = 64
TILE = 64
STEPS = 2
SWEEPS = 3
COOLANT = 2.0

LANES = 128
WIDE = 6
REGION = 140
STEP_ROWS = 70
BLOCK = 35
SPAN = 35
SUM_ROWS = 272
HALF_ROWS = 144
SWAP = 3 * HALF_ROWS + 16
EDGE = 72
SLOTS = LANES // WIDE
ROWS_P = 2 * EDGE + 8 + 16
ROWS_G = SUM_ROWS // 2 + 16 + 16
ROWS_D = 40
F32 = jnp.float32
VMEM = pl.BlockSpec(memory_space=pltpu.VMEM)
SMEM = pl.BlockSpec(memory_space=pltpu.SMEM)
ANY = pl.BlockSpec(memory_space=pl.ANY)
HBM = pl.BlockSpec(memory_space=pltpu.HBM)


def params(megabytes):
    return pltpu.CompilerParams(vmem_limit_bytes=megabytes << 20)


def rows8(start):
    return pl.ds(pl.multiple_of(start, 8), 8)


def lane_ids():
    return lax.broadcasted_iota(jnp.int32, (8, LANES), 1)


def turn(value, shift):
    shift = shift % LANES
    return pltpu.roll(value, shift, 1) if shift else value


def by_side(sides, body, *lists):
    for place, side in enumerate(sides):
        rest = [values[place] for values in lists]
        if side is None:
            first = lax.axis_index("gy") == 0
            pl.when(first)(functools.partial(body, True, place, *rest))
            pl.when(jnp.logical_not(first))(functools.partial(body, False, place, *rest))
        else:
            body(side, place, *rest)


def send_kernel(sides, mantissa_in, exponent_in, t_in, *refs):
    count = len(sides)
    whole, to_first, to_second = refs[:3]
    to_g, to_d_first, to_d_second = refs[3 : 3 + count], refs[3 + count : 3 + 2 * count], refs[3 + 2 * count : 3 + 3 * count]
    plain, mantissa, exponent, t_ref, sems, in_sems, exponent_sem = refs[3 + 3 * count :]
    depth, rows, _ = mantissa.shape
    lane = lane_ids()
    low = lane < 64
    wide_lane = lax.broadcasted_iota(jnp.int32, (16, LANES), 1)

    def place(total, value, source, target, width):
        moved = turn(value, target - source)
        return jnp.where((lane >= target) & (lane < target + width), moved, total)

    odd = lax.rem(lax.axis_index("gx"), 2)
    edges = [which * (rows - EDGE) for which in (1 - odd, odd)]
    t_edges = [which * (rows - 2 * RIM - 8) for which in (1 - odd, odd)]

    def copy(layer):
        return pltpu.make_async_copy(plain.at[layer], whole.at[layer], sems.at[layer])

    def pack(layer):
        def cells(col, row):
            return plain[layer, col, rows8(row), :]

        def t_cells(col, row):
            return t_ref[layer, rows8(row), col * LANES : (col + 1) * LANES]

        for out, edge, t_edge in ((to_first, edges[0], t_edges[0]), (to_second, edges[1], t_edges[1])):
            extra = jnp.zeros((8, LANES), F32)
            for j in range(9):
                left, right = cells(0, edge + 8 * j), cells(2, edge + 8 * j)
                out[layer, 8 * j : 8 * j + 8, :] = cells(1, edge + 8 * j)
                out[layer, EDGE + 8 * j : EDGE + 8 * j + 8, :] = jnp.where(low, right, left)
                extra = place(extra, jnp.where(low, left, right), 64 - WIDE, 2 * WIDE * j, 2 * WIDE)
            out[layer, 2 * EDGE : 2 * EDGE + 8, :] = extra
            for col in range(2):
                start = 2 * EDGE + 8 + 8 * col
                out[layer, start : start + 8, :] = t_cells(col, t_edge)

        def side(right, _, g_ref, first_ref, second_ref):
            col, t_col = (2, 1) if right else (0, 0)
            at, t_at = (64 - WIDE, LANES - WIDE) if right else (64, 0)
            half = SUM_ROWS // 2

            def both(one, two):
                return jnp.where(low, turn(two, 64), one) if right else jnp.where(low, one, turn(two, 64))

            for j in range(17):
                one, two = cells(col, RIM - 8 + 8 * j), cells(col, RIM - 8 + half + 8 * j)
                g_ref[layer, 8 * j : 8 * j + 8, :] = both(one, two)
            for first, parts, source in (
                (half, [cells(col, RIM - 8 + 8 * j) for j in range(34)], at),
                (half + 16, [t_cells(t_col, 8 * j) for j in range(32)], t_at),
            ):
                for part in range(2):
                    extra = jnp.zeros((8, LANES), F32)
                    for slot, value in enumerate(parts[part * SLOTS : (part + 1) * SLOTS]):
                        extra = place(extra, value, source, WIDE * slot, WIDE)
                    g_ref[layer, first + 8 * part : first + 8 * part + 8, :] = extra
            for out, edge, t_edge in ((first_ref, edges[0], t_edges[0]), (second_ref, edges[1], t_edges[1])):
                strips = [cells(col, edge + 8 * j) for j in range(9)]
                for j in range(4):
                    out[layer, 8 * j : 8 * j + 8, :] = both(strips[j], strips[j + 5])
                start = 0 if right else 64
                extra = strips[4]
                for j in range(9):
                    extra = place(extra, strips[j], at, start + WIDE * j, WIDE)
                extra = place(extra, t_cells(t_col, t_edge), t_at, start + 9 * WIDE, WIDE)
                out[layer, 32:40, :] = extra

        by_side(sides, side, to_g, to_d_first, to_d_second)

    def arrivals(layer):
        return (
            pltpu.make_async_copy(mantissa_in.at[layer], mantissa.at[layer], in_sems.at[0, layer]),
            pltpu.make_async_copy(t_in.at[layer], t_ref.at[layer], in_sems.at[1, layer]),
        )

    scales = pltpu.make_async_copy(exponent_in, exponent, exponent_sem)
    scales.start()
    for layer in range(depth):
        for one in arrivals(layer):
            one.start()
    scales.wait()

    @pl.loop(0, depth)
    def _(layer):
        for one in arrivals(layer):
            one.wait()

        @pl.loop(0, rows // TILE)
        def _(tile_row):
            for col in range(3):
                left = exponent[tile_row, layer, 2 * col]
                right = exponent[tile_row, layer, 2 * col + 1]
                scale = jnp.exp2(jnp.where(wide_lane < TILE, left, right).astype(F32))
                for part in range(TILE // 16):
                    where = pl.ds(pl.multiple_of(tile_row * TILE + part * 16, 16), 16)
                    cells = mantissa[layer, where, col * LANES : (col + 1) * LANES]
                    plain[layer, col, where, :] = cells.astype(F32) * scale

        copy(layer).start()
        pack(layer)

    for layer in range(depth):
        copy(layer).wait()


def sum_kernel(sides, *refs):
    count = len(sides)
    plain, payloads = refs[0], refs[1:]
    from_g, payloads = payloads[:count], payloads[count:]
    from_first, payloads = payloads[0], payloads[1:]
    from_second, payloads = payloads[0], payloads[1:]
    d_first, payloads = payloads[:count], payloads[count:]
    d_second, payloads = payloads[:count], payloads[count:]
    own, other, total, t_edge, sems = refs[3 + 3 * count :]
    depth = plain.shape[0]
    core = lax.axis_index("ta")
    odd = lax.rem(lax.axis_index("gx"), 2)
    after = (1 - odd, odd)
    lane = lane_ids()
    low = lane < 64
    half = SUM_ROWS // 2
    centre = (lane >= 64 - WIDE) & (lane < 64 + WIDE)

    def copies(side, out, index):
        row = pl.multiple_of(side * (SUM_ROWS - HALF_ROWS), 8)
        made = [
            pltpu.make_async_copy(
                total.at[:, col, pl.ds(row, HALF_ROWS), :],
                out.at[:, pl.ds(col * HALF_ROWS, HALF_ROWS), :],
                sems.at[index, col],
            )
            for col in range(3)
        ]
        made.append(pltpu.make_async_copy(t_edge.at[side], out.at[:, pl.ds(3 * HALF_ROWS, 16), :], sems.at[index, 3]))
        return made

    @pl.loop(0, depth)
    def _(layer):
        for j in range(SUM_ROWS // 8):
            row, where = RIM - 8 + 8 * j, pl.ds(8 * j, 8)
            left, right = plain[layer, 0, row : row + 8, :], plain[layer, 2, row : row + 8, :]
            total[layer, 0, where, :] = plain[layer, 1, row : row + 8, :]
            total[layer, 1, where, :] = jnp.where(low, right, left)
            total[layer, 2, where, :] = jnp.where(centre, jnp.where(low, left, right), 0.0)

        def add(col, row, value):
            total[layer, col, rows8(row), :] = total[layer, col, rows8(row), :] + value

        for which, ref in zip(after, (from_first, from_second)):
            edge = which * (SUM_ROWS - EDGE)
            t_edge[which, layer, :, :] = ref[layer, 2 * EDGE + 8 :, :]
            extra = ref[layer, 2 * EDGE : 2 * EDGE + 8, :]
            for j in range(9):
                add(0, edge + 8 * j, ref[layer, 8 * j : 8 * j + 8, :])
                add(1, edge + 8 * j, ref[layer, EDGE + 8 * j : EDGE + 8 * j + 8, :])
                add(2, edge + 8 * j, jnp.where(centre, turn(extra, 64 - WIDE - 2 * WIDE * j), 0.0))

        def side(right, _, g_ref, first_ref, second_ref):
            main = low if right else jnp.logical_not(low)
            at, t_at = (64, 0) if right else (64 - WIDE, LANES - WIDE)

            def window(value, source, target):
                return jnp.where((lane >= target) & (lane < target + WIDE), turn(value, target - source), 0.0)

            for j in range(17):
                value = g_ref[layer, 8 * j : 8 * j + 8, :]
                add(1, 8 * j, jnp.where(main, value, 0.0))
                add(1, half + 8 * j, jnp.where(main, turn(value, 64), 0.0))
            extras = [g_ref[layer, half + 8 * j : half + 8 * j + 8, :] for j in range(4)]
            for j in range(34):
                value = window(extras[j // SLOTS], WIDE * (j % SLOTS), at)
                if 1 <= j <= 32:
                    k = j - 1
                    value = value + window(extras[2 + k // SLOTS], WIDE * (k % SLOTS), t_at)
                add(2, 8 * j, value)
            for which, ref in zip(after, (first_ref, second_ref)):
                edge, t_row = which * (SUM_ROWS - EDGE), which * (SUM_ROWS - 8)
                extra = ref[layer, 32:40, :]
                start = 64 if right else 0
                for j in range(9):
                    value = ref[layer, 8 * (j % 5) : 8 * (j % 5) + 8, :]
                    if j > 4:
                        value = turn(value, 64)
                    add(1, edge + 8 * j, jnp.where(main, value, 0.0))
                    add(2, edge + 8 * j, window(extra, start + WIDE * j, at))
                add(2, t_row, window(extra, start + 9 * WIDE, t_at))

        by_side(sides, side, from_g, d_first, d_second)

    made = copies(1 - core, other, 0) + copies(core, own, 1)
    for one in made:
        one.start()
    for one in made:
        one.wait()


def heat_kernel(own, other, out):
    depth = own.shape[0]
    core = lax.axis_index("ta")
    low = lane_ids() < 64

    def move(src, first):
        @pl.loop(0, depth)
        def _(layer):
            for j in range(16):
                one = turn(src[layer, 8 + 8 * j : 16 + 8 * j, :], 64)
                two = turn(src[layer, HALF_ROWS + 8 + 8 * j : HALF_ROWS + 16 + 8 * j, :], 64)
                out[layer, rows8(first + 8 * j), :LANES] = jnp.where(low, two, one)
                out[layer, rows8(first + 8 * j), LANES:] = jnp.where(low, one, two)

    move(own, core * 128)
    move(other, 128 - core * 128)


def permutation(inverse=False, shift=0):
    rows = lax.broadcasted_iota(jnp.int32, (256, 256), 0)
    cols = lax.broadcasted_iota(jnp.int32, (256, 256), 1)
    if inverse:
        rows, cols = cols, rows
    return jnp.where((rows + shift) % 256 == 4 * (cols % 64) + cols // 64, 1.0, 0.0).astype(jnp.bfloat16)


def permuted(value, matrix):
    parts = []
    for _ in range(3):
        part = value.astype(jnp.bfloat16)
        value = value - part.astype(F32)
        parts.append(part)
    moved = jnp.dot(jnp.concatenate(parts, axis=0), matrix, preferred_element_type=F32)
    high, middle, low = (moved[k * value.shape[0] : (k + 1) * value.shape[0]] for k in range(3))
    return high + (middle + low)


def to_groups(first, second):
    low = lane_ids() < 64
    out = []
    for half in range(2):
        one = first[:, half * LANES : (half + 1) * LANES]
        two = second[:, half * LANES : (half + 1) * LANES]
        out += [jnp.where(low, one, turn(two, 64)), jnp.where(low, turn(one, 64), two)]
    return out


def to_rows(parts):
    low = lane_ids() < 64
    one, two = [], []
    for half in range(2):
        left, right = parts[2 * half], parts[2 * half + 1]
        one.append(jnp.where(low, left, turn(right, 64)))
        two.append(jnp.where(low, turn(left, 64), right))
    return jnp.concatenate(one, axis=1), jnp.concatenate(two, axis=1)


def group_cells(load, dst, matrix):
    @pl.loop(0, STEP_ROWS // BLOCK)
    def _(block):
        rows = [group * STEP_ROWS + block * BLOCK + step for group in range(2) for step in range(BLOCK)]
        halves = [jnp.concatenate([load(row, half) for row in rows], axis=0) for half in range(2)]
        value = permuted(jnp.concatenate(halves, axis=1), matrix)
        for step in range(BLOCK):
            parts = to_groups(*(value[8 * at : 8 * at + 8] for at in (step, BLOCK + step)))
            for col in range(4):
                dst[rows8((block * BLOCK + step + 1) * 40 + 8 * col), :] = parts[col]


def stack_kernel(t_own, t_other, now, t_cells, t_sems):
    core = lax.axis_index("ta")
    depth, rows, _ = t_own.shape
    layers = 2 * depth
    copies = []
    for which, t_src in enumerate((t_own, t_other)):
        base = core * depth if which == 0 else (1 - core) * depth
        for layer in range(depth):
            for col in range(2):
                copies.append(
                    pltpu.make_async_copy(
                        t_src.at[layer, :, col * LANES : (col + 1) * LANES],
                        t_cells.at[col, base + layer, pl.ds(8, rows), :],
                        t_sems.at[which, layer, col],
                    )
                )
    for copy in copies:
        copy.start()
    zero = jnp.zeros((8, LANES), F32)
    for col in range(2):
        for layer in range(layers):
            t_cells[col, layer, 0:8, :] = zero
            t_cells[col, layer, rows + 8 : rows + 16, :] = zero

    @pl.loop(0, STEP_ROWS + 2)
    def _(step):
        now[rows8(step * 40 + 32), :] = zero

    for copy in copies:
        copy.wait()
    flat = t_cells.reshape(2, layers * (rows + 16), LANES)
    first = 2 + core * 128

    def load(row, half):
        return flat[half, pl.ds(first + row, layers, stride=rows + 16), :]

    group_cells(load, now, permutation())


def solve_kernel(bounds, own, other, now_in, flow, material, conductivity, t_out, sent, *refs):
    cells, rows_t, heat, now, later, cond, f_down, f_right, f_above, inverse, base, t_stage, in_sems, sems = refs
    core = lax.axis_index("ta")
    gx, gy = lax.axis_index("gx"), lax.axis_index("gy")
    lane = lane_ids()
    level = lax.broadcasted_iota(jnp.int32, (8, LANES), 0)
    low = lane < 64
    layers = 8
    depth = layers // 2

    def at(step, col):
        return rows8(step * 40 + 8 * col)

    incoming = [
        pltpu.make_async_copy(src, cells.at[pl.ds(first, depth)], in_sems.at[which])
        for which, (src, first) in enumerate(((own, core * depth), (other, (1 - core) * depth)))
    ]
    for copy in incoming:
        copy.start()
    for copy in incoming:
        copy.wait()
    flat = cells.reshape(layers * SWAP, LANES)

    def across(row):
        return flat[pl.ds(row, layers, stride=SWAP), :]

    def to_stage(stage, src):
        @pl.loop(0, 16)
        def _(tile):
            for layer in range(layers):
                for col in range(2):
                    value = src[col, pl.ds((6 + 8 * tile) * 8 + layer, 8, stride=8), :]
                    stage[layer, rows8(8 * tile), col * LANES : (col + 1) * LANES] = value

    def outputs():
        mine = t_stage.at[pl.ds(core * depth, depth)]
        theirs = t_stage.at[pl.ds((1 - core) * depth, depth)]
        half = t_stage.shape[1]
        place = pl.ds(pl.multiple_of(core * half, half), half)
        return (
            pltpu.make_async_copy(theirs, sent, sems.at[0]),
            pltpu.make_async_copy(mine, t_out.at[:, place, :], sems.at[1]),
        )

    group_cells(lambda row, half: across(half * HALF_ROWS + 2 + row), heat, permutation(shift=64))
    t_edge = jnp.concatenate(
        [
            jnp.concatenate([across(3 * HALF_ROWS + 8 * col + i) for i in range(8)], axis=0)
            for col in range(2)
        ],
        axis=1,
    )
    t_edge = permuted(t_edge, permutation())
    halo_lanes = (lane < WIDE) | ((lane >= 64 - WIDE) & (lane < 64 + WIDE)) | (lane >= LANES - WIDE)

    @pl.loop(0, STEP_ROWS // 5)
    def _(block):
        for part in range(5):
            step = block * 5 + part
            first, second = across(2 * HALF_ROWS + 2 + step), across(2 * HALF_ROWS + 2 + step + STEP_ROWS)
            first_turned, second_turned = turn(first, 64), turn(second, 64)
            upper_lanes = jnp.where(lane < 64 + WIDE, first, first_turned)
            lower_lanes = jnp.where(lane < WIDE, second_turned, second)
            heat[at(step + 1, 4), :] = jnp.where(halo_lanes, jnp.where(low, lower_lanes, upper_lanes), 0.0)
            upper_lanes = jnp.where(lane < 64 + WIDE, first_turned, first)
            lower_lanes = jnp.where(lane < WIDE, second, second_turned)
            now[at(step + 1, 4), :] = jnp.where(halo_lanes, jnp.where(low, lower_lanes, upper_lanes), 0.0)
            for col in range(4):
                now[at(step + 1, col), :] = now_in[at(step + 1, col), :]

    @pl.when(core == 0)
    def _():
        for row in range(6):
            value = t_edge[8 * row + 16 : 8 * row + 24]
            parts = to_groups(value, value)
            for col in range(4):
                now[at(row + 1, col), :] = jnp.where(low, parts[col], now[at(row + 1, col), :])

    @pl.when(core == 1)
    def _():
        for row in range(6):
            value = t_edge[8 * row : 8 * row + 8]
            parts = to_groups(value, value)
            for col in range(4):
                now[at(row + 65, col), :] = jnp.where(low, now[at(row + 65, col), :], parts[col])

    def ghosts(ref):
        for col in range(5):
            ref[at(0, col), :] = turn(ref[at(STEP_ROWS, col), :], 64)
            ref[at(STEP_ROWS + 1, col), :] = turn(ref[at(1, col), :], 64)

    last = (lane == 63) | (lane == 127)
    first = (lane == 0) | (lane == 64)

    def to_right(values):
        inner, outer = turn(values[0], -1), turn(values[4], -1)
        return values[1:4] + [jnp.where(last, outer, inner), jnp.where(last, inner, outer)]

    def to_left(values):
        inner, outer = turn(values[3], 1), turn(values[4], 1)
        return [jnp.where(first, outer, inner)] + values[:3] + [jnp.where(first, inner, outer)]

    def upper(value):
        return pltpu.roll(value, 7, 0)

    def lower(value):
        return pltpu.roll(value, 1, 0)

    has_right = (gy + 1) * 256 < bounds[1]
    half_lane = jnp.where(low, lane, lane - 64)
    keep = ((half_lane < WIDE) & has_right) | ((half_lane >= 64 - WIDE) & (gy > 0))
    halo_mask = jnp.where(keep, 1.0, 0.0)
    scale = jnp.full((8, LANES), conductivity[material[0]], F32)
    for layer in range(1, layers):
        scale = jnp.where(level == layer, conductivity[material[layer]], scale)
    not_top = jnp.where(level < layers - 1, 1.0, 0.0)
    not_bottom = jnp.where(level > 0, 1.0, 0.0)
    flows = [flow[8 * col : 8 * col + 8, :] for col in range(5)]
    first_row = gx * 256 + core * 128 - 6

    def masks(step):
        ones = []
        for group in range(2):
            row = first_row + step + group * STEP_ROWS
            ones.append(jnp.where((row >= 0) & (row < bounds[0]), 1.0, 0.0))
        inner = jnp.where(low, ones[0], ones[1])
        return [inner] * 4 + [jnp.where(low, ones[1], ones[0]) * halo_mask]

    def conductances(src):
        @pl.loop(0, STEP_ROWS // 14)
        def _(block):
            for part in range(14):
                step = block * 14 + part
                mask = masks(step)
                for col in range(5):
                    where = at(step + 1, col)
                    cond[where, :] = (scale * mask[col]) * (1.0 + 0.5 * jnp.tanh(src[where, :]))

        ghosts(cond)

    def coefficients(src):
        @pl.loop(0, STEP_ROWS // 10)
        def _(block):
            start = block * 10
            lines = [[cond[at(start + part, col), :] for col in range(5)] for part in range(12)]
            for part in range(10):
                up, here, down = lines[part], lines[part + 1], lines[part + 2]
                mask = masks(start + part)
                rights, lefts = to_right(here), to_left(here)
                for col in range(5):
                    where = at(start + part + 1, col)
                    centre = here[col]
                    over = centre + upper(centre) * not_top
                    under = centre + lower(centre) * not_bottom
                    face_down = 0.5 * (centre + down[col])
                    face_right = 0.5 * (centre + rights[col])
                    total = (1.0 + flows[col]) + 0.5 * (centre + up[col]) + face_down
                    total = total + face_right + 0.5 * (centre + lefts[col]) + over + under
                    f_down[where, :] = face_down
                    f_right[where, :] = face_right
                    f_above[where, :] = over * not_top
                    inverse[where, :] = mask[col] / total
                    base[where, :] = src[where, :] + heat[where, :]

        for col in range(5):
            f_down[at(0, col), :] = 0.5 * (cond[at(0, col), :] + cond[at(1, col), :])

    def sweep(src, dst):
        @pl.loop(0, STEP_ROWS // SPAN)
        def _(block):
            start = block * SPAN
            lines = [[src[at(start + part, col), :] for col in range(5)] for part in range(SPAN + 2)]
            faces = [[f_down[at(start + part, col), :] for col in range(5)] for part in range(SPAN + 1)]
            for part in range(SPAN):
                up, here, down = lines[part], lines[part + 1], lines[part + 2]
                face_right = [f_right[at(start + part + 1, col), :] for col in range(5)]
                rights = to_right(here)
                lefts = to_left([face * value for face, value in zip(face_right, here)])
                for col in range(5):
                    where = at(start + part + 1, col)
                    face_above = f_above[where, :]
                    total = base[where, :] + (faces[part][col] + flows[col]) * up[col]
                    total = total + faces[part + 1][col] * down[col]
                    total = total + (face_right[col] * rights[col] + lefts[col])
                    total = total + (face_above * upper(here[col]) + lower(face_above * here[col]))
                    dst[where, :] = total * inverse[where, :]

        ghosts(dst)

    ghosts(now)
    for _ in range(STEPS):
        conductances(now)
        coefficients(now)
        for _ in range(SWEEPS):
            sweep(now, later)
            now, later = later, now

    back = permutation(inverse=True)

    @pl.loop(0, STEP_ROWS // BLOCK)
    def _(block):
        pairs = [
            to_rows([now[at(block * BLOCK + part + 1, col), :] for col in range(4)]) for part in range(BLOCK)
        ]
        value = jnp.concatenate([pair[group] for group in range(2) for pair in pairs], axis=0)
        value = permuted(value, back)
        for group in range(2):
            where = pl.ds(pl.multiple_of((group * STEP_ROWS + block * BLOCK) * 8, 8), BLOCK * 8)
            for col in range(2):
                part = value[group * BLOCK * 8 : (group + 1) * BLOCK * 8, col * LANES : (col + 1) * LANES]
                rows_t[col, where, :] = part

    to_stage(t_stage, rows_t)
    for copy in outputs():
        copy.start()
    for copy in outputs():
        copy.wait()


def place_kernel(received, t_in, t_out, sem):
    core = lax.axis_index("ta")
    half = received.shape[1]
    place = pl.ds(pl.multiple_of((1 - core) * half, half), half)
    copy = pltpu.make_async_copy(received, t_out.at[:, place, :], sem)
    copy.start()
    copy.wait()


def on_device(t_initial, power_mantissa, tile_exponent, channel_mask, material, conductivity):
    depth, rows, cols = t_initial.shape
    layers = 2 * depth
    n_gx, n_gy = lax.axis_size("gx"), lax.axis_size("gy")
    array = jax.ShapeDtypeStruct
    swap = [(0, 1), (1, 0)]
    out_sides = [None] if n_gy == 2 else [True, False]
    in_sides = [None] if n_gy == 2 else [False, True]
    count = len(out_sides)

    t_other = lax.ppermute(t_initial, "ta", swap)
    exponents = tile_exponent.transpose(1, 0, 2)
    plain_shape = array((depth, 3, rows + 2 * RIM, LANES), F32)
    along = array((depth, ROWS_P, LANES), F32)
    across = (array((depth, ROWS_G, LANES), F32),) * count
    corner = (array((depth, ROWS_D, LANES), F32),) * (2 * count)
    sent = pl.pallas_call(
        functools.partial(send_kernel, out_sides),
        out_shape=(plain_shape, along, along) + across + corner,
        in_specs=[HBM, HBM, HBM],
        out_specs=(ANY,) + (VMEM,) * (2 + 3 * count),
        scratch_shapes=[
            pltpu.VMEM(plain_shape.shape, F32),
            pltpu.VMEM(power_mantissa.shape, power_mantissa.dtype),
            pltpu.SMEM(exponents.shape, jnp.int32),
            pltpu.VMEM(t_initial.shape, F32),
            pltpu.SemaphoreType.DMA((depth,)),
            pltpu.SemaphoreType.DMA((2, depth)),
            pltpu.SemaphoreType.DMA,
        ],
        compiler_params=params(12),
        name="send",
    )(*(pltpu.with_memory_space_constraint(value, pltpu.HBM) for value in (power_mantissa, exponents, t_initial)))
    sent = tuple(sent[:1]) + tuple(lax.optimization_barrier(tuple(sent[1:]) + (t_other,)))
    sent, t_other = sent[:-1], sent[-1]
    plain, first, second = sent[:3]
    to_g, to_d_first, to_d_second = sent[3 : 3 + count], sent[3 + count : 3 + 2 * count], sent[3 + 2 * count :]

    def move(value, start, step_x):
        pairs = []
        for z in range(n_gx):
            to_z = z if start is None else z + 1 if (z - start) % 2 == 0 else z - 1
            for x in range(n_gy):
                to_x = x ^ 1 if step_x is None else x + step_x
                if 0 <= to_z < n_gx and 0 <= to_x < n_gy:
                    pairs.append((z * n_gy + x, to_z * n_gy + to_x))
        return lax.ppermute(value, ("gx", "gy"), pairs)

    steps = [None] if n_gy == 2 else [1, -1]
    from_g = [move(value, None, step) for value, step in zip(to_g, steps)]
    from_first = move(first, 0, 0)
    from_second = move(second, 1, 0)
    d_first = [move(value, 0, step) for value, step in zip(to_d_first, steps)]
    d_second = [move(value, 1, step) for value, step in zip(to_d_second, steps)]

    wide = jnp.pad(channel_mask, ((0, 0), (RIM, RIM)))
    mask = lax.dynamic_slice_in_dim(wide, lax.axis_index("gy") * cols, cols + 2 * RIM, 1).astype(F32) * COOLANT
    inner = mask[:, RIM : RIM + cols].reshape(layers, 64, 4).transpose(2, 0, 1)
    outer = jnp.zeros((layers, 64 - 2 * WIDE), F32)
    outer = jnp.concatenate([mask[:, RIM + cols :][:, :WIDE], outer, mask[:, RIM - WIDE : RIM]], axis=1)
    flow = jnp.concatenate([inner, outer[None]], axis=0).reshape(layers * 5, 64)
    flow = jnp.concatenate([flow, flow], axis=1)

    grouped = array(((STEP_ROWS + 2) * 40, LANES), F32)
    now = pl.pallas_call(
        stack_kernel,
        out_shape=grouped,
        in_specs=[ANY] * 2,
        out_specs=VMEM,
        scratch_shapes=[
            pltpu.VMEM((2, layers, rows + 16, LANES), F32),
            pltpu.SemaphoreType.DMA((2, depth, 2)),
        ],
        compiler_params=params(24),
        name="stack",
    )(t_initial, t_other)

    half = array((depth, SWAP, LANES), F32)
    own, other = pl.pallas_call(
        functools.partial(sum_kernel, in_sides),
        out_shape=(half, half),
        in_specs=[VMEM] * (3 + 3 * count),
        out_specs=(ANY, ANY),
        scratch_shapes=[
            pltpu.VMEM((depth, 3, SUM_ROWS, LANES), F32),
            pltpu.VMEM((2, depth, 16, LANES), F32),
            pltpu.SemaphoreType.DMA((2, 4)),
        ],
        compiler_params=params(12),
        name="sum",
    )(plain, *from_g, from_first, from_second, *d_first, *d_second)
    received = lax.ppermute(other, "ta", swap)
    whole = array((depth, rows, cols), F32)
    heat_source = pl.pallas_call(
        heat_kernel,
        out_shape=whole,
        in_specs=[VMEM] * 2,
        out_specs=VMEM,
        compiler_params=params(8),
        name="heat",
    )(own, other)

    work = pltpu.VMEM(grouped.shape, F32)
    t_part, sent = pl.pallas_call(
        functools.partial(solve_kernel, (n_gx * rows, n_gy * cols)),
        out_shape=(whole, array((depth, rows // 2, cols), F32)),
        in_specs=[ANY, ANY] + [VMEM] * 2 + [SMEM, SMEM],
        out_specs=(ANY, ANY),
        scratch_shapes=[
            pltpu.VMEM((layers, SWAP, LANES), F32),
            pltpu.VMEM((2, REGION * 8, LANES), F32),
        ]
        + [work] * 9
        + [
            pltpu.VMEM((layers, rows // 2, cols), F32),
            pltpu.SemaphoreType.DMA((2,)),
            pltpu.SemaphoreType.DMA((2,)),
        ],
        compiler_params=params(30),
        name="solve",
    )(own, received, now, flow, material, conductivity)
    received = lax.ppermute(sent, "ta", swap)
    temperature = pl.pallas_call(
        place_kernel,
        out_shape=whole,
        in_specs=[ANY, ANY],
        out_specs=ANY,
        scratch_shapes=[pltpu.SemaphoreType.DMA],
        input_output_aliases={1: 0},
        compiler_params=params(4),
        name="place",
    )(received, t_part)
    return temperature, heat_source


def solution(mesh):
    cells = P("ta", ("group", "gx"), "gy")
    return jax.shard_map(
        on_device,
        mesh=mesh,
        in_specs=(cells, cells, cells, P(), P(), P()),
        out_specs=(cells, cells),
        check_vma=False,
    )
```

```python
import functools

import jax
import jax.numpy as jnp
from jax import lax
from jax.experimental import pallas as pl
from jax.experimental.pallas import tpu as pltpu
from jax.sharding import PartitionSpec as P

RIM = 64
TILE = 64
STEPS = 2
SWEEPS = 3
COOLANT = 2.0

LANES = 128
WIDE = 6
REGION = 140
STEP_ROWS = 70
BLOCK = 35
SPAN = 35
SUM_ROWS = 272
HALF_ROWS = 144
SWAP = 3 * HALF_ROWS + 16
EDGE = 72
SLOTS = LANES // WIDE
ROWS_P = 2 * EDGE + 8 + 16
ROWS_G = SUM_ROWS // 2 + 16 + 16
ROWS_D = 40
F32 = jnp.float32
VMEM = pl.BlockSpec(memory_space=pltpu.VMEM)
SMEM = pl.BlockSpec(memory_space=pltpu.SMEM)
ANY = pl.BlockSpec(memory_space=pl.ANY)
HBM = pl.BlockSpec(memory_space=pltpu.HBM)


def params(megabytes):
    return pltpu.CompilerParams(vmem_limit_bytes=megabytes << 20)


def rows8(start):
    return pl.ds(pl.multiple_of(start, 8), 8)


def lane_ids():
    return lax.broadcasted_iota(jnp.int32, (8, LANES), 1)


def turn(value, shift):
    shift = shift % LANES
    return pltpu.roll(value, shift, 1) if shift else value


def by_side(sides, body, *lists):
    for place, side in enumerate(sides):
        rest = [values[place] for values in lists]
        if side is None:
            first = lax.axis_index("gy") == 0
            pl.when(first)(functools.partial(body, True, place, *rest))
            pl.when(jnp.logical_not(first))(functools.partial(body, False, place, *rest))
        else:
            body(side, place, *rest)


def send_kernel(sides, mantissa_in, exponent_in, t_in, *refs):
    count = len(sides)
    whole, to_first, to_second = refs[:3]
    to_g, to_d_first, to_d_second = refs[3 : 3 + count], refs[3 + count : 3 + 2 * count], refs[3 + 2 * count : 3 + 3 * count]
    plain, mantissa, exponent, t_ref, sems, in_sems, exponent_sem = refs[3 + 3 * count :]
    depth, rows, _ = mantissa.shape
    lane = lane_ids()
    low = lane < 64
    wide_lane = lax.broadcasted_iota(jnp.int32, (16, LANES), 1)

    def place(total, value, source, target, width):
        moved = turn(value, target - source)
        return jnp.where((lane >= target) & (lane < target + width), moved, total)

    odd = lax.rem(lax.axis_index("gx"), 2)
    edges = [which * (rows - EDGE) for which in (1 - odd, odd)]
    t_edges = [which * (rows - 2 * RIM - 8) for which in (1 - odd, odd)]

    def copy(layer):
        return pltpu.make_async_copy(plain.at[layer], whole.at[layer], sems.at[layer])

    def pack(layer):
        def cells(col, row):
            return plain[layer, col, rows8(row), :]

        def t_cells(col, row):
            return t_ref[layer, rows8(row), col * LANES : (col + 1) * LANES]

        for out, edge, t_edge in ((to_first, edges[0], t_edges[0]), (to_second, edges[1], t_edges[1])):
            extra = jnp.zeros((8, LANES), F32)
            for j in range(9):
                left, right = cells(0, edge + 8 * j), cells(2, edge + 8 * j)
                out[layer, 8 * j : 8 * j + 8, :] = cells(1, edge + 8 * j)
                out[layer, EDGE + 8 * j : EDGE + 8 * j + 8, :] = jnp.where(low, right, left)
                extra = place(extra, jnp.where(low, left, right), 64 - WIDE, 2 * WIDE * j, 2 * WIDE)
            out[layer, 2 * EDGE : 2 * EDGE + 8, :] = extra
            for col in range(2):
                start = 2 * EDGE + 8 + 8 * col
                out[layer, start : start + 8, :] = t_cells(col, t_edge)

        def side(right, _, g_ref, first_ref, second_ref):
            col, t_col = (2, 1) if right else (0, 0)
            at, t_at = (64 - WIDE, LANES - WIDE) if right else (64, 0)
            half = SUM_ROWS // 2

            def both(one, two):
                return jnp.where(low, turn(two, 64), one) if right else jnp.where(low, one, turn(two, 64))

            for j in range(17):
                one, two = cells(col, RIM - 8 + 8 * j), cells(col, RIM - 8 + half + 8 * j)
                g_ref[layer, 8 * j : 8 * j + 8, :] = both(one, two)
            for first, parts, source in (
                (half, [cells(col, RIM - 8 + 8 * j) for j in range(34)], at),
                (half + 16, [t_cells(t_col, 8 * j) for j in range(32)], t_at),
            ):
                for part in range(2):
                    extra = jnp.zeros((8, LANES), F32)
                    for slot, value in enumerate(parts[part * SLOTS : (part + 1) * SLOTS]):
                        extra = place(extra, value, source, WIDE * slot, WIDE)
                    g_ref[layer, first + 8 * part : first + 8 * part + 8, :] = extra
            for out, edge, t_edge in ((first_ref, edges[0], t_edges[0]), (second_ref, edges[1], t_edges[1])):
                strips = [cells(col, edge + 8 * j) for j in range(9)]
                for j in range(4):
                    out[layer, 8 * j : 8 * j + 8, :] = both(strips[j], strips[j + 5])
                start = 0 if right else 64
                extra = strips[4]
                for j in range(9):
                    extra = place(extra, strips[j], at, start + WIDE * j, WIDE)
                extra = place(extra, t_cells(t_col, t_edge), t_at, start + 9 * WIDE, WIDE)
                out[layer, 32:40, :] = extra

        by_side(sides, side, to_g, to_d_first, to_d_second)

    def arrivals(layer):
        return (
            pltpu.make_async_copy(mantissa_in.at[layer], mantissa.at[layer], in_sems.at[0, layer]),
            pltpu.make_async_copy(t_in.at[layer], t_ref.at[layer], in_sems.at[1, layer]),
        )

    scales = pltpu.make_async_copy(exponent_in, exponent, exponent_sem)
    scales.start()
    for layer in range(depth):
        for one in arrivals(layer):
            one.start()
    scales.wait()

    @pl.loop(0, depth)
    def _(layer):
        for one in arrivals(layer):
            one.wait()

        @pl.loop(0, rows // TILE)
        def _(tile_row):
            for col in range(3):
                left = exponent[tile_row, layer, 2 * col]
                right = exponent[tile_row, layer, 2 * col + 1]
                scale = jnp.exp2(jnp.where(wide_lane < TILE, left, right).astype(F32))
                for part in range(TILE // 16):
                    where = pl.ds(pl.multiple_of(tile_row * TILE + part * 16, 16), 16)
                    cells = mantissa[layer, where, col * LANES : (col + 1) * LANES]
                    plain[layer, col, where, :] = cells.astype(F32) * scale

        copy(layer).start()
        pack(layer)

    for layer in range(depth):
        copy(layer).wait()


def sum_kernel(sides, *refs):
    count = len(sides)
    plain, payloads = refs[0], refs[1:]
    from_g, payloads = payloads[:count], payloads[count:]
    from_first, payloads = payloads[0], payloads[1:]
    from_second, payloads = payloads[0], payloads[1:]
    d_first, payloads = payloads[:count], payloads[count:]
    d_second, payloads = payloads[:count], payloads[count:]
    own, other, total, t_edge, sems = refs[3 + 3 * count :]
    depth = plain.shape[0]
    core = lax.axis_index("ta")
    odd = lax.rem(lax.axis_index("gx"), 2)
    after = (1 - odd, odd)
    lane = lane_ids()
    low = lane < 64
    half = SUM_ROWS // 2
    centre = (lane >= 64 - WIDE) & (lane < 64 + WIDE)

    def copies(side, out, index):
        row = pl.multiple_of(side * (SUM_ROWS - HALF_ROWS), 8)
        made = [
            pltpu.make_async_copy(
                total.at[:, col, pl.ds(row, HALF_ROWS), :],
                out.at[:, pl.ds(col * HALF_ROWS, HALF_ROWS), :],
                sems.at[index, col],
            )
            for col in range(3)
        ]
        made.append(pltpu.make_async_copy(t_edge.at[side], out.at[:, pl.ds(3 * HALF_ROWS, 16), :], sems.at[index, 3]))
        return made

    @pl.loop(0, depth)
    def _(layer):
        for j in range(SUM_ROWS // 8):
            row, where = RIM - 8 + 8 * j, pl.ds(8 * j, 8)
            left, right = plain[layer, 0, row : row + 8, :], plain[layer, 2, row : row + 8, :]
            total[layer, 0, where, :] = plain[layer, 1, row : row + 8, :]
            total[layer, 1, where, :] = jnp.where(low, right, left)
            total[layer, 2, where, :] = jnp.where(centre, jnp.where(low, left, right), 0.0)

        def add(col, row, value):
            total[layer, col, rows8(row), :] = total[layer, col, rows8(row), :] + value

        for which, ref in zip(after, (from_first, from_second)):
            edge = which * (SUM_ROWS - EDGE)
            t_edge[which, layer, :, :] = ref[layer, 2 * EDGE + 8 :, :]
            extra = ref[layer, 2 * EDGE : 2 * EDGE + 8, :]
            for j in range(9):
                add(0, edge + 8 * j, ref[layer, 8 * j : 8 * j + 8, :])
                add(1, edge + 8 * j, ref[layer, EDGE + 8 * j : EDGE + 8 * j + 8, :])
                add(2, edge + 8 * j, jnp.where(centre, turn(extra, 64 - WIDE - 2 * WIDE * j), 0.0))

        def side(right, _, g_ref, first_ref, second_ref):
            main = low if right else jnp.logical_not(low)
            at, t_at = (64, 0) if right else (64 - WIDE, LANES - WIDE)

            def window(value, source, target):
                return jnp.where((lane >= target) & (lane < target + WIDE), turn(value, target - source), 0.0)

            for j in range(17):
                value = g_ref[layer, 8 * j : 8 * j + 8, :]
                add(1, 8 * j, jnp.where(main, value, 0.0))
                add(1, half + 8 * j, jnp.where(main, turn(value, 64), 0.0))
            extras = [g_ref[layer, half + 8 * j : half + 8 * j + 8, :] for j in range(4)]
            for j in range(34):
                value = window(extras[j // SLOTS], WIDE * (j % SLOTS), at)
                if 1 <= j <= 32:
                    k = j - 1
                    value = value + window(extras[2 + k // SLOTS], WIDE * (k % SLOTS), t_at)
                add(2, 8 * j, value)
            for which, ref in zip(after, (first_ref, second_ref)):
                edge, t_row = which * (SUM_ROWS - EDGE), which * (SUM_ROWS - 8)
                extra = ref[layer, 32:40, :]
                start = 64 if right else 0
                for j in range(9):
                    value = ref[layer, 8 * (j % 5) : 8 * (j % 5) + 8, :]
                    if j > 4:
                        value = turn(value, 64)
                    add(1, edge + 8 * j, jnp.where(main, value, 0.0))
                    add(2, edge + 8 * j, window(extra, start + WIDE * j, at))
                add(2, t_row, window(extra, start + 9 * WIDE, t_at))

        by_side(sides, side, from_g, d_first, d_second)

    made = copies(1 - core, other, 0) + copies(core, own, 1)
    for one in made:
        one.start()
    for one in made:
        one.wait()


def heat_kernel(own, other, out):
    depth = own.shape[0]
    core = lax.axis_index("ta")
    low = lane_ids() < 64

    def move(src, first):
        @pl.loop(0, depth)
        def _(layer):
            for j in range(16):
                one = turn(src[layer, 8 + 8 * j : 16 + 8 * j, :], 64)
                two = turn(src[layer, HALF_ROWS + 8 + 8 * j : HALF_ROWS + 16 + 8 * j, :], 64)
                out[layer, rows8(first + 8 * j), :LANES] = jnp.where(low, two, one)
                out[layer, rows8(first + 8 * j), LANES:] = jnp.where(low, one, two)

    move(own, core * 128)
    move(other, 128 - core * 128)


def permutation(inverse=False, shift=0):
    rows = lax.broadcasted_iota(jnp.int32, (256, 256), 0)
    cols = lax.broadcasted_iota(jnp.int32, (256, 256), 1)
    if inverse:
        rows, cols = cols, rows
    return jnp.where((rows + shift) % 256 == 4 * (cols % 64) + cols // 64, 1.0, 0.0).astype(jnp.bfloat16)


def permuted(value, matrix):
    parts = []
    for _ in range(3):
        part = value.astype(jnp.bfloat16)
        value = value - part.astype(F32)
        parts.append(part)
    moved = jnp.dot(jnp.concatenate(parts, axis=0), matrix, preferred_element_type=F32)
    high, middle, low = (moved[k * value.shape[0] : (k + 1) * value.shape[0]] for k in range(3))
    return high + (middle + low)


def to_groups(first, second):
    low = lane_ids() < 64
    out = []
    for half in range(2):
        one = first[:, half * LANES : (half + 1) * LANES]
        two = second[:, half * LANES : (half + 1) * LANES]
        out += [jnp.where(low, one, turn(two, 64)), jnp.where(low, turn(one, 64), two)]
    return out


def to_rows(parts):
    low = lane_ids() < 64
    one, two = [], []
    for half in range(2):
        left, right = parts[2 * half], parts[2 * half + 1]
        one.append(jnp.where(low, left, turn(right, 64)))
        two.append(jnp.where(low, turn(left, 64), right))
    return jnp.concatenate(one, axis=1), jnp.concatenate(two, axis=1)


def group_cells(load, dst, matrix):
    @pl.loop(0, STEP_ROWS // BLOCK)
    def _(block):
        rows = [group * STEP_ROWS + block * BLOCK + step for group in range(2) for step in range(BLOCK)]
        halves = [jnp.concatenate([load(row, half) for row in rows], axis=0) for half in range(2)]
        value = permuted(jnp.concatenate(halves, axis=1), matrix)
        for step in range(BLOCK):
            parts = to_groups(*(value[8 * at : 8 * at + 8] for at in (step, BLOCK + step)))
            for col in range(4):
                dst[rows8((block * BLOCK + step + 1) * 40 + 8 * col), :] = parts[col]


def stack_kernel(t_own, t_other, now, t_cells, t_sems):
    core = lax.axis_index("ta")
    depth, rows, _ = t_own.shape
    layers = 2 * depth
    copies = []
    for which, t_src in enumerate((t_own, t_other)):
        base = core * depth if which == 0 else (1 - core) * depth
        for layer in range(depth):
            for col in range(2):
                copies.append(
                    pltpu.make_async_copy(
                        t_src.at[layer, :, col * LANES : (col + 1) * LANES],
                        t_cells.at[col, base + layer, pl.ds(8, rows), :],
                        t_sems.at[which, layer, col],
                    )
                )
    for copy in copies:
        copy.start()
    zero = jnp.zeros((8, LANES), F32)
    for col in range(2):
        for layer in range(layers):
            t_cells[col, layer, 0:8, :] = zero
            t_cells[col, layer, rows + 8 : rows + 16, :] = zero

    @pl.loop(0, STEP_ROWS + 2)
    def _(step):
        now[rows8(step * 40 + 32), :] = zero

    for copy in copies:
        copy.wait()
    flat = t_cells.reshape(2, layers * (rows + 16), LANES)
    first = 2 + core * 128

    def load(row, half):
        return flat[half, pl.ds(first + row, layers, stride=rows + 16), :]

    group_cells(load, now, permutation())


def solve_kernel(bounds, own, other, now_in, flow, material, conductivity, t_out, sent, *refs):
    cells, rows_t, heat, now, later, cond, f_down, f_right, f_above, inverse, base, t_stage, in_sems, sems = refs
    core = lax.axis_index("ta")
    gx, gy = lax.axis_index("gx"), lax.axis_index("gy")
    lane = lane_ids()
    level = lax.broadcasted_iota(jnp.int32, (8, LANES), 0)
    low = lane < 64
    layers = 8
    depth = layers // 2

    def at(step, col):
        return rows8(step * 40 + 8 * col)

    incoming = [
        pltpu.make_async_copy(src, cells.at[pl.ds(first, depth)], in_sems.at[which])
        for which, (src, first) in enumerate(((own, core * depth), (other, (1 - core) * depth)))
    ]
    for copy in incoming:
        copy.start()
    for copy in incoming:
        copy.wait()
    flat = cells.reshape(layers * SWAP, LANES)

    def across(row):
        return flat[pl.ds(row, layers, stride=SWAP), :]

    def to_stage(stage, src):
        @pl.loop(0, 16)
        def _(tile):
            for layer in range(layers):
                for col in range(2):
                    value = src[col, pl.ds((6 + 8 * tile) * 8 + layer, 8, stride=8), :]
                    stage[layer, rows8(8 * tile), col * LANES : (col + 1) * LANES] = value

    def outputs():
        mine = t_stage.at[pl.ds(core * depth, depth)]
        theirs = t_stage.at[pl.ds((1 - core) * depth, depth)]
        half = t_stage.shape[1]
        place = pl.ds(pl.multiple_of(core * half, half), half)
        return (
            pltpu.make_async_copy(theirs, sent, sems.at[0]),
            pltpu.make_async_copy(mine, t_out.at[:, place, :], sems.at[1]),
        )

    group_cells(lambda row, half: across(half * HALF_ROWS + 2 + row), heat, permutation(shift=64))
    t_edge = jnp.concatenate(
        [
            jnp.concatenate([across(3 * HALF_ROWS + 8 * col + i) for i in range(8)], axis=0)
            for col in range(2)
        ],
        axis=1,
    )
    t_edge = permuted(t_edge, permutation())
    halo_lanes = (lane < WIDE) | ((lane >= 64 - WIDE) & (lane < 64 + WIDE)) | (lane >= LANES - WIDE)

    @pl.loop(0, STEP_ROWS // 14)
    def _(block):
        for part in range(14):
            step = block * 14 + part
            first, second = across(2 * HALF_ROWS + 2 + step), across(2 * HALF_ROWS + 2 + step + STEP_ROWS)
            first_turned, second_turned = turn(first, 64), turn(second, 64)
            upper_lanes = jnp.where(lane < 64 + WIDE, first, first_turned)
            lower_lanes = jnp.where(lane < WIDE, second_turned, second)
            heat[at(step + 1, 4), :] = jnp.where(halo_lanes, jnp.where(low, lower_lanes, upper_lanes), 0.0)
            upper_lanes = jnp.where(lane < 64 + WIDE, first_turned, first)
            lower_lanes = jnp.where(lane < WIDE, second, second_turned)
            now[at(step + 1, 4), :] = jnp.where(halo_lanes, jnp.where(low, lower_lanes, upper_lanes), 0.0)
            for col in range(4):
                now[at(step + 1, col), :] = now_in[at(step + 1, col), :]

    @pl.when(core == 0)
    def _():
        for row in range(6):
            value = t_edge[8 * row + 16 : 8 * row + 24]
            parts = to_groups(value, value)
            for col in range(4):
                now[at(row + 1, col), :] = jnp.where(low, parts[col], now[at(row + 1, col), :])

    @pl.when(core == 1)
    def _():
        for row in range(6):
            value = t_edge[8 * row : 8 * row + 8]
            parts = to_groups(value, value)
            for col in range(4):
                now[at(row + 65, col), :] = jnp.where(low, now[at(row + 65, col), :], parts[col])

    def ghosts(ref):
        for col in range(5):
            ref[at(0, col), :] = turn(ref[at(STEP_ROWS, col), :], 64)
            ref[at(STEP_ROWS + 1, col), :] = turn(ref[at(1, col), :], 64)

    last = (lane == 63) | (lane == 127)
    first = (lane == 0) | (lane == 64)

    def to_right(values):
        inner, outer = turn(values[0], -1), turn(values[4], -1)
        return values[1:4] + [jnp.where(last, outer, inner), jnp.where(last, inner, outer)]

    def to_left(values):
        inner, outer = turn(values[3], 1), turn(values[4], 1)
        return [jnp.where(first, outer, inner)] + values[:3] + [jnp.where(first, inner, outer)]

    def upper(value):
        return pltpu.roll(value, 7, 0)

    def lower(value):
        return pltpu.roll(value, 1, 0)

    has_right = (gy + 1) * 256 < bounds[1]
    half_lane = jnp.where(low, lane, lane - 64)
    keep = ((half_lane < WIDE) & has_right) | ((half_lane >= 64 - WIDE) & (gy > 0))
    halo_mask = jnp.where(keep, 1.0, 0.0)
    scale = jnp.full((8, LANES), conductivity[material[0]], F32)
    for layer in range(1, layers):
        scale = jnp.where(level == layer, conductivity[material[layer]], scale)
    not_top = jnp.where(level < layers - 1, 1.0, 0.0)
    not_bottom = jnp.where(level > 0, 1.0, 0.0)
    flows = [flow[8 * col : 8 * col + 8, :] for col in range(5)]
    first_row = gx * 256 + core * 128 - 6

    def masks(step):
        ones = []
        for group in range(2):
            row = first_row + step + group * STEP_ROWS
            ones.append(jnp.where((row >= 0) & (row < bounds[0]), 1.0, 0.0))
        inner = jnp.where(low, ones[0], ones[1])
        return [inner] * 4 + [jnp.where(low, ones[1], ones[0]) * halo_mask]

    def conductances(src):
        @pl.loop(0, STEP_ROWS // 35)
        def _(block):
            for part in range(35):
                step = block * 35 + part
                mask = masks(step)
                for col in range(5):
                    where = at(step + 1, col)
                    cond[where, :] = (scale * mask[col]) * (1.0 + 0.5 * jnp.tanh(src[where, :]))

        ghosts(cond)

    def coefficients(src):
        @pl.loop(0, STEP_ROWS // 10)
        def _(block):
            start = block * 10
            lines = [[cond[at(start + part, col), :] for col in range(5)] for part in range(12)]
            for part in range(10):
                up, here, down = lines[part], lines[part + 1], lines[part + 2]
                mask = masks(start + part)
                rights, lefts = to_right(here), to_left(here)
                for col in range(5):
                    where = at(start + part + 1, col)
                    centre = here[col]
                    over = centre + upper(centre) * not_top
                    under = centre + lower(centre) * not_bottom
                    face_down = 0.5 * (centre + down[col])
                    face_right = 0.5 * (centre + rights[col])
                    total = (1.0 + flows[col]) + 0.5 * (centre + up[col]) + face_down
                    total = total + face_right + 0.5 * (centre + lefts[col]) + over + under
                    f_down[where, :] = face_down
                    f_right[where, :] = face_right
                    f_above[where, :] = over * not_top
                    inverse[where, :] = mask[col] / total
                    base[where, :] = src[where, :] + heat[where, :]

        for col in range(5):
            f_down[at(0, col), :] = 0.5 * (cond[at(0, col), :] + cond[at(1, col), :])

    def sweep(src, dst):
        @pl.loop(0, STEP_ROWS // SPAN)
        def _(block):
            start = block * SPAN
            lines = [[src[at(start + part, col), :] for col in range(5)] for part in range(SPAN + 2)]
            faces = [[f_down[at(start + part, col), :] for col in range(5)] for part in range(SPAN + 1)]
            for part in range(SPAN):
                up, here, down = lines[part], lines[part + 1], lines[part + 2]
                face_right = [f_right[at(start + part + 1, col), :] for col in range(5)]
                rights = to_right(here)
                lefts = to_left([face * value for face, value in zip(face_right, here)])
                for col in range(5):
                    where = at(start + part + 1, col)
                    face_above = f_above[where, :]
                    total = base[where, :] + (faces[part][col] + flows[col]) * up[col]
                    total = total + faces[part + 1][col] * down[col]
                    total = total + (face_right[col] * rights[col] + lefts[col])
                    total = total + (face_above * upper(here[col]) + lower(face_above * here[col]))
                    dst[where, :] = total * inverse[where, :]

        ghosts(dst)

    ghosts(now)
    for _ in range(STEPS):
        conductances(now)
        coefficients(now)
        for _ in range(SWEEPS):
            sweep(now, later)
            now, later = later, now

    back = permutation(inverse=True)

    @pl.loop(0, STEP_ROWS // BLOCK)
    def _(block):
        pairs = [
            to_rows([now[at(block * BLOCK + part + 1, col), :] for col in range(4)]) for part in range(BLOCK)
        ]
        value = jnp.concatenate([pair[group] for group in range(2) for pair in pairs], axis=0)
        value = permuted(value, back)
        for group in range(2):
            where = pl.ds(pl.multiple_of((group * STEP_ROWS + block * BLOCK) * 8, 8), BLOCK * 8)
            for col in range(2):
                part = value[group * BLOCK * 8 : (group + 1) * BLOCK * 8, col * LANES : (col + 1) * LANES]
                rows_t[col, where, :] = part

    to_stage(t_stage, rows_t)
    for copy in outputs():
        copy.start()
    for copy in outputs():
        copy.wait()


def place_kernel(received, t_in, t_out, sem):
    core = lax.axis_index("ta")
    half = received.shape[1]
    place = pl.ds(pl.multiple_of((1 - core) * half, half), half)
    copy = pltpu.make_async_copy(received, t_out.at[:, place, :], sem)
    copy.start()
    copy.wait()


def on_device(t_initial, power_mantissa, tile_exponent, channel_mask, material, conductivity):
    depth, rows, cols = t_initial.shape
    layers = 2 * depth
    n_gx, n_gy = lax.axis_size("gx"), lax.axis_size("gy")
    array = jax.ShapeDtypeStruct
    swap = [(0, 1), (1, 0)]
    out_sides = [None] if n_gy == 2 else [True, False]
    in_sides = [None] if n_gy == 2 else [False, True]
    count = len(out_sides)

    t_other = lax.ppermute(t_initial, "ta", swap)
    exponents = tile_exponent.transpose(1, 0, 2)
    plain_shape = array((depth, 3, rows + 2 * RIM, LANES), F32)
    along = array((depth, ROWS_P, LANES), F32)
    across = (array((depth, ROWS_G, LANES), F32),) * count
    corner = (array((depth, ROWS_D, LANES), F32),) * (2 * count)
    sent = pl.pallas_call(
        functools.partial(send_kernel, out_sides),
        out_shape=(plain_shape, along, along) + across + corner,
        in_specs=[HBM, HBM, HBM],
        out_specs=(ANY,) + (VMEM,) * (2 + 3 * count),
        scratch_shapes=[
            pltpu.VMEM(plain_shape.shape, F32),
            pltpu.VMEM(power_mantissa.shape, power_mantissa.dtype),
            pltpu.SMEM(exponents.shape, jnp.int32),
            pltpu.VMEM(t_initial.shape, F32),
            pltpu.SemaphoreType.DMA((depth,)),
            pltpu.SemaphoreType.DMA((2, depth)),
            pltpu.SemaphoreType.DMA,
        ],
        compiler_params=params(12),
        name="send",
    )(*(pltpu.with_memory_space_constraint(value, pltpu.HBM) for value in (power_mantissa, exponents, t_initial)))
    sent = tuple(sent[:1]) + tuple(lax.optimization_barrier(tuple(sent[1:]) + (t_other,)))
    sent, t_other = sent[:-1], sent[-1]
    plain, first, second = sent[:3]
    to_g, to_d_first, to_d_second = sent[3 : 3 + count], sent[3 + count : 3 + 2 * count], sent[3 + 2 * count :]

    def move(value, start, step_x):
        pairs = []
        for z in range(n_gx):
            to_z = z if start is None else z + 1 if (z - start) % 2 == 0 else z - 1
            for x in range(n_gy):
                to_x = x ^ 1 if step_x is None else x + step_x
                if 0 <= to_z < n_gx and 0 <= to_x < n_gy:
                    pairs.append((z * n_gy + x, to_z * n_gy + to_x))
        return lax.ppermute(value, ("gx", "gy"), pairs)

    steps = [None] if n_gy == 2 else [1, -1]
    from_g = [move(value, None, step) for value, step in zip(to_g, steps)]
    from_first = move(first, 0, 0)
    from_second = move(second, 1, 0)
    d_first = [move(value, 0, step) for value, step in zip(to_d_first, steps)]
    d_second = [move(value, 1, step) for value, step in zip(to_d_second, steps)]

    wide = jnp.pad(channel_mask, ((0, 0), (RIM, RIM)))
    mask = lax.dynamic_slice_in_dim(wide, lax.axis_index("gy") * cols, cols + 2 * RIM, 1).astype(F32) * COOLANT
    inner = mask[:, RIM : RIM + cols].reshape(layers, 64, 4).transpose(2, 0, 1)
    outer = jnp.zeros((layers, 64 - 2 * WIDE), F32)
    outer = jnp.concatenate([mask[:, RIM + cols :][:, :WIDE], outer, mask[:, RIM - WIDE : RIM]], axis=1)
    flow = jnp.concatenate([inner, outer[None]], axis=0).reshape(layers * 5, 64)
    flow = jnp.concatenate([flow, flow], axis=1)

    grouped = array(((STEP_ROWS + 2) * 40, LANES), F32)
    now = pl.pallas_call(
        stack_kernel,
        out_shape=grouped,
        in_specs=[ANY] * 2,
        out_specs=VMEM,
        scratch_shapes=[
            pltpu.VMEM((2, layers, rows + 16, LANES), F32),
            pltpu.SemaphoreType.DMA((2, depth, 2)),
        ],
        compiler_params=params(24),
        name="stack",
    )(t_initial, t_other)

    from_first, now = lax.optimization_barrier((from_first, now))
    half = array((depth, SWAP, LANES), F32)
    own, other = pl.pallas_call(
        functools.partial(sum_kernel, in_sides),
        out_shape=(half, half),
        in_specs=[VMEM] * (3 + 3 * count),
        out_specs=(ANY, ANY),
        scratch_shapes=[
            pltpu.VMEM((depth, 3, SUM_ROWS, LANES), F32),
            pltpu.VMEM((2, depth, 16, LANES), F32),
            pltpu.SemaphoreType.DMA((2, 4)),
        ],
        compiler_params=params(12),
        name="sum",
    )(plain, *from_g, from_first, from_second, *d_first, *d_second)
    received = lax.ppermute(other, "ta", swap)
    whole = array((depth, rows, cols), F32)
    heat_source = pl.pallas_call(
        heat_kernel,
        out_shape=whole,
        in_specs=[VMEM] * 2,
        out_specs=VMEM,
        compiler_params=params(8),
        name="heat",
    )(own, other)

    received, heat_source = lax.optimization_barrier((received, heat_source))
    work = pltpu.VMEM(grouped.shape, F32)
    t_part, sent = pl.pallas_call(
        functools.partial(solve_kernel, (n_gx * rows, n_gy * cols)),
        out_shape=(whole, array((depth, rows // 2, cols), F32)),
        in_specs=[ANY, ANY] + [VMEM] * 2 + [SMEM, SMEM],
        out_specs=(ANY, ANY),
        scratch_shapes=[
            pltpu.VMEM((layers, SWAP, LANES), F32),
            pltpu.VMEM((2, REGION * 8, LANES), F32),
        ]
        + [work] * 9
        + [
            pltpu.VMEM((layers, rows // 2, cols), F32),
            pltpu.SemaphoreType.DMA((2,)),
            pltpu.SemaphoreType.DMA((2,)),
        ],
        compiler_params=params(30),
        name="solve",
    )(own, received, now, flow, material, conductivity)
    received = lax.ppermute(sent, "ta", swap)
    temperature = pl.pallas_call(
        place_kernel,
        out_shape=whole,
        in_specs=[ANY, ANY],
        out_specs=ANY,
        scratch_shapes=[pltpu.SemaphoreType.DMA],
        input_output_aliases={1: 0},
        compiler_params=params(4),
        name="place",
    )(received, t_part)
    return temperature, heat_source


def solution(mesh):
    cells = P("ta", ("group", "gx"), "gy")
    return jax.shard_map(
        on_device,
        mesh=mesh,
        in_specs=(cells, cells, cells, P(), P(), P()),
        out_specs=(cells, cells),
        check_vma=False,
    )
```

```python
import functools

import jax
import jax.numpy as jnp
from jax import lax
from jax.experimental import pallas as pl
from jax.experimental.pallas import tpu as pltpu
from jax.sharding import PartitionSpec as P

RIM = 64
TILE = 64
STEPS = 2
SWEEPS = 3
COOLANT = 2.0

LANES = 128
WIDE = 6
REGION = 140
STEP_ROWS = 70
BLOCK = 35
SPAN = 35
SUM_ROWS = 272
HALF_ROWS = 144
SWAP = 3 * HALF_ROWS + 16
EDGE = 72
SLOTS = LANES // WIDE
ROWS_P = 2 * EDGE + 8 + 16
ROWS_G = SUM_ROWS // 2 + 16 + 16
ROWS_D = 40
F32 = jnp.float32
VMEM = pl.BlockSpec(memory_space=pltpu.VMEM)
SMEM = pl.BlockSpec(memory_space=pltpu.SMEM)
ANY = pl.BlockSpec(memory_space=pl.ANY)
HBM = pl.BlockSpec(memory_space=pltpu.HBM)


def params(megabytes):
    return pltpu.CompilerParams(vmem_limit_bytes=megabytes << 20)


def rows8(start):
    return pl.ds(pl.multiple_of(start, 8), 8)


def lane_ids():
    return lax.broadcasted_iota(jnp.int32, (8, LANES), 1)


def turn(value, shift):
    shift = shift % LANES
    return pltpu.roll(value, shift, 1) if shift else value


def by_side(sides, body, *lists):
    for place, side in enumerate(sides):
        rest = [values[place] for values in lists]
        if side is None:
            first = lax.axis_index("gy") == 0
            pl.when(first)(functools.partial(body, True, place, *rest))
            pl.when(jnp.logical_not(first))(functools.partial(body, False, place, *rest))
        else:
            body(side, place, *rest)


def send_kernel(sides, mantissa_in, exponent_in, t_in, *refs):
    count = len(sides)
    whole, to_first, to_second = refs[:3]
    to_g, to_d_first, to_d_second = refs[3 : 3 + count], refs[3 + count : 3 + 2 * count], refs[3 + 2 * count : 3 + 3 * count]
    plain, mantissa, exponent, t_ref, sems, in_sems, exponent_sem = refs[3 + 3 * count :]
    depth, rows, _ = mantissa.shape
    lane = lane_ids()
    low = lane < 64
    wide_lane = lax.broadcasted_iota(jnp.int32, (16, LANES), 1)

    def place(total, value, source, target, width):
        moved = turn(value, target - source)
        return jnp.where((lane >= target) & (lane < target + width), moved, total)

    odd = lax.rem(lax.axis_index("gx"), 2)
    edges = [which * (rows - EDGE) for which in (1 - odd, odd)]
    t_edges = [which * (rows - 2 * RIM - 8) for which in (1 - odd, odd)]

    def copy(layer):
        return pltpu.make_async_copy(plain.at[layer], whole.at[layer], sems.at[layer])

    def pack(layer):
        def cells(col, row):
            return plain[layer, col, rows8(row), :]

        def t_cells(col, row):
            return t_ref[layer, rows8(row), col * LANES : (col + 1) * LANES]

        for out, edge, t_edge in ((to_first, edges[0], t_edges[0]), (to_second, edges[1], t_edges[1])):
            extra = jnp.zeros((8, LANES), F32)
            for j in range(9):
                left, right = cells(0, edge + 8 * j), cells(2, edge + 8 * j)
                out[layer, 8 * j : 8 * j + 8, :] = cells(1, edge + 8 * j)
                out[layer, EDGE + 8 * j : EDGE + 8 * j + 8, :] = jnp.where(low, right, left)
                extra = place(extra, jnp.where(low, left, right), 64 - WIDE, 2 * WIDE * j, 2 * WIDE)
            out[layer, 2 * EDGE : 2 * EDGE + 8, :] = extra
            for col in range(2):
                start = 2 * EDGE + 8 + 8 * col
                out[layer, start : start + 8, :] = t_cells(col, t_edge)

        def side(right, _, g_ref, first_ref, second_ref):
            col, t_col = (2, 1) if right else (0, 0)
            at, t_at = (64 - WIDE, LANES - WIDE) if right else (64, 0)
            half = SUM_ROWS // 2

            def both(one, two):
                return jnp.where(low, turn(two, 64), one) if right else jnp.where(low, one, turn(two, 64))

            for j in range(17):
                one, two = cells(col, RIM - 8 + 8 * j), cells(col, RIM - 8 + half + 8 * j)
                g_ref[layer, 8 * j : 8 * j + 8, :] = both(one, two)
            for first, parts, source in (
                (half, [cells(col, RIM - 8 + 8 * j) for j in range(34)], at),
                (half + 16, [t_cells(t_col, 8 * j) for j in range(32)], t_at),
            ):
                for part in range(2):
                    extra = jnp.zeros((8, LANES), F32)
                    for slot, value in enumerate(parts[part * SLOTS : (part + 1) * SLOTS]):
                        extra = place(extra, value, source, WIDE * slot, WIDE)
                    g_ref[layer, first + 8 * part : first + 8 * part + 8, :] = extra
            for out, edge, t_edge in ((first_ref, edges[0], t_edges[0]), (second_ref, edges[1], t_edges[1])):
                strips = [cells(col, edge + 8 * j) for j in range(9)]
                for j in range(4):
                    out[layer, 8 * j : 8 * j + 8, :] = both(strips[j], strips[j + 5])
                start = 0 if right else 64
                extra = strips[4]
                for j in range(9):
                    extra = place(extra, strips[j], at, start + WIDE * j, WIDE)
                extra = place(extra, t_cells(t_col, t_edge), t_at, start + 9 * WIDE, WIDE)
                out[layer, 32:40, :] = extra

        by_side(sides, side, to_g, to_d_first, to_d_second)

    def arrivals(layer):
        return (
            pltpu.make_async_copy(mantissa_in.at[layer], mantissa.at[layer], in_sems.at[0, layer]),
            pltpu.make_async_copy(t_in.at[layer], t_ref.at[layer], in_sems.at[1, layer]),
        )

    scales = pltpu.make_async_copy(exponent_in, exponent, exponent_sem)
    scales.start()
    for layer in range(depth):
        for one in arrivals(layer):
            one.start()
    scales.wait()

    @pl.loop(0, depth)
    def _(layer):
        for one in arrivals(layer):
            one.wait()

        @pl.loop(0, rows // TILE)
        def _(tile_row):
            for col in range(3):
                left = exponent[tile_row, layer, 2 * col]
                right = exponent[tile_row, layer, 2 * col + 1]
                scale = jnp.exp2(jnp.where(wide_lane < TILE, left, right).astype(F32))
                for part in range(TILE // 16):
                    where = pl.ds(pl.multiple_of(tile_row * TILE + part * 16, 16), 16)
                    cells = mantissa[layer, where, col * LANES : (col + 1) * LANES]
                    plain[layer, col, where, :] = cells.astype(F32) * scale

        copy(layer).start()
        pack(layer)

    for layer in range(depth):
        copy(layer).wait()


def sum_kernel(sides, *refs):
    count = len(sides)
    plain, payloads = refs[0], refs[1:]
    from_g, payloads = payloads[:count], payloads[count:]
    from_first, payloads = payloads[0], payloads[1:]
    from_second, payloads = payloads[0], payloads[1:]
    d_first, payloads = payloads[:count], payloads[count:]
    d_second, payloads = payloads[:count], payloads[count:]
    own, other, total, t_edge, sems = refs[3 + 3 * count :]
    depth = plain.shape[0]
    core = lax.axis_index("ta")
    odd = lax.rem(lax.axis_index("gx"), 2)
    after = (1 - odd, odd)
    lane = lane_ids()
    low = lane < 64
    half = SUM_ROWS // 2
    centre = (lane >= 64 - WIDE) & (lane < 64 + WIDE)

    def copies(side, out, index):
        row = pl.multiple_of(side * (SUM_ROWS - HALF_ROWS), 8)
        made = [
            pltpu.make_async_copy(
                total.at[:, col, pl.ds(row, HALF_ROWS), :],
                out.at[:, pl.ds(col * HALF_ROWS, HALF_ROWS), :],
                sems.at[index, col],
            )
            for col in range(3)
        ]
        made.append(pltpu.make_async_copy(t_edge.at[side], out.at[:, pl.ds(3 * HALF_ROWS, 16), :], sems.at[index, 3]))
        return made

    @pl.loop(0, depth)
    def _(layer):
        for j in range(SUM_ROWS // 8):
            row, where = RIM - 8 + 8 * j, pl.ds(8 * j, 8)
            left, right = plain[layer, 0, row : row + 8, :], plain[layer, 2, row : row + 8, :]
            total[layer, 0, where, :] = plain[layer, 1, row : row + 8, :]
            total[layer, 1, where, :] = jnp.where(low, right, left)
            total[layer, 2, where, :] = jnp.where(centre, jnp.where(low, left, right), 0.0)

        def add(col, row, value):
            total[layer, col, rows8(row), :] = total[layer, col, rows8(row), :] + value

        for which, ref in zip(after, (from_first, from_second)):
            edge = which * (SUM_ROWS - EDGE)
            t_edge[which, layer, :, :] = ref[layer, 2 * EDGE + 8 :, :]
            extra = ref[layer, 2 * EDGE : 2 * EDGE + 8, :]
            for j in range(9):
                add(0, edge + 8 * j, ref[layer, 8 * j : 8 * j + 8, :])
                add(1, edge + 8 * j, ref[layer, EDGE + 8 * j : EDGE + 8 * j + 8, :])
                add(2, edge + 8 * j, jnp.where(centre, turn(extra, 64 - WIDE - 2 * WIDE * j), 0.0))

        def side(right, _, g_ref, first_ref, second_ref):
            main = low if right else jnp.logical_not(low)
            at, t_at = (64, 0) if right else (64 - WIDE, LANES - WIDE)

            def window(value, source, target):
                return jnp.where((lane >= target) & (lane < target + WIDE), turn(value, target - source), 0.0)

            for j in range(17):
                value = g_ref[layer, 8 * j : 8 * j + 8, :]
                add(1, 8 * j, jnp.where(main, value, 0.0))
                add(1, half + 8 * j, jnp.where(main, turn(value, 64), 0.0))
            extras = [g_ref[layer, half + 8 * j : half + 8 * j + 8, :] for j in range(4)]
            for j in range(34):
                value = window(extras[j // SLOTS], WIDE * (j % SLOTS), at)
                if 1 <= j <= 32:
                    k = j - 1
                    value = value + window(extras[2 + k // SLOTS], WIDE * (k % SLOTS), t_at)
                add(2, 8 * j, value)
            for which, ref in zip(after, (first_ref, second_ref)):
                edge, t_row = which * (SUM_ROWS - EDGE), which * (SUM_ROWS - 8)
                extra = ref[layer, 32:40, :]
                start = 64 if right else 0
                for j in range(9):
                    value = ref[layer, 8 * (j % 5) : 8 * (j % 5) + 8, :]
                    if j > 4:
                        value = turn(value, 64)
                    add(1, edge + 8 * j, jnp.where(main, value, 0.0))
                    add(2, edge + 8 * j, window(extra, start + WIDE * j, at))
                add(2, t_row, window(extra, start + 9 * WIDE, t_at))

        by_side(sides, side, from_g, d_first, d_second)

    made = copies(1 - core, other, 0) + copies(core, own, 1)
    for one in made:
        one.start()
    for one in made:
        one.wait()


def heat_kernel(own, other, out):
    depth = own.shape[0]
    core = lax.axis_index("ta")
    low = lane_ids() < 64

    def move(src, first):
        @pl.loop(0, depth)
        def _(layer):
            for j in range(16):
                one = turn(src[layer, 8 + 8 * j : 16 + 8 * j, :], 64)
                two = turn(src[layer, HALF_ROWS + 8 + 8 * j : HALF_ROWS + 16 + 8 * j, :], 64)
                out[layer, rows8(first + 8 * j), :LANES] = jnp.where(low, two, one)
                out[layer, rows8(first + 8 * j), LANES:] = jnp.where(low, one, two)

    move(own, core * 128)
    move(other, 128 - core * 128)


def permutation(inverse=False, shift=0):
    rows = lax.broadcasted_iota(jnp.int32, (256, 256), 0)
    cols = lax.broadcasted_iota(jnp.int32, (256, 256), 1)
    if inverse:
        rows, cols = cols, rows
    return jnp.where((rows + shift) % 256 == 4 * (cols % 64) + cols // 64, 1.0, 0.0).astype(jnp.bfloat16)


def permuted(value, matrix):
    parts = []
    for _ in range(3):
        part = value.astype(jnp.bfloat16)
        value = value - part.astype(F32)
        parts.append(part)
    moved = jnp.dot(jnp.concatenate(parts, axis=0), matrix, preferred_element_type=F32)
    high, middle, low = (moved[k * value.shape[0] : (k + 1) * value.shape[0]] for k in range(3))
    return high + (middle + low)


def to_groups(first, second):
    low = lane_ids() < 64
    out = []
    for half in range(2):
        one = first[:, half * LANES : (half + 1) * LANES]
        two = second[:, half * LANES : (half + 1) * LANES]
        out += [jnp.where(low, one, turn(two, 64)), jnp.where(low, turn(one, 64), two)]
    return out


def to_rows(parts):
    low = lane_ids() < 64
    one, two = [], []
    for half in range(2):
        left, right = parts[2 * half], parts[2 * half + 1]
        one.append(jnp.where(low, left, turn(right, 64)))
        two.append(jnp.where(low, turn(left, 64), right))
    return jnp.concatenate(one, axis=1), jnp.concatenate(two, axis=1)


def group_cells(load, dst, matrix):
    @pl.loop(0, STEP_ROWS // BLOCK)
    def _(block):
        rows = [group * STEP_ROWS + block * BLOCK + step for group in range(2) for step in range(BLOCK)]
        halves = [jnp.concatenate([load(row, half) for row in rows], axis=0) for half in range(2)]
        value = permuted(jnp.concatenate(halves, axis=1), matrix)
        for step in range(BLOCK):
            parts = to_groups(*(value[8 * at : 8 * at + 8] for at in (step, BLOCK + step)))
            for col in range(4):
                dst[rows8((block * BLOCK + step + 1) * 40 + 8 * col), :] = parts[col]


def stack_kernel(t_own, t_other, now, t_cells, t_sems):
    core = lax.axis_index("ta")
    depth, rows, _ = t_own.shape
    layers = 2 * depth
    copies = []
    for which, t_src in enumerate((t_own, t_other)):
        base = core * depth if which == 0 else (1 - core) * depth
        for layer in range(depth):
            for col in range(2):
                copies.append(
                    pltpu.make_async_copy(
                        t_src.at[layer, :, col * LANES : (col + 1) * LANES],
                        t_cells.at[col, base + layer, pl.ds(8, rows), :],
                        t_sems.at[which, layer, col],
                    )
                )
    for copy in copies:
        copy.start()
    zero = jnp.zeros((8, LANES), F32)
    for col in range(2):
        for layer in range(layers):
            t_cells[col, layer, 0:8, :] = zero
            t_cells[col, layer, rows + 8 : rows + 16, :] = zero

    @pl.loop(0, STEP_ROWS + 2)
    def _(step):
        now[rows8(step * 40 + 32), :] = zero

    for copy in copies:
        copy.wait()
    flat = t_cells.reshape(2, layers * (rows + 16), LANES)
    first = 2 + core * 128

    def load(row, half):
        return flat[half, pl.ds(first + row, layers, stride=rows + 16), :]

    group_cells(load, now, permutation())


def solve_kernel(bounds, own, other, now_in, flow, material, conductivity, kept, sent, *refs):
    cells, rows_t, heat, now, later, cond, f_down, f_right, f_above, inverse, base, t_stage, in_sems, sems = refs
    core = lax.axis_index("ta")
    gx, gy = lax.axis_index("gx"), lax.axis_index("gy")
    lane = lane_ids()
    level = lax.broadcasted_iota(jnp.int32, (8, LANES), 0)
    low = lane < 64
    layers = 8
    depth = layers // 2

    def at(step, col):
        return rows8(step * 40 + 8 * col)

    incoming = [
        pltpu.make_async_copy(src, cells.at[pl.ds(first, depth)], in_sems.at[which])
        for which, (src, first) in enumerate(((own, core * depth), (other, (1 - core) * depth)))
    ]
    for copy in incoming:
        copy.start()

    @pl.loop(0, STEP_ROWS // 14)
    def _(block):
        for part in range(14):
            for col in range(4):
                where = at(block * 14 + part + 1, col)
                now[where, :] = now_in[where, :]

    for copy in incoming:
        copy.wait()
    flat = cells.reshape(layers * SWAP, LANES)

    def across(row):
        return flat[pl.ds(row, layers, stride=SWAP), :]

    def to_stage(stage, src):
        @pl.loop(0, 16)
        def _(tile):
            for layer in range(layers):
                for col in range(2):
                    value = src[col, pl.ds((6 + 8 * tile) * 8 + layer, 8, stride=8), :]
                    stage[layer, rows8(8 * tile), col * LANES : (col + 1) * LANES] = value

    def outputs():
        mine = t_stage.at[pl.ds(core * depth, depth)]
        theirs = t_stage.at[pl.ds((1 - core) * depth, depth)]
        return (
            pltpu.make_async_copy(theirs, sent, sems.at[0]),
            pltpu.make_async_copy(mine, kept, sems.at[1]),
        )

    group_cells(lambda row, half: across(half * HALF_ROWS + 2 + row), heat, permutation(shift=64))
    t_edge = jnp.concatenate(
        [
            jnp.concatenate([across(3 * HALF_ROWS + 8 * col + i) for i in range(8)], axis=0)
            for col in range(2)
        ],
        axis=1,
    )
    t_edge = permuted(t_edge, permutation())
    halo_lanes = (lane < WIDE) | ((lane >= 64 - WIDE) & (lane < 64 + WIDE)) | (lane >= LANES - WIDE)

    @pl.loop(0, STEP_ROWS // 14)
    def _(block):
        for part in range(14):
            step = block * 14 + part
            first, second = across(2 * HALF_ROWS + 2 + step), across(2 * HALF_ROWS + 2 + step + STEP_ROWS)
            first_turned, second_turned = turn(first, 64), turn(second, 64)
            upper_lanes = jnp.where(lane < 64 + WIDE, first, first_turned)
            lower_lanes = jnp.where(lane < WIDE, second_turned, second)
            heat[at(step + 1, 4), :] = jnp.where(halo_lanes, jnp.where(low, lower_lanes, upper_lanes), 0.0)
            upper_lanes = jnp.where(lane < 64 + WIDE, first_turned, first)
            lower_lanes = jnp.where(lane < WIDE, second, second_turned)
            now[at(step + 1, 4), :] = jnp.where(halo_lanes, jnp.where(low, lower_lanes, upper_lanes), 0.0)
    @pl.when(core == 0)
    def _():
        for row in range(6):
            value = t_edge[8 * row + 16 : 8 * row + 24]
            parts = to_groups(value, value)
            for col in range(4):
                now[at(row + 1, col), :] = jnp.where(low, parts[col], now[at(row + 1, col), :])

    @pl.when(core == 1)
    def _():
        for row in range(6):
            value = t_edge[8 * row : 8 * row + 8]
            parts = to_groups(value, value)
            for col in range(4):
                now[at(row + 65, col), :] = jnp.where(low, now[at(row + 65, col), :], parts[col])

    def ghosts(ref):
        for col in range(5):
            ref[at(0, col), :] = turn(ref[at(STEP_ROWS, col), :], 64)
            ref[at(STEP_ROWS + 1, col), :] = turn(ref[at(1, col), :], 64)

    last = (lane == 63) | (lane == 127)
    first = (lane == 0) | (lane == 64)

    def to_right(values):
        inner, outer = turn(values[0], -1), turn(values[4], -1)
        return values[1:4] + [jnp.where(last, outer, inner), jnp.where(last, inner, outer)]

    def to_left(values):
        inner, outer = turn(values[3], 1), turn(values[4], 1)
        return [jnp.where(first, outer, inner)] + values[:3] + [jnp.where(first, inner, outer)]

    def upper(value):
        return pltpu.roll(value, 7, 0)

    def lower(value):
        return pltpu.roll(value, 1, 0)

    has_right = (gy + 1) * 256 < bounds[1]
    half_lane = jnp.where(low, lane, lane - 64)
    keep = ((half_lane < WIDE) & has_right) | ((half_lane >= 64 - WIDE) & (gy > 0))
    halo_mask = jnp.where(keep, 1.0, 0.0)
    scale = jnp.full((8, LANES), conductivity[material[0]], F32)
    for layer in range(1, layers):
        scale = jnp.where(level == layer, conductivity[material[layer]], scale)
    not_top = jnp.where(level < layers - 1, 1.0, 0.0)
    not_bottom = jnp.where(level > 0, 1.0, 0.0)
    flows = [flow[8 * col : 8 * col + 8, :] for col in range(5)]
    first_row = gx * 256 + core * 128 - 6

    def masks(step):
        ones = []
        for group in range(2):
            row = first_row + step + group * STEP_ROWS
            ones.append(jnp.where((row >= 0) & (row < bounds[0]), 1.0, 0.0))
        inner = jnp.where(low, ones[0], ones[1])
        return [inner] * 4 + [jnp.where(low, ones[1], ones[0]) * halo_mask]

    def conductances(src):
        @pl.loop(0, STEP_ROWS // 35)
        def _(block):
            for part in range(35):
                step = block * 35 + part
                mask = masks(step)
                for col in range(5):
                    where = at(step + 1, col)
                    cond[where, :] = (scale * mask[col]) * (1.0 + 0.5 * jnp.tanh(src[where, :]))

        ghosts(cond)

    def coefficients(src):
        @pl.loop(0, STEP_ROWS // 10)
        def _(block):
            start = block * 10
            lines = [[cond[at(start + part, col), :] for col in range(5)] for part in range(12)]
            for part in range(10):
                up, here, down = lines[part], lines[part + 1], lines[part + 2]
                mask = masks(start + part)
                rights, lefts = to_right(here), to_left(here)
                for col in range(5):
                    where = at(start + part + 1, col)
                    centre = here[col]
                    over = centre + upper(centre) * not_top
                    under = centre + lower(centre) * not_bottom
                    face_down = 0.5 * (centre + down[col])
                    face_right = 0.5 * (centre + rights[col])
                    total = (1.0 + flows[col]) + 0.5 * (centre + up[col]) + face_down
                    total = total + face_right + 0.5 * (centre + lefts[col]) + over + under
                    f_down[where, :] = face_down
                    f_right[where, :] = face_right
                    f_above[where, :] = over * not_top
                    inverse[where, :] = mask[col] / total
                    base[where, :] = src[where, :] + heat[where, :]

        for col in range(5):
            f_down[at(0, col), :] = 0.5 * (cond[at(0, col), :] + cond[at(1, col), :])

    def sweep(src, dst, cols=5):
        @pl.loop(0, STEP_ROWS // SPAN)
        def _(block):
            start = block * SPAN
            lines = [[src[at(start + part, col), :] for col in range(5)] for part in range(SPAN + 2)]
            faces = [[f_down[at(start + part, col), :] for col in range(5)] for part in range(SPAN + 1)]
            for part in range(SPAN):
                up, here, down = lines[part], lines[part + 1], lines[part + 2]
                face_right = [f_right[at(start + part + 1, col), :] for col in range(5)]
                rights = to_right(here)
                lefts = to_left([face * value for face, value in zip(face_right, here)])
                for col in range(cols):
                    where = at(start + part + 1, col)
                    face_above = f_above[where, :]
                    total = base[where, :] + (faces[part][col] + flows[col]) * up[col]
                    total = total + faces[part + 1][col] * down[col]
                    total = total + (face_right[col] * rights[col] + lefts[col])
                    total = total + (face_above * upper(here[col]) + lower(face_above * here[col]))
                    dst[where, :] = total * inverse[where, :]

        if cols == 5:
            ghosts(dst)

    ghosts(now)
    for step in range(STEPS):
        conductances(now)
        coefficients(now)
        for turn_of in range(SWEEPS):
            sweep(now, later, 4 if (step, turn_of) == (STEPS - 1, SWEEPS - 1) else 5)
            now, later = later, now

    back = permutation(inverse=True)

    @pl.loop(0, STEP_ROWS // BLOCK)
    def _(block):
        pairs = [
            to_rows([now[at(block * BLOCK + part + 1, col), :] for col in range(4)]) for part in range(BLOCK)
        ]
        value = jnp.concatenate([pair[group] for group in range(2) for pair in pairs], axis=0)
        value = permuted(value, back)
        for group in range(2):
            where = pl.ds(pl.multiple_of((group * STEP_ROWS + block * BLOCK) * 8, 8), BLOCK * 8)
            for col in range(2):
                part = value[group * BLOCK * 8 : (group + 1) * BLOCK * 8, col * LANES : (col + 1) * LANES]
                rows_t[col, where, :] = part

    to_stage(t_stage, rows_t)
    for copy in outputs():
        copy.start()
    for copy in outputs():
        copy.wait()


def place_kernel(mine, part, *refs):
    t_out, sem = refs[-2:]
    core = lax.axis_index("ta") if mine else 1 - lax.axis_index("ta")
    half = part.shape[1]
    copy = pltpu.make_async_copy(part, t_out.at[:, pl.ds(pl.multiple_of(core * half, half), half), :], sem)
    copy.start()
    copy.wait()


def on_device(t_initial, power_mantissa, tile_exponent, channel_mask, material, conductivity):
    depth, rows, cols = t_initial.shape
    layers = 2 * depth
    n_gx, n_gy = lax.axis_size("gx"), lax.axis_size("gy")
    array = jax.ShapeDtypeStruct
    swap = [(0, 1), (1, 0)]
    out_sides = [None] if n_gy == 2 else [True, False]
    in_sides = [None] if n_gy == 2 else [False, True]
    count = len(out_sides)

    t_other = lax.ppermute(t_initial, "ta", swap)
    exponents = tile_exponent.transpose(1, 0, 2)
    plain_shape = array((depth, 3, rows + 2 * RIM, LANES), F32)
    along = array((depth, ROWS_P, LANES), F32)
    across = (array((depth, ROWS_G, LANES), F32),) * count
    corner = (array((depth, ROWS_D, LANES), F32),) * (2 * count)
    sent = pl.pallas_call(
        functools.partial(send_kernel, out_sides),
        out_shape=(plain_shape, along, along) + across + corner,
        in_specs=[HBM, HBM, HBM],
        out_specs=(ANY,) + (VMEM,) * (2 + 3 * count),
        scratch_shapes=[
            pltpu.VMEM(plain_shape.shape, F32),
            pltpu.VMEM(power_mantissa.shape, power_mantissa.dtype),
            pltpu.SMEM(exponents.shape, jnp.int32),
            pltpu.VMEM(t_initial.shape, F32),
            pltpu.SemaphoreType.DMA((depth,)),
            pltpu.SemaphoreType.DMA((2, depth)),
            pltpu.SemaphoreType.DMA,
        ],
        compiler_params=params(12),
        name="send",
    )(*(pltpu.with_memory_space_constraint(value, pltpu.HBM) for value in (power_mantissa, exponents, t_initial)))
    sent = tuple(sent[:1]) + tuple(lax.optimization_barrier(tuple(sent[1:]) + (t_other,)))
    sent, t_other = sent[:-1], sent[-1]
    plain, first, second = sent[:3]
    to_g, to_d_first, to_d_second = sent[3 : 3 + count], sent[3 + count : 3 + 2 * count], sent[3 + 2 * count :]

    def move(value, start, step_x):
        pairs = []
        for z in range(n_gx):
            to_z = z if start is None else z + 1 if (z - start) % 2 == 0 else z - 1
            for x in range(n_gy):
                to_x = x ^ 1 if step_x is None else x + step_x
                if 0 <= to_z < n_gx and 0 <= to_x < n_gy:
                    pairs.append((z * n_gy + x, to_z * n_gy + to_x))
        return lax.ppermute(value, ("gx", "gy"), pairs)

    steps = [None] if n_gy == 2 else [1, -1]
    from_g = [move(value, None, step) for value, step in zip(to_g, steps)]
    from_first = move(first, 0, 0)
    from_second = move(second, 1, 0)
    d_first = [move(value, 0, step) for value, step in zip(to_d_first, steps)]
    d_second = [move(value, 1, step) for value, step in zip(to_d_second, steps)]

    wide = jnp.pad(channel_mask, ((0, 0), (RIM, RIM)))
    mask = lax.dynamic_slice_in_dim(wide, lax.axis_index("gy") * cols, cols + 2 * RIM, 1).astype(F32) * COOLANT
    inner = mask[:, RIM : RIM + cols].reshape(layers, 64, 4).transpose(2, 0, 1)
    outer = jnp.zeros((layers, 64 - 2 * WIDE), F32)
    outer = jnp.concatenate([mask[:, RIM + cols :][:, :WIDE], outer, mask[:, RIM - WIDE : RIM]], axis=1)
    flow = jnp.concatenate([inner, outer[None]], axis=0).reshape(layers * 5, 64)
    flow = jnp.concatenate([flow, flow], axis=1)

    grouped = array(((STEP_ROWS + 2) * 40, LANES), F32)
    now = pl.pallas_call(
        stack_kernel,
        out_shape=grouped,
        in_specs=[ANY] * 2,
        out_specs=VMEM,
        scratch_shapes=[
            pltpu.VMEM((2, layers, rows + 16, LANES), F32),
            pltpu.SemaphoreType.DMA((2, depth, 2)),
        ],
        compiler_params=params(24),
        name="stack",
    )(t_initial, t_other)

    from_first, now = lax.optimization_barrier((from_first, now))
    half = array((depth, SWAP, LANES), F32)
    own, other = pl.pallas_call(
        functools.partial(sum_kernel, in_sides),
        out_shape=(half, half),
        in_specs=[VMEM] * (3 + 3 * count),
        out_specs=(ANY, ANY),
        scratch_shapes=[
            pltpu.VMEM((depth, 3, SUM_ROWS, LANES), F32),
            pltpu.VMEM((2, depth, 16, LANES), F32),
            pltpu.SemaphoreType.DMA((2, 4)),
        ],
        compiler_params=params(12),
        name="sum",
    )(plain, *from_g, from_first, from_second, *d_first, *d_second)
    received = lax.ppermute(other, "ta", swap)
    whole = array((depth, rows, cols), F32)
    heat_source = pl.pallas_call(
        heat_kernel,
        out_shape=whole,
        in_specs=[VMEM] * 2,
        out_specs=VMEM,
        compiler_params=params(8),
        name="heat",
    )(own, other)

    received, heat_source = lax.optimization_barrier((received, heat_source))
    work = pltpu.VMEM(grouped.shape, F32)
    kept, sent = pl.pallas_call(
        functools.partial(solve_kernel, (n_gx * rows, n_gy * cols)),
        out_shape=(array((depth, rows // 2, cols), F32),) * 2,
        in_specs=[ANY, ANY] + [VMEM] * 2 + [SMEM, SMEM],
        out_specs=(ANY, ANY),
        scratch_shapes=[
            pltpu.VMEM((layers, SWAP, LANES), F32),
            pltpu.VMEM((2, REGION * 8, LANES), F32),
        ]
        + [work] * 9
        + [
            pltpu.VMEM((layers, rows // 2, cols), F32),
            pltpu.SemaphoreType.DMA((2,)),
            pltpu.SemaphoreType.DMA((2,)),
        ],
        compiler_params=params(30),
        name="solve",
    )(own, received, now, flow, material, conductivity)
    received = lax.ppermute(sent, "ta", swap)

    def place(mine, part, *whole_in):
        return pl.pallas_call(
            functools.partial(place_kernel, mine),
            out_shape=whole,
            in_specs=[ANY] * (1 + len(whole_in)),
            out_specs=ANY,
            scratch_shapes=[pltpu.SemaphoreType.DMA],
            input_output_aliases={1: 0} if whole_in else {},
            compiler_params=params(4),
            name="keep" if mine else "place",
        )(part, *whole_in)

    temperature = place(False, received, place(True, kept))
    return temperature, heat_source


def solution(mesh):
    cells = P("ta", ("group", "gx"), "gy")
    return jax.shard_map(
        on_device,
        mesh=mesh,
        in_specs=(cells, cells, cells, P(), P(), P()),
        out_specs=(cells, cells),
        check_vma=False,
    )
```

```python
import functools

import jax
import jax.numpy as jnp
from jax import lax
from jax.experimental import pallas as pl
from jax.experimental.pallas import tpu as pltpu
from jax.sharding import PartitionSpec as P

RIM = 64
TILE = 64
STEPS = 2
SWEEPS = 3
COOLANT = 2.0

LANES = 128
WIDE = 6
REGION = 140
STEP_ROWS = 70
BLOCK = 35
SPAN = 35
SUM_ROWS = 272
HALF_ROWS = 144
SWAP = 3 * HALF_ROWS + 16
EDGE = 72
SLOTS = LANES // WIDE
ROWS_P = 2 * EDGE + 8 + 16
ROWS_G = SUM_ROWS // 2 + 16 + 16
ROWS_D = 40
F32 = jnp.float32
VMEM = pl.BlockSpec(memory_space=pltpu.VMEM)
SMEM = pl.BlockSpec(memory_space=pltpu.SMEM)
ANY = pl.BlockSpec(memory_space=pl.ANY)
HBM = pl.BlockSpec(memory_space=pltpu.HBM)


def params(megabytes):
    return pltpu.CompilerParams(vmem_limit_bytes=megabytes << 20)


def rows8(start):
    return pl.ds(pl.multiple_of(start, 8), 8)


def lane_ids():
    return lax.broadcasted_iota(jnp.int32, (8, LANES), 1)


def turn(value, shift):
    shift = shift % LANES
    return pltpu.roll(value, shift, 1) if shift else value


def by_side(sides, body, *lists):
    for place, side in enumerate(sides):
        rest = [values[place] for values in lists]
        if side is None:
            first = lax.axis_index("gy") == 0
            pl.when(first)(functools.partial(body, True, place, *rest))
            pl.when(jnp.logical_not(first))(functools.partial(body, False, place, *rest))
        else:
            body(side, place, *rest)


def send_kernel(sides, mantissa_in, exponent_in, t_in, *refs):
    count = len(sides)
    whole, to_first, to_second = refs[:3]
    to_g, to_d_first, to_d_second = refs[3 : 3 + count], refs[3 + count : 3 + 2 * count], refs[3 + 2 * count : 3 + 3 * count]
    plain, mantissa, exponent, t_ref, sems, in_sems, exponent_sem = refs[3 + 3 * count :]
    depth, rows, _ = mantissa.shape
    lane = lane_ids()
    low = lane < 64
    wide_lane = lax.broadcasted_iota(jnp.int32, (16, LANES), 1)

    def place(total, value, source, target, width):
        moved = turn(value, target - source)
        return jnp.where((lane >= target) & (lane < target + width), moved, total)

    odd = lax.rem(lax.axis_index("gx"), 2)
    edges = [which * (rows - EDGE) for which in (1 - odd, odd)]
    t_edges = [which * (rows - 2 * RIM - 8) for which in (1 - odd, odd)]

    def copy(layer):
        return pltpu.make_async_copy(plain.at[layer], whole.at[layer], sems.at[layer])

    def pack(layer):
        def cells(col, row):
            return plain[layer, col, rows8(row), :]

        def t_cells(col, row):
            return t_ref[layer, rows8(row), col * LANES : (col + 1) * LANES]

        for out, edge, t_edge in ((to_first, edges[0], t_edges[0]), (to_second, edges[1], t_edges[1])):
            extra = jnp.zeros((8, LANES), F32)
            for j in range(9):
                left, right = cells(0, edge + 8 * j), cells(2, edge + 8 * j)
                out[layer, 8 * j : 8 * j + 8, :] = cells(1, edge + 8 * j)
                out[layer, EDGE + 8 * j : EDGE + 8 * j + 8, :] = jnp.where(low, right, left)
                extra = place(extra, jnp.where(low, left, right), 64 - WIDE, 2 * WIDE * j, 2 * WIDE)
            out[layer, 2 * EDGE : 2 * EDGE + 8, :] = extra
            for col in range(2):
                start = 2 * EDGE + 8 + 8 * col
                out[layer, start : start + 8, :] = t_cells(col, t_edge)

        def side(right, _, g_ref, first_ref, second_ref):
            col, t_col = (2, 1) if right else (0, 0)
            at, t_at = (64 - WIDE, LANES - WIDE) if right else (64, 0)
            half = SUM_ROWS // 2

            def both(one, two):
                return jnp.where(low, turn(two, 64), one) if right else jnp.where(low, one, turn(two, 64))

            for j in range(17):
                one, two = cells(col, RIM - 8 + 8 * j), cells(col, RIM - 8 + half + 8 * j)
                g_ref[layer, 8 * j : 8 * j + 8, :] = both(one, two)
            for first, parts, source in (
                (half, [cells(col, RIM - 8 + 8 * j) for j in range(34)], at),
                (half + 16, [t_cells(t_col, 8 * j) for j in range(32)], t_at),
            ):
                for part in range(2):
                    extra = jnp.zeros((8, LANES), F32)
                    for slot, value in enumerate(parts[part * SLOTS : (part + 1) * SLOTS]):
                        extra = place(extra, value, source, WIDE * slot, WIDE)
                    g_ref[layer, first + 8 * part : first + 8 * part + 8, :] = extra
            for out, edge, t_edge in ((first_ref, edges[0], t_edges[0]), (second_ref, edges[1], t_edges[1])):
                strips = [cells(col, edge + 8 * j) for j in range(9)]
                for j in range(4):
                    out[layer, 8 * j : 8 * j + 8, :] = both(strips[j], strips[j + 5])
                start = 0 if right else 64
                extra = strips[4]
                for j in range(9):
                    extra = place(extra, strips[j], at, start + WIDE * j, WIDE)
                extra = place(extra, t_cells(t_col, t_edge), t_at, start + 9 * WIDE, WIDE)
                out[layer, 32:40, :] = extra

        by_side(sides, side, to_g, to_d_first, to_d_second)

    def arrivals(layer):
        return (
            pltpu.make_async_copy(mantissa_in.at[layer], mantissa.at[layer], in_sems.at[0, layer]),
            pltpu.make_async_copy(t_in.at[layer], t_ref.at[layer], in_sems.at[1, layer]),
        )

    scales = pltpu.make_async_copy(exponent_in, exponent, exponent_sem)
    scales.start()
    for layer in range(depth):
        for one in arrivals(layer):
            one.start()
    scales.wait()

    @pl.loop(0, depth)
    def _(layer):
        for one in arrivals(layer):
            one.wait()

        @pl.loop(0, rows // TILE)
        def _(tile_row):
            for col in range(3):
                left = exponent[tile_row, layer, 2 * col]
                right = exponent[tile_row, layer, 2 * col + 1]
                scale = jnp.exp2(jnp.where(wide_lane < TILE, left, right).astype(F32))
                for part in range(TILE // 16):
                    where = pl.ds(pl.multiple_of(tile_row * TILE + part * 16, 16), 16)
                    cells = mantissa[layer, where, col * LANES : (col + 1) * LANES]
                    plain[layer, col, where, :] = cells.astype(F32) * scale

        copy(layer).start()
        pack(layer)

    for layer in range(depth):
        copy(layer).wait()


def sum_kernel(sides, *refs):
    count = len(sides)
    plain, payloads = refs[0], refs[1:]
    from_g, payloads = payloads[:count], payloads[count:]
    from_first, payloads = payloads[0], payloads[1:]
    from_second, payloads = payloads[0], payloads[1:]
    d_first, payloads = payloads[:count], payloads[count:]
    d_second, payloads = payloads[:count], payloads[count:]
    own, other, total, t_edge, sems = refs[3 + 3 * count :]
    depth = plain.shape[0]
    core = lax.axis_index("ta")
    odd = lax.rem(lax.axis_index("gx"), 2)
    after = (1 - odd, odd)
    lane = lane_ids()
    low = lane < 64
    half = SUM_ROWS // 2
    centre = (lane >= 64 - WIDE) & (lane < 64 + WIDE)

    def copies(side, out, index):
        row = pl.multiple_of(side * (SUM_ROWS - HALF_ROWS), 8)
        made = [
            pltpu.make_async_copy(
                total.at[:, col, pl.ds(row, HALF_ROWS), :],
                out.at[:, pl.ds(col * HALF_ROWS, HALF_ROWS), :],
                sems.at[index, col],
            )
            for col in range(3)
        ]
        made.append(pltpu.make_async_copy(t_edge.at[side], out.at[:, pl.ds(3 * HALF_ROWS, 16), :], sems.at[index, 3]))
        return made

    @pl.loop(0, depth)
    def _(layer):
        for j in range(SUM_ROWS // 8):
            row, where = RIM - 8 + 8 * j, pl.ds(8 * j, 8)
            left, right = plain[layer, 0, row : row + 8, :], plain[layer, 2, row : row + 8, :]
            total[layer, 0, where, :] = plain[layer, 1, row : row + 8, :]
            total[layer, 1, where, :] = jnp.where(low, right, left)
            total[layer, 2, where, :] = jnp.where(centre, jnp.where(low, left, right), 0.0)

        def add(col, row, value):
            total[layer, col, rows8(row), :] = total[layer, col, rows8(row), :] + value

        for which, ref in zip(after, (from_first, from_second)):
            edge = which * (SUM_ROWS - EDGE)
            t_edge[which, layer, :, :] = ref[layer, 2 * EDGE + 8 :, :]
            extra = ref[layer, 2 * EDGE : 2 * EDGE + 8, :]
            for j in range(9):
                add(0, edge + 8 * j, ref[layer, 8 * j : 8 * j + 8, :])
                add(1, edge + 8 * j, ref[layer, EDGE + 8 * j : EDGE + 8 * j + 8, :])
                add(2, edge + 8 * j, jnp.where(centre, turn(extra, 64 - WIDE - 2 * WIDE * j), 0.0))

        def side(right, _, g_ref, first_ref, second_ref):
            main = low if right else jnp.logical_not(low)
            at, t_at = (64, 0) if right else (64 - WIDE, LANES - WIDE)

            def window(value, source, target):
                return jnp.where((lane >= target) & (lane < target + WIDE), turn(value, target - source), 0.0)

            for j in range(17):
                value = g_ref[layer, 8 * j : 8 * j + 8, :]
                add(1, 8 * j, jnp.where(main, value, 0.0))
                add(1, half + 8 * j, jnp.where(main, turn(value, 64), 0.0))
            extras = [g_ref[layer, half + 8 * j : half + 8 * j + 8, :] for j in range(4)]
            for j in range(34):
                value = window(extras[j // SLOTS], WIDE * (j % SLOTS), at)
                if 1 <= j <= 32:
                    k = j - 1
                    value = value + window(extras[2 + k // SLOTS], WIDE * (k % SLOTS), t_at)
                add(2, 8 * j, value)
            for which, ref in zip(after, (first_ref, second_ref)):
                edge, t_row = which * (SUM_ROWS - EDGE), which * (SUM_ROWS - 8)
                extra = ref[layer, 32:40, :]
                start = 64 if right else 0
                for j in range(9):
                    value = ref[layer, 8 * (j % 5) : 8 * (j % 5) + 8, :]
                    if j > 4:
                        value = turn(value, 64)
                    add(1, edge + 8 * j, jnp.where(main, value, 0.0))
                    add(2, edge + 8 * j, window(extra, start + WIDE * j, at))
                add(2, t_row, window(extra, start + 9 * WIDE, t_at))

        by_side(sides, side, from_g, d_first, d_second)

    made = copies(1 - core, other, 0) + copies(core, own, 1)
    for one in made:
        one.start()
    for one in made:
        one.wait()


def heat_kernel(own, other, out):
    depth = own.shape[0]
    core = lax.axis_index("ta")
    low = lane_ids() < 64

    def move(src, first):
        @pl.loop(0, depth)
        def _(layer):
            for j in range(16):
                one = turn(src[layer, 8 + 8 * j : 16 + 8 * j, :], 64)
                two = turn(src[layer, HALF_ROWS + 8 + 8 * j : HALF_ROWS + 16 + 8 * j, :], 64)
                out[layer, rows8(first + 8 * j), :LANES] = jnp.where(low, two, one)
                out[layer, rows8(first + 8 * j), LANES:] = jnp.where(low, one, two)

    move(own, core * 128)
    move(other, 128 - core * 128)


def permutation(inverse=False, shift=0):
    rows = lax.broadcasted_iota(jnp.int32, (256, 256), 0)
    cols = lax.broadcasted_iota(jnp.int32, (256, 256), 1)
    if inverse:
        rows, cols = cols, rows
    return jnp.where((rows + shift) % 256 == 4 * (cols % 64) + cols // 64, 1.0, 0.0).astype(jnp.bfloat16)


def permuted(value, matrix):
    parts = []
    for _ in range(3):
        part = value.astype(jnp.bfloat16)
        value = value - part.astype(F32)
        parts.append(part)
    moved = jnp.dot(jnp.concatenate(parts, axis=0), matrix, preferred_element_type=F32)
    high, middle, low = (moved[k * value.shape[0] : (k + 1) * value.shape[0]] for k in range(3))
    return high + (middle + low)


def to_groups(first, second):
    low = lane_ids() < 64
    out = []
    for half in range(2):
        one = first[:, half * LANES : (half + 1) * LANES]
        two = second[:, half * LANES : (half + 1) * LANES]
        out += [jnp.where(low, one, turn(two, 64)), jnp.where(low, turn(one, 64), two)]
    return out


def to_rows(parts):
    low = lane_ids() < 64
    one, two = [], []
    for half in range(2):
        left, right = parts[2 * half], parts[2 * half + 1]
        one.append(jnp.where(low, left, turn(right, 64)))
        two.append(jnp.where(low, turn(left, 64), right))
    return jnp.concatenate(one, axis=1), jnp.concatenate(two, axis=1)


def group_cells(load, dst, matrix):
    @pl.loop(0, STEP_ROWS // BLOCK)
    def _(block):
        rows = [group * STEP_ROWS + block * BLOCK + step for group in range(2) for step in range(BLOCK)]
        halves = [jnp.concatenate([load(row, half) for row in rows], axis=0) for half in range(2)]
        value = permuted(jnp.concatenate(halves, axis=1), matrix)
        for step in range(BLOCK):
            parts = to_groups(*(value[8 * at : 8 * at + 8] for at in (step, BLOCK + step)))
            for col in range(4):
                dst[rows8((block * BLOCK + step + 1) * 40 + 8 * col), :] = parts[col]


def stack_kernel(t_own, t_other, now, t_cells, t_sems):
    core = lax.axis_index("ta")
    depth, rows, _ = t_own.shape
    layers = 2 * depth
    copies = []
    for which, t_src in enumerate((t_own, t_other)):
        base = core * depth if which == 0 else (1 - core) * depth
        for layer in range(depth):
            for col in range(2):
                copies.append(
                    pltpu.make_async_copy(
                        t_src.at[layer, :, col * LANES : (col + 1) * LANES],
                        t_cells.at[col, base + layer, pl.ds(8, rows), :],
                        t_sems.at[which, layer, col],
                    )
                )
    for copy in copies:
        copy.start()
    zero = jnp.zeros((8, LANES), F32)
    for col in range(2):
        for layer in range(layers):
            t_cells[col, layer, 0:8, :] = zero
            t_cells[col, layer, rows + 8 : rows + 16, :] = zero

    @pl.loop(0, STEP_ROWS + 2)
    def _(step):
        now[rows8(step * 40 + 32), :] = zero

    for copy in copies:
        copy.wait()
    flat = t_cells.reshape(2, layers * (rows + 16), LANES)
    first = 2 + core * 128

    def load(row, half):
        return flat[half, pl.ds(first + row, layers, stride=rows + 16), :]

    group_cells(load, now, permutation())


def solve_kernel(bounds, own, other, now_in, flow, material, conductivity, kept, sent, *refs):
    cells, rows_t, heat, now, later, cond, f_up, f_down, f_right, f_above, inverse, base, t_stage, in_sems, sems = refs
    core = lax.axis_index("ta")
    gx, gy = lax.axis_index("gx"), lax.axis_index("gy")
    lane = lane_ids()
    level = lax.broadcasted_iota(jnp.int32, (8, LANES), 0)
    low = lane < 64
    layers = 8
    depth = layers // 2

    def at(step, col):
        return rows8(step * 40 + 8 * col)

    incoming = [
        pltpu.make_async_copy(src, cells.at[pl.ds(first, depth)], in_sems.at[which])
        for which, (src, first) in enumerate(((own, core * depth), (other, (1 - core) * depth)))
    ]
    for copy in incoming:
        copy.start()

    @pl.loop(0, STEP_ROWS // 14)
    def _(block):
        for part in range(14):
            for col in range(4):
                where = at(block * 14 + part + 1, col)
                now[where, :] = now_in[where, :]

    for copy in incoming:
        copy.wait()
    flat = cells.reshape(layers * SWAP, LANES)

    def across(row):
        return flat[pl.ds(row, layers, stride=SWAP), :]

    def to_stage(stage, src):
        @pl.loop(0, 16)
        def _(tile):
            for layer in range(layers):
                for col in range(2):
                    value = src[col, pl.ds((6 + 8 * tile) * 8 + layer, 8, stride=8), :]
                    stage[layer, rows8(8 * tile), col * LANES : (col + 1) * LANES] = value

    def outputs():
        mine = t_stage.at[pl.ds(core * depth, depth)]
        theirs = t_stage.at[pl.ds((1 - core) * depth, depth)]
        return (
            pltpu.make_async_copy(theirs, sent, sems.at[0]),
            pltpu.make_async_copy(mine, kept, sems.at[1]),
        )

    group_cells(lambda row, half: across(half * HALF_ROWS + 2 + row), heat, permutation(shift=64))
    t_edge = jnp.concatenate(
        [
            jnp.concatenate([across(3 * HALF_ROWS + 8 * col + i) for i in range(8)], axis=0)
            for col in range(2)
        ],
        axis=1,
    )
    t_edge = permuted(t_edge, permutation())
    halo_lanes = (lane < WIDE) | ((lane >= 64 - WIDE) & (lane < 64 + WIDE)) | (lane >= LANES - WIDE)

    @pl.loop(0, STEP_ROWS // 14)
    def _(block):
        for part in range(14):
            step = block * 14 + part
            first, second = across(2 * HALF_ROWS + 2 + step), across(2 * HALF_ROWS + 2 + step + STEP_ROWS)
            first_turned, second_turned = turn(first, 64), turn(second, 64)
            upper_lanes = jnp.where(lane < 64 + WIDE, first, first_turned)
            lower_lanes = jnp.where(lane < WIDE, second_turned, second)
            heat[at(step + 1, 4), :] = jnp.where(halo_lanes, jnp.where(low, lower_lanes, upper_lanes), 0.0)
            upper_lanes = jnp.where(lane < 64 + WIDE, first_turned, first)
            lower_lanes = jnp.where(lane < WIDE, second, second_turned)
            now[at(step + 1, 4), :] = jnp.where(halo_lanes, jnp.where(low, lower_lanes, upper_lanes), 0.0)
    @pl.when(core == 0)
    def _():
        for row in range(6):
            value = t_edge[8 * row + 16 : 8 * row + 24]
            parts = to_groups(value, value)
            for col in range(4):
                now[at(row + 1, col), :] = jnp.where(low, parts[col], now[at(row + 1, col), :])

    @pl.when(core == 1)
    def _():
        for row in range(6):
            value = t_edge[8 * row : 8 * row + 8]
            parts = to_groups(value, value)
            for col in range(4):
                now[at(row + 65, col), :] = jnp.where(low, now[at(row + 65, col), :], parts[col])

    def ghosts(ref):
        for col in range(5):
            ref[at(0, col), :] = turn(ref[at(STEP_ROWS, col), :], 64)
            ref[at(STEP_ROWS + 1, col), :] = turn(ref[at(1, col), :], 64)

    last = (lane == 63) | (lane == 127)
    first = (lane == 0) | (lane == 64)

    def to_right(values):
        inner, outer = turn(values[0], -1), turn(values[4], -1)
        return values[1:4] + [jnp.where(last, outer, inner), jnp.where(last, inner, outer)]

    def to_left(values):
        inner, outer = turn(values[3], 1), turn(values[4], 1)
        return [jnp.where(first, outer, inner)] + values[:3] + [jnp.where(first, inner, outer)]

    def upper(value):
        return pltpu.roll(value, 7, 0)

    def lower(value):
        return pltpu.roll(value, 1, 0)

    has_right = (gy + 1) * 256 < bounds[1]
    half_lane = jnp.where(low, lane, lane - 64)
    keep = ((half_lane < WIDE) & has_right) | ((half_lane >= 64 - WIDE) & (gy > 0))
    halo_mask = jnp.where(keep, 1.0, 0.0)
    scale = jnp.full((8, LANES), conductivity[material[0]], F32)
    for layer in range(1, layers):
        scale = jnp.where(level == layer, conductivity[material[layer]], scale)
    not_top = jnp.where(level < layers - 1, 1.0, 0.0)
    not_bottom = jnp.where(level > 0, 1.0, 0.0)
    flows = [flow[8 * col : 8 * col + 8, :] for col in range(5)]
    first_row = gx * 256 + core * 128 - 6

    def masks(step):
        ones = []
        for group in range(2):
            row = first_row + step + group * STEP_ROWS
            ones.append(jnp.where((row >= 0) & (row < bounds[0]), 1.0, 0.0))
        inner = jnp.where(low, ones[0], ones[1])
        return [inner] * 4 + [jnp.where(low, ones[1], ones[0]) * halo_mask]

    def conductances(src):
        @pl.loop(0, STEP_ROWS // 35)
        def _(block):
            for part in range(35):
                step = block * 35 + part
                mask = masks(step)
                for col in range(5):
                    where = at(step + 1, col)
                    cond[where, :] = (scale * mask[col]) * (1.0 + 0.5 * jnp.tanh(src[where, :]))

        ghosts(cond)

    def coefficients(src):
        @pl.loop(0, STEP_ROWS // 10)
        def _(block):
            start = block * 10
            lines = [[cond[at(start + part, col), :] for col in range(5)] for part in range(12)]
            for part in range(10):
                up, here, down = lines[part], lines[part + 1], lines[part + 2]
                mask = masks(start + part)
                rights, lefts = to_right(here), to_left(here)
                for col in range(5):
                    where = at(start + part + 1, col)
                    centre = here[col]
                    over = centre + upper(centre) * not_top
                    under = centre + lower(centre) * not_bottom
                    face_down = 0.5 * (centre + down[col])
                    face_right = 0.5 * (centre + rights[col])
                    face_up = 0.5 * (centre + up[col]) + flows[col]
                    total = 1.0 + face_up + face_down
                    total = total + face_right + 0.5 * (centre + lefts[col]) + over + under
                    f_up[where, :] = face_up
                    f_down[where, :] = face_down
                    f_right[where, :] = face_right
                    f_above[where, :] = over * not_top
                    inverse[where, :] = mask[col] / total
                    base[where, :] = src[where, :] + heat[where, :]

    def sweep(src, dst, cols=5):
        @pl.loop(0, STEP_ROWS // SPAN)
        def _(block):
            start = block * SPAN
            lines = [[src[at(start + part, col), :] for col in range(5)] for part in range(SPAN + 2)]
            for part in range(SPAN):
                up, here, down = lines[part], lines[part + 1], lines[part + 2]
                face_right = [f_right[at(start + part + 1, col), :] for col in range(5)]
                rights = to_right(here)
                lefts = to_left([face * value for face, value in zip(face_right, here)])
                for col in range(cols):
                    where = at(start + part + 1, col)
                    face_above = f_above[where, :]
                    total = base[where, :] + f_up[where, :] * up[col]
                    total = total + f_down[where, :] * down[col]
                    total = total + (face_right[col] * rights[col] + lefts[col])
                    total = total + (face_above * upper(here[col]) + lower(face_above * here[col]))
                    dst[where, :] = total * inverse[where, :]

        if cols == 5:
            ghosts(dst)

    ghosts(now)
    for step in range(STEPS):
        conductances(now)
        coefficients(now)
        for turn_of in range(SWEEPS):
            sweep(now, later, 4 if (step, turn_of) == (STEPS - 1, SWEEPS - 1) else 5)
            now, later = later, now

    back = permutation(inverse=True)

    @pl.loop(0, STEP_ROWS // BLOCK)
    def _(block):
        pairs = [
            to_rows([now[at(block * BLOCK + part + 1, col), :] for col in range(4)]) for part in range(BLOCK)
        ]
        value = jnp.concatenate([pair[group] for group in range(2) for pair in pairs], axis=0)
        value = permuted(value, back)
        for group in range(2):
            where = pl.ds(pl.multiple_of((group * STEP_ROWS + block * BLOCK) * 8, 8), BLOCK * 8)
            for col in range(2):
                part = value[group * BLOCK * 8 : (group + 1) * BLOCK * 8, col * LANES : (col + 1) * LANES]
                rows_t[col, where, :] = part

    to_stage(t_stage, rows_t)
    for copy in outputs():
        copy.start()
    for copy in outputs():
        copy.wait()


def place_kernel(mine, part, *refs):
    t_out, sem = refs[-2:]
    core = lax.axis_index("ta") if mine else 1 - lax.axis_index("ta")
    half = part.shape[1]
    copy = pltpu.make_async_copy(part, t_out.at[:, pl.ds(pl.multiple_of(core * half, half), half), :], sem)
    copy.start()
    copy.wait()


def on_device(t_initial, power_mantissa, tile_exponent, channel_mask, material, conductivity):
    depth, rows, cols = t_initial.shape
    layers = 2 * depth
    n_gx, n_gy = lax.axis_size("gx"), lax.axis_size("gy")
    array = jax.ShapeDtypeStruct
    swap = [(0, 1), (1, 0)]
    out_sides = [None] if n_gy == 2 else [True, False]
    in_sides = [None] if n_gy == 2 else [False, True]
    count = len(out_sides)

    t_other = lax.ppermute(t_initial, "ta", swap)
    exponents = tile_exponent.transpose(1, 0, 2)
    plain_shape = array((depth, 3, rows + 2 * RIM, LANES), F32)
    along = array((depth, ROWS_P, LANES), F32)
    across = (array((depth, ROWS_G, LANES), F32),) * count
    corner = (array((depth, ROWS_D, LANES), F32),) * (2 * count)
    sent = pl.pallas_call(
        functools.partial(send_kernel, out_sides),
        out_shape=(plain_shape, along, along) + across + corner,
        in_specs=[HBM, HBM, HBM],
        out_specs=(ANY,) + (VMEM,) * (2 + 3 * count),
        scratch_shapes=[
            pltpu.VMEM(plain_shape.shape, F32),
            pltpu.VMEM(power_mantissa.shape, power_mantissa.dtype),
            pltpu.SMEM(exponents.shape, jnp.int32),
            pltpu.VMEM(t_initial.shape, F32),
            pltpu.SemaphoreType.DMA((depth,)),
            pltpu.SemaphoreType.DMA((2, depth)),
            pltpu.SemaphoreType.DMA,
        ],
        compiler_params=params(12),
        name="send",
    )(*(pltpu.with_memory_space_constraint(value, pltpu.HBM) for value in (power_mantissa, exponents, t_initial)))
    sent = tuple(sent[:1]) + tuple(lax.optimization_barrier(tuple(sent[1:]) + (t_other,)))
    sent, t_other = sent[:-1], sent[-1]
    plain, first, second = sent[:3]
    to_g, to_d_first, to_d_second = sent[3 : 3 + count], sent[3 + count : 3 + 2 * count], sent[3 + 2 * count :]

    def move(value, start, step_x):
        pairs = []
        for z in range(n_gx):
            to_z = z if start is None else z + 1 if (z - start) % 2 == 0 else z - 1
            for x in range(n_gy):
                to_x = x ^ 1 if step_x is None else x + step_x
                if 0 <= to_z < n_gx and 0 <= to_x < n_gy:
                    pairs.append((z * n_gy + x, to_z * n_gy + to_x))
        return lax.ppermute(value, ("gx", "gy"), pairs)

    steps = [None] if n_gy == 2 else [1, -1]
    from_g = [move(value, None, step) for value, step in zip(to_g, steps)]
    from_first = move(first, 0, 0)
    from_second = move(second, 1, 0)
    d_first = [move(value, 0, step) for value, step in zip(to_d_first, steps)]
    d_second = [move(value, 1, step) for value, step in zip(to_d_second, steps)]

    wide = jnp.pad(channel_mask, ((0, 0), (RIM, RIM)))
    mask = lax.dynamic_slice_in_dim(wide, lax.axis_index("gy") * cols, cols + 2 * RIM, 1).astype(F32) * COOLANT
    inner = mask[:, RIM : RIM + cols].reshape(layers, 64, 4).transpose(2, 0, 1)
    outer = jnp.zeros((layers, 64 - 2 * WIDE), F32)
    outer = jnp.concatenate([mask[:, RIM + cols :][:, :WIDE], outer, mask[:, RIM - WIDE : RIM]], axis=1)
    flow = jnp.concatenate([inner, outer[None]], axis=0).reshape(layers * 5, 64)
    flow = jnp.concatenate([flow, flow], axis=1)

    grouped = array(((STEP_ROWS + 2) * 40, LANES), F32)
    now = pl.pallas_call(
        stack_kernel,
        out_shape=grouped,
        in_specs=[ANY] * 2,
        out_specs=VMEM,
        scratch_shapes=[
            pltpu.VMEM((2, layers, rows + 16, LANES), F32),
            pltpu.SemaphoreType.DMA((2, depth, 2)),
        ],
        compiler_params=params(24),
        name="stack",
    )(t_initial, t_other)

    from_first, now = lax.optimization_barrier((from_first, now))
    half = array((depth, SWAP, LANES), F32)
    own, other = pl.pallas_call(
        functools.partial(sum_kernel, in_sides),
        out_shape=(half, half),
        in_specs=[VMEM] * (3 + 3 * count),
        out_specs=(ANY, ANY),
        scratch_shapes=[
            pltpu.VMEM((depth, 3, SUM_ROWS, LANES), F32),
            pltpu.VMEM((2, depth, 16, LANES), F32),
            pltpu.SemaphoreType.DMA((2, 4)),
        ],
        compiler_params=params(12),
        name="sum",
    )(plain, *from_g, from_first, from_second, *d_first, *d_second)
    received = lax.ppermute(other, "ta", swap)
    whole = array((depth, rows, cols), F32)
    heat_source = pl.pallas_call(
        heat_kernel,
        out_shape=whole,
        in_specs=[VMEM] * 2,
        out_specs=VMEM,
        compiler_params=params(8),
        name="heat",
    )(own, other)

    received, heat_source = lax.optimization_barrier((received, heat_source))
    work = pltpu.VMEM(grouped.shape, F32)
    kept, sent = pl.pallas_call(
        functools.partial(solve_kernel, (n_gx * rows, n_gy * cols)),
        out_shape=(array((depth, rows // 2, cols), F32),) * 2,
        in_specs=[ANY, ANY] + [VMEM] * 2 + [SMEM, SMEM],
        out_specs=(ANY, ANY),
        scratch_shapes=[
            pltpu.VMEM((layers, SWAP, LANES), F32),
            pltpu.VMEM((2, REGION * 8, LANES), F32),
        ]
        + [work] * 10
        + [
            pltpu.VMEM((layers, rows // 2, cols), F32),
            pltpu.SemaphoreType.DMA((2,)),
            pltpu.SemaphoreType.DMA((2,)),
        ],
        compiler_params=params(30),
        name="solve",
    )(own, received, now, flow, material, conductivity)
    received = lax.ppermute(sent, "ta", swap)

    def place(mine, part, *whole_in):
        return pl.pallas_call(
            functools.partial(place_kernel, mine),
            out_shape=whole,
            in_specs=[ANY] * (1 + len(whole_in)),
            out_specs=ANY,
            scratch_shapes=[pltpu.SemaphoreType.DMA],
            input_output_aliases={1: 0} if whole_in else {},
            compiler_params=params(4),
            name="keep" if mine else "place",
        )(part, *whole_in)

    temperature = place(False, received, place(True, kept))
    return temperature, heat_source


def solution(mesh):
    cells = P("ta", ("group", "gx"), "gy")
    return jax.shard_map(
        on_device,
        mesh=mesh,
        in_specs=(cells, cells, cells, P(), P(), P()),
        out_specs=(cells, cells),
        check_vma=False,
    )
```
